32 devices in a mesh: grp: 4 (over x, core), own: 8 (over z, y).
Axes of the slice: x: 2, y: 2, z: 4, core: 2. Of those that a mesh axis runs over, the one named last changes fastest.
Arguments:
- orbitals: bfloat16 [32, 32, 1024], P(('grp', 'own')), may hold values from -3 to 3
- offsets: int32 [32, 2], P(('grp', 'own')), may hold values from 0 to 32
- pairs: int32 [32, 2], P('grp'), may hold values from 0 to 7, as said below
- ext_pot: bfloat16 [32, 4096], replicated, may hold values from -6 to 6
Outputs:
- gradient: float32 [32, 32, 1024], P(('grp', 'own'))
The draws below stay inside these ranges and needn't reach their ends.
Inputs may be any that keep to these rules, and one draw needn't show every extreme that they name: `pairs`: rows g * 8 to g * 8 + 7 belong to group g; each row names two different orbitals of the group. Calling owner o the device holding orbital o of a group, at most 2 rows of a group have orbital o as their first orbital, and in every group some owner has exactly 2.
All inputs are finite; a program needn't handle non-finite values.
Results may differ from the reference program's by a relative error of at most 0.0006.
Values may be sent and summed in bfloat16 or wider, within the bound.
A program may use at most 64 MiB of HBM per device.

```python
import math
import jax
import jax.numpy as jnp
from jax import lax

B = 32
BZ = 32
G = 64
ORB_DEV = 1
TASK_CAP = 2
GROUPS = 4
OWNERS = 8
ORB_GRP = 8
ORBITALS = 32
PAIRS_GRP = 8
PAIRS = 32


def draw_pairs(key, part):

    def one_group(group):
        base = jax.random.fold_in(jax.random.fold_in(key, 7001), group)
        keys = jax.random.split(base, 5)
        heavy = jax.random.randint(keys[0], (), 0, OWNERS)
        spare = jax.random.permutation(keys[1], (OWNERS - 1) * TASK_CAP)[:PAIRS_GRP - TASK_CAP]
        others = (spare // TASK_CAP).astype(jnp.int32)
        others = others + (others >= heavy).astype(jnp.int32)
        owners = jnp.concatenate([jnp.full((TASK_CAP,), heavy, jnp.int32), others])
        first = owners * ORB_DEV + jax.random.randint(keys[2], (PAIRS_GRP,), 0, ORB_DEV)
        second = (first + jax.random.randint(keys[3], (PAIRS_GRP,), 1, ORB_GRP)) % ORB_GRP
        listed = jnp.stack([first, second], axis=1)
        ranking = jax.random.permutation(keys[4], PAIRS_GRP)
        return listed[ranking]
    every = jax.vmap(one_group)(jnp.arange(GROUPS, dtype=jnp.int32))
    return every.reshape(PAIRS, 2).astype(jnp.int32)


def set_ends(drawn, stream_key, least, largest):
    longest = drawn.shape.index(max(drawn.shape))
    spots = []
    for shift in (0, 1):
        where = [jax.random.randint(jax.random.fold_in(stream_key, axis), (), 0, length) for axis, length in enumerate(drawn.shape)]
        where[longest] = (where[longest] + shift) % drawn.shape[longest]
        spots.append(tuple(where))
    return drawn.at[spots[0]].set(least).at[spots[1]].set(largest)


def block_scale(key, dims, shards, least, high):
    level, own = 1.0, jax.random.fold_in(key, 6)
    for position, blocks in shards:
        draws = jnp.exp(jax.random.uniform(jax.random.fold_in(own, position), (blocks,), jnp.float32, least / len(shards), high / len(shards)))
        level = level * jnp.repeat(draws, dims[position] // blocks).reshape([-1 if axis == position else 1 for axis in range(len(dims))])
    return level


def scatter_about(own_key, dims, scale, limit, cuts=(), kind=jnp.bfloat16):
    entries = jax.random.normal(own_key, dims, jnp.float32) * scale
    if len(cuts) > 0:
        entries = block_scale(own_key, dims, cuts, -0.22, 0.18) * entries
    return jnp.clip(entries, min=-limit, max=limit).astype(kind)


def setup_inputs(seed: int = 0) -> dict:
    splits = jax.random.split(jax.random.key(seed), 5)
    return {
        "orbitals": scatter_about(splits[0], (ORBITALS, BZ, B * B), 0.5, 3.0, ((0, 32),)),
        "offsets": set_ends(jax.random.randint(splits[1], (ORBITALS, 2), 0, G - B + 1), jax.random.fold_in(splits[1], 1), 0, G - B).astype(jnp.int32),
        "pairs": draw_pairs(jax.random.fold_in(splits[4], 71), 0),
        "ext_pot": scatter_about(splits[3], (BZ, G * G), 1.0, 6.0),
    }


SCREEN = 0.0025
MIXING = 0.25
EXCHANGE_COEF = (3.0 / math.pi) ** (1.0 / 3.0)


def wave_squares(length):
    positions = jnp.arange(length, dtype=jnp.int32)
    signed = jnp.where(positions < length // 2, positions, positions - length)
    wavenumber = (2.0 * math.pi / length) * signed.astype(jnp.float32)
    return wavenumber * wavenumber


def green_table(depth, width):
    along_z = wave_squares(2 * depth)
    along_y = wave_squares(2 * width)
    squared_sum = along_z[:, None, None] + along_y[None, :, None] + along_y[None, None, :]
    return (4.0 * math.pi) / (squared_sum + SCREEN)


def shifted(box_data, shift_y, shift_x):
    padded = jnp.pad(box_data, ((0, 0), (B, B), (B, B)))
    anchor = jnp.zeros((), jnp.int32)
    corner = (anchor, (B + shift_y).astype(jnp.int32), (B + shift_x).astype(jnp.int32))
    return lax.dynamic_slice(padded, corner, (BZ, B, B))


def poisson_solve(pair_density, green_values):
    padded = jnp.pad(pair_density, ((0, BZ), (0, B), (0, B)))
    spectrum = jnp.fft.fftn(padded) * green_values
    return jnp.real(jnp.fft.ifftn(spectrum))[:BZ, :B, :B]


def reference(orbitals, offsets, pairs, ext_pot):
    box_data = orbitals.astype(jnp.float32).reshape(ORBITALS, BZ, B, B)
    green_values = green_table(BZ, B)

    def add_pair(item, running):
        group = (item // PAIRS_GRP).astype(jnp.int32)
        first = (pairs[item, 0] + group * ORB_GRP).astype(jnp.int32)
        second = (pairs[item, 1] + group * ORB_GRP).astype(jnp.int32)
        shift = offsets[second] - offsets[first]
        near_box = box_data[first]
        moved_box = shifted(box_data[second], -shift[0], -shift[1])
        potential_box = poisson_solve(near_box * moved_box, green_values)
        running = running.at[first].add(potential_box * moved_box)
        return running.at[second].add(shifted(potential_box * near_box, shift[0], shift[1]))

    exchange = lax.fori_loop(0, PAIRS, add_pair, jnp.zeros((ORBITALS, BZ, B, B), jnp.float32))

    def add_box(item, density):
        anchor = jnp.zeros((), jnp.int32)
        corner = (anchor, offsets[item, 0].astype(jnp.int32), offsets[item, 1].astype(jnp.int32))
        current = lax.dynamic_slice(density, corner, (BZ, B, B))
        values = box_data[item]
        return lax.dynamic_update_slice(density, current + values * values, corner)

    density = lax.fori_loop(0, ORBITALS, add_box, jnp.zeros((BZ, G, G), jnp.float32))
    potential = ext_pot.astype(jnp.float32).reshape(BZ, G, G) - EXCHANGE_COEF * jnp.cbrt(density)

    def read_box(item):
        anchor = jnp.zeros((), jnp.int32)
        corner = (anchor, offsets[item, 0].astype(jnp.int32), offsets[item, 1].astype(jnp.int32))
        return lax.dynamic_slice(potential, corner, (BZ, B, B))

    local_potential = lax.map(read_box, jnp.arange(ORBITALS, dtype=jnp.int32))
    gradient = local_potential * box_data - MIXING * exchange
    return gradient.reshape(ORBITALS, BZ, B * B)
```

```python
import functools
import math

import jax
import jax.numpy as jnp
import ml_dtypes
import numpy as np
from jax import lax
from jax.experimental import pallas as pl
from jax.experimental.pallas import tpu as pltpu
from jax.sharding import PartitionSpec as P

SCREEN = 0.0025
MIXING = 0.25
EXCHANGE_COEF = (3.0 / math.pi) ** (1.0 / 3.0)
LANES = 128
TILE = 8
CHUNK = 16
VMEM = pltpu.VMEM
MESH = pl.DeviceIdType.MESH
F32 = jnp.float32
BF16 = jnp.bfloat16


class Sizes:
    def __init__(self, owners, groups, levels, cells, grid_cells, pairs):
        self.owners, self.groups, self.levels, self.cells, self.pairs = owners, groups, levels, cells, pairs
        self.side, self.grid = math.isqrt(cells), math.isqrt(grid_cells)
        self.depth = levels // owners
        self.each = pairs // owners
        self.rows = cells // LANES
        self.per = LANES // self.side
        self.slab = self.depth * self.rows
        self.grid_rows = grid_cells // LANES
        self.halves = self.per * self.grid // LANES
        self.waves = 2 * levels
        self.turns = 2 * self.side // self.per
        self.wide = self.per * 2 * self.side
        self.block = self.turns * CHUNK
        self.chunks = self.waves // CHUNK


def halves_of(table):
    high = table.astype(ml_dtypes.bfloat16)
    low = (table - high.astype(np.float64)).astype(ml_dtypes.bfloat16)
    return high, low


def cas(angle):
    return np.cos(angle) + np.sin(angle)


def tables(n):
    side, per, levels = n.side, n.per, n.levels
    along_z = cas(2.0 * np.pi / n.waves * np.outer(np.arange(n.waves), np.arange(levels)))
    high, low = halves_of(along_z)
    to_waves = np.concatenate([high, high, low], axis=1)
    high, low = halves_of(along_z.T)
    from_waves = np.concatenate([high, high, low], axis=1)
    along_x = cas(np.pi / side * np.outer(np.arange(side), np.arange(2 * side)))
    phase = 2.0 * np.pi / per * np.outer(np.arange(per), np.arange(per))
    lane = np.concatenate(
        [np.einsum("yh,xk->yxhk", wave(phase), along_x).reshape(LANES, n.wide) for wave in (np.cos, np.sin)]
    )
    lane = np.stack(halves_of(lane))
    lane_back = np.ascontiguousarray(np.swapaxes(lane, 1, 2))
    angle = np.pi / side * np.outer(np.arange(n.turns), np.arange(LANES) // side)
    twiddle = np.concatenate([cas(angle), cas(-angle)]).astype(np.float32)

    def squares(length):
        m = np.arange(length)
        return (2.0 * np.pi / length * np.where(m < length // 2, m, m - length)) ** 2

    z = squares(n.waves).reshape(n.chunks, 1, CHUNK, 1, 1)
    y = squares(2 * side).reshape(per, n.turns).T.reshape(1, n.turns, 1, per, 1)
    x = squares(2 * side).reshape(1, 1, 1, 1, 2 * side)
    green = 4.0 * np.pi / (z + y + x + SCREEN) / (n.waves * 4.0 * side * side)
    green = green.reshape(n.chunks * n.block, n.wide).astype(np.float32)
    spread = np.zeros((LANES, n.halves * LANES), ml_dtypes.bfloat16)
    for cell in range(LANES):
        spread[cell, cell // side * n.grid + cell % side] = 1
    gather = np.ascontiguousarray(spread.T)
    return to_waves, from_waves, lane, lane_back, twiddle, green, spread, gather


def split(value):
    high = value.astype(BF16)
    return high, (value - high.astype(F32)).astype(BF16)


def dot(left, right):
    return jnp.dot(left, right, preferred_element_type=F32)


def thrice(high, low, matrix):
    return dot(high, matrix[0]) + dot(low, matrix[0]) + dot(high, matrix[1])


def flat_roll(value, amount):
    carried = lax.rem(amount, LANES)
    down = amount // LANES
    rows = value.shape[1]
    turned = pltpu.roll(value, carried, axis=2)
    here = pltpu.roll(turned, down, axis=1)
    above = pltpu.roll(turned, lax.rem(down + 1, rows), axis=1)
    lane = lax.broadcasted_iota(jnp.int32, value.shape, 2)
    return jnp.where(lane >= carried, here, above)


def slide(n, value, shift_y, shift_x):
    shape = value.shape
    value = value.reshape(shape[0] // n.rows, n.rows, LANES)
    row = lax.broadcasted_iota(jnp.int32, value.shape, 1)
    lane = lax.broadcasted_iota(jnp.int32, value.shape, 2)
    y = row * n.per + lane // n.side - shift_y
    x = lax.rem(lane, n.side) - shift_x
    inside = (y >= 0) & (y < n.side) & (x >= 0) & (x < n.side)
    amount = lax.rem(shift_y * n.side + shift_x + 2 * n.cells, n.cells)
    return jnp.where(inside, flat_roll(value, amount), 0.0).reshape(shape)


def wave_sums(n, values):
    top, half = n.turns // 2, n.turns // 4
    cosines, sines = [None] * (top + 1), [None] * (top + 1)
    for q in range(half + 1):
        sums = []
        for wave in (math.cos, math.sin):
            for parity in (0, 1):
                total = None
                for s in range(parity, n.rows, 2):
                    factor = wave(2.0 * math.pi * q * s / n.turns)
                    total = weighted(total, factor, values[s])
                sums.append(total)
        even_cos, odd_cos, even_sin, odd_sin = sums
        cosines[q] = plus(even_cos, odd_cos)
        cosines[top - q] = minus(even_cos, odd_cos)
        sines[q] = plus(even_sin, odd_sin)
        sines[top - q] = minus(odd_sin, even_sin)
    return cosines, sines


def weighted(total, factor, value):
    if value is None or abs(factor) < 1e-12:
        return total
    if abs(abs(factor) - 1.0) < 1e-12:
        if factor > 0:
            return value if total is None else total + value
        return -value if total is None else total - value
    term = factor * value
    return term if total is None else total + term


def plus(left, right):
    if left is None or right is None:
        return right if left is None else left
    return left + right


def minus(left, right):
    if right is None:
        return left
    return -right if left is None else left - right


def cell_sums(n, cosines, sines):
    top, half = n.turns // 2, n.turns // 4
    values = []
    folded = {}
    for q in range(half + 1):
        if q == top - q:
            folded[q] = (cosines[q], cosines[q], sines[q], sines[q])
        else:
            c, d, s, t = cosines[q], cosines[top - q], sines[q], sines[top - q]
            folded[q] = (plus(c, d), minus(c, d), minus(s, t), plus(s, t))
    for s in range(n.rows):
        total = None
        odd = s % 2
        for q in range(half + 1):
            angle = 2.0 * math.pi * q * s / n.turns
            total = weighted(total, math.cos(angle), folded[q][odd])
            total = weighted(total, math.sin(angle), folded[q][2 + odd])
        values.append(total)
    return values


def solve(n, rho, stack, waves, high_ref, low_ref, back, spectrum, to_waves, from_waves, lane, lane_back, twiddle, green):
    levels = n.levels
    for s in range(n.rows):
        columns = slice(s * LANES, (s + 1) * LANES)
        high, low = split(rho[pl.ds(s, levels, stride=n.rows), :])
        stack[0:levels, columns] = high
        stack[levels : 2 * levels, columns] = low
        stack[2 * levels : 3 * levels, columns] = high
    waves[...] = dot(to_waves[...], stack[...])
    top = n.turns // 2
    for chunk in range(n.chunks):
        band = slice(chunk * CHUNK, (chunk + 1) * CHUNK)
        cosines, sines = wave_sums(n, [waves[band, s * LANES : (s + 1) * LANES] for s in range(n.rows)])
        for q in range(n.turns):
            same = q <= top
            a = cosines[q if same else n.turns - q]
            b = sines[q if same else n.turns - q]
            ahead = twiddle[q : q + 1, :]
            behind = twiddle[n.turns + q : n.turns + q + 1, :]
            u, w = ahead * a, behind * a
            if b is not None and q % top:
                u = u + behind * b if same else u - behind * b
                w = w - ahead * b if same else w + ahead * b
            rows = slice(chunk * n.block + q * CHUNK, chunk * n.block + (q + 1) * CHUNK)
            for index, part in enumerate((u, w)):
                columns = slice(index * LANES, (index + 1) * LANES)
                high_ref[rows, columns], low_ref[rows, columns] = split(part)
    for chunk in range(n.chunks):
        rows = slice(chunk * n.block, (chunk + 1) * n.block)
        value = thrice(high_ref[rows, :], low_ref[rows, :], lane) * green[rows, :]
        high, low = split(value)
        back[rows, :] = thrice(high, low, lane_back)
    for chunk in range(n.chunks):
        cosines, sines = [None] * (top + 1), [None] * (top + 1)
        for q in range(n.turns):
            rows = slice(chunk * n.block + q * CHUNK, chunk * n.block + (q + 1) * CHUNK)
            u, w = back[rows, 0:LANES], back[rows, LANES : 2 * LANES]
            ahead = twiddle[q : q + 1, :]
            behind = twiddle[n.turns + q : n.turns + q + 1, :]
            a = ahead * u + behind * w
            if q <= top:
                cosines[q] = a
            else:
                cosines[n.turns - q] = cosines[n.turns - q] + a
            if q % top:
                b = behind * u - ahead * w
                sines[q if q <= top else n.turns - q] = (
                    b if q <= top else sines[n.turns - q] - b
                )
        values = cell_sums(n, cosines, sines)
        for s in range(n.rows):
            columns = slice(s * LANES, (s + 1) * LANES)
            high, low = split(values[s])
            for place, part in enumerate((high, low, high)):
                start = place * n.waves + chunk * CHUNK
                spectrum[start : start + CHUNK, columns] = part
    return dot(from_waves[...], spectrum[...])


def kernel(n, pairs, offsets, orbital, external, *refs):
    table_refs, refs = refs[:8], refs[8:]
    out, refs = refs[0], refs[1:]
    table_dst, refs = refs[:8], refs[8:]
    (own_box, flat, box_send, box_land, place_send, place_land, corner, near, moved, rho_send, rho_land) = refs[:11]
    (field_send, field_land, ext_block, ext_flat, dens_grid, dens_send, dens_land, level, read_in, read) = refs[11:21]
    (grad_send, stack, waves, high_ref, low_ref, back, spectrum) = refs[21:28]
    local_sem, own_send, own_recv, grp_send, grp_recv = refs[28:]
    to_waves, from_waves, lane, lane_back, twiddle, green, spread, gather = table_dst
    owners, groups, depth, slab = n.owners, n.groups, n.depth, n.slab
    me, team = lax.axis_index("own"), lax.axis_index("grp")

    own_in = pltpu.make_async_copy(orbital, own_box, local_sem.at[0])
    own_in.start()
    first_level = pl.multiple_of(me * depth // TILE * TILE, TILE)
    taken = ext_block.shape[0]
    ext_in = pltpu.make_async_copy(external.at[pl.ds(first_level, taken)], ext_block, local_sem.at[1])
    ext_in.start()
    table_in = [
        pltpu.make_async_copy(source, target, local_sem.at[2 + i])
        for i, (source, target) in enumerate(zip(table_refs, table_dst))
    ]
    for item in table_in:
        item.start()
    barrier = pltpu.get_barrier_semaphore()
    for step in range(1, owners):
        peer = lax.rem(me + step, owners)
        pl.semaphore_signal(barrier, inc=1, device_id={"own": peer}, device_id_type=MESH)
    for step in range(1, groups):
        peer = lax.rem(team + step, groups)
        pl.semaphore_signal(barrier, inc=1, device_id={"grp": peer}, device_id_type=MESH)

    row_index = lax.broadcasted_iota(jnp.int32, place_send.shape, 0)
    place_send[...] = jnp.where(row_index == 0, offsets[0, 0], offsets[0, 1])
    own_in.wait()
    for s in range(n.rows):
        flat[pl.ds(s, n.levels, stride=n.rows), :] = own_box[:, s * LANES : (s + 1) * LANES].astype(F32)
    for owner in range(owners):
        box_send[owner] = flat[owner * slab : (owner + 1) * slab, :].astype(BF16)
    pl.semaphore_wait(barrier, owners + groups - 2)

    def to_owner(phase, step, source, target):
        peer = lax.rem(me + step, owners)
        return pltpu.make_async_remote_copy(
            src_ref=source,
            dst_ref=target,
            send_sem=own_send.at[phase, step],
            recv_sem=own_recv.at[phase, step],
            device_id={"own": peer},
            device_id_type=MESH,
        )

    def part(ref, index, size):
        return ref.at[pl.ds(pl.multiple_of(index * size, size), size)]

    sent = []
    boxes_in = []
    for step in range(1, owners):
        peer = lax.rem(me + step, owners)
        boxes_in.append(to_owner(0, step, place_send, place_land.at[me]))
        boxes_in.append(to_owner(1, step, box_send.at[peer], box_land.at[me]))
        boxes_in[-2].start()
        boxes_in[-1].start()
    sent += boxes_in
    place_land[me] = place_send[...]
    box_land[me] = box_send[me]
    for item in boxes_in:
        item.wait_recv()
    for owner in range(owners):
        corner[owner, 0] = place_land[owner, 0, 0]
        corner[owner, 1] = place_land[owner, 1, 0]

    def shift_of(row):
        first, second = pairs[row, 0], pairs[row, 1]
        return corner[second, 0] - corner[first, 0], corner[second, 1] - corner[first, 1]

    rho_in = []
    bundle = n.each * slab
    for step in [*range(1, owners), 0]:
        peer = lax.rem(me + step, owners)
        for turn in range(n.each):
            row = peer * n.each + turn
            dy, dx = shift_of(row)
            a = box_land[pairs[row, 0]].astype(F32)
            b = slide(n, box_land[pairs[row, 1]].astype(F32), dy, dx)
            near[row] = a
            moved[row] = b
            if step:
                rho_send[peer, turn] = a * b
            else:
                rho_land[turn, pl.ds(pl.multiple_of(me * slab, slab), slab), :] = a * b
        if step:
            for turn in range(n.each):
                target = rho_land.at[turn, pl.ds(pl.multiple_of(me * slab, slab), slab)]
                rho_in.append(to_owner(2 + turn, step, rho_send.at[peer, turn], target))
                rho_in[-1].start()
    sent += rho_in

    for item in table_in:
        item.wait()
    grid_shape = (depth, n.grid_rows, LANES)
    for owner in range(owners):
        value = box_land[owner].astype(F32)
        high, low = split(value * value)
        wide = dot(high, spread[...]) + dot(low, spread[...])
        for z in range(depth):
            start = z * n.grid_rows
            for half in range(n.halves):
                rows = pl.ds(start + half, n.rows, stride=n.halves)
                dens_grid[owner, rows, :] = wide[z * n.rows : (z + 1) * n.rows, half * LANES : (half + 1) * LANES]
            rest = n.grid_rows - n.rows * n.halves
            dens_grid[owner, start + n.rows * n.halves : start + n.grid_rows, :] = jnp.zeros((rest, LANES), F32)
    total = jnp.zeros(grid_shape, F32)
    for owner in range(owners):
        amount = corner[owner, 0] * n.grid + corner[owner, 1]
        total = total + flat_roll(dens_grid[owner].reshape(grid_shape), amount)
    dens_send[...] = total.reshape(dens_send.shape)
    dens_in = []
    for step in range(1, groups):
        dens_in.append(
            pltpu.make_async_remote_copy(
                src_ref=dens_send,
                dst_ref=dens_land.at[step],
                send_sem=grp_send.at[step],
                recv_sem=grp_recv.at[step],
                device_id={"grp": lax.rem(team + step, groups)},
                device_id_type=MESH,
            )
        )
        dens_in[-1].start()
    sent += dens_in

    for item in rho_in:
        item.wait_recv()
    field_in = []
    for turn in range(n.each):
        field = solve(
            n, rho_land.at[turn], stack, waves, high_ref, low_ref, back, spectrum,
            to_waves, from_waves, lane, lane_back, twiddle, green,
        )
        for s in range(n.rows):
            field_send[turn, pl.ds(s, n.levels, stride=n.rows), :] = field[:, s * LANES : (s + 1) * LANES]
        for step in range(1, owners):
            peer = lax.rem(me + step, owners)
            source = field_send.at[turn, pl.ds(pl.multiple_of(peer * slab, slab), slab)]
            field_in.append(to_owner(2 + n.each + turn, step, source, field_land.at[me * n.each + turn]))
            field_in[-1].start()
        field_land[me * n.each + turn] = field_send[turn, pl.ds(pl.multiple_of(me * slab, slab), slab), :]
    sent += field_in

    ext_in.wait()
    ext_values = ext_block[...].astype(F32)
    for k in range(n.grid_rows):
        ext_flat[pl.ds(k, taken, stride=n.grid_rows), :] = ext_values[:, k * LANES : (k + 1) * LANES]
    for item in dens_in:
        item.wait_recv()
    density = dens_send[...]
    for step in range(1, groups):
        density = density + dens_land[step]
    start = pl.multiple_of((me * depth - first_level) * n.grid_rows, n.grid_rows)
    outside = ext_flat[pl.ds(start, depth * n.grid_rows), :]
    safe = jnp.where(density > 0.0, density, 1.0)
    root = jnp.exp(jnp.log(safe) * (1.0 / 3.0))
    root = root - (root - safe / (root * root)) * (1.0 / 3.0)
    level[...] = outside - EXCHANGE_COEF * jnp.where(density > 0.0, root, 0.0)
    whole = n.grid_rows * LANES
    for owner in range(owners):
        amount = lax.rem(whole - corner[owner, 0] * n.grid - corner[owner, 1], whole)
        turned = flat_roll(level[...].reshape(grid_shape), amount)
        read_in[owner] = turned.reshape(read_in.shape[1:])
        parts = []
        for z in range(depth):
            pieces = [
                read_in[owner, pl.ds(z * n.grid_rows + half, n.rows, stride=n.halves), :] for half in range(n.halves)
            ]
            parts.append(jnp.concatenate(pieces, axis=1) if n.halves > 1 else pieces[0])
        value = jnp.concatenate(parts, axis=0) if depth > 1 else parts[0]
        high, low = split(value)
        read[owner] = (dot(high, gather[...]) + dot(low, gather[...])) * box_land[owner].astype(F32)

    for item in field_in:
        item.wait_recv()
    for row in range(n.pairs):
        dy, dx = shift_of(row)
        field = field_land[row] * MIXING
        moved[row] = field * moved[row]
        near[row] = slide(n, field * near[row], -dy, -dx)
    grad_in = []
    for step in [*range(1, owners), 0]:
        peer = lax.rem(me + step, owners)
        total = read[peer]
        for row in range(n.pairs):
            total = total - jnp.where(pairs[row, 0] == peer, moved[row], 0.0)
            total = total - jnp.where(pairs[row, 1] == peer, near[row], 0.0)
        if step:
            grad_send[peer] = total
            grad_in.append(to_owner(2 + 2 * n.each, step, grad_send.at[peer], out.at[me]))
            grad_in[-1].start()
        else:
            out[me] = total
    sent += grad_in
    for item in grad_in:
        item.wait_recv()
    for item in sent:
        item.wait_send()


def relayout_kernel(n, slabs, out):
    for owner in range(n.owners):
        for z in range(n.depth):
            rows = slabs[owner, z * n.rows : (z + 1) * n.rows, :]
            for s in range(n.rows):
                row = owner * n.depth + z
                out[row : row + 1, s * LANES : (s + 1) * LANES] = rows[s : s + 1, :]


def body(owners, groups, orbitals, offsets, pairs, ext_pot):
    _, levels, cells = orbitals.shape
    n = Sizes(owners, groups, levels, cells, ext_pot.shape[1], pairs.shape[0])
    consts = tables(n)
    taken = max(n.depth, TILE)
    slabs = (n.owners, n.slab, LANES)
    flat_rows = levels * n.rows
    scratch = [VMEM(c.shape, c.dtype) for c in consts]
    scratch += [
        VMEM((levels, cells), BF16),
        VMEM((flat_rows, LANES), F32),
        VMEM(slabs, BF16),
        VMEM(slabs, BF16),
        VMEM((TILE, LANES), jnp.int32),
        VMEM((owners, TILE, LANES), jnp.int32),
        pltpu.SMEM((owners, 2), jnp.int32),
        VMEM((n.pairs, n.slab, LANES), F32),
        VMEM((n.pairs, n.slab, LANES), F32),
        VMEM((owners, n.each, n.slab, LANES), F32),
        VMEM((n.each, flat_rows, LANES), F32),
        VMEM((n.each, flat_rows, LANES), F32),
        VMEM((n.pairs, n.slab, LANES), F32),
        VMEM((taken, ext_pot.shape[1]), BF16),
        VMEM((taken * n.grid_rows, LANES), F32),
        VMEM((owners, n.depth * n.grid_rows, LANES), F32),
        VMEM((n.depth * n.grid_rows, LANES), F32),
        VMEM((groups, n.depth * n.grid_rows, LANES), F32),
        VMEM((n.depth * n.grid_rows, LANES), F32),
        VMEM((owners, n.depth * n.grid_rows, LANES), F32),
        VMEM(slabs, F32),
        VMEM(slabs, F32),
        VMEM((3 * levels, cells), BF16),
        VMEM((n.waves, cells), F32),
        VMEM((n.chunks * n.block, 2 * LANES), BF16),
        VMEM((n.chunks * n.block, 2 * LANES), BF16),
        VMEM((n.chunks * n.block, 2 * LANES), F32),
        VMEM((3 * n.waves, cells), BF16),
        pltpu.SemaphoreType.DMA((2 + len(consts),)),
        pltpu.SemaphoreType.DMA((3 + 2 * n.each, owners)),
        pltpu.SemaphoreType.DMA((3 + 2 * n.each, owners)),
        pltpu.SemaphoreType.DMA((groups,)),
        pltpu.SemaphoreType.DMA((groups,)),
    ]
    smem = pl.BlockSpec(memory_space=pltpu.SMEM)
    anywhere = pl.BlockSpec(memory_space=pl.ANY)
    slab_out = pl.pallas_call(
        functools.partial(kernel, n),
        out_shape=jax.ShapeDtypeStruct(slabs, F32),
        in_specs=[smem, smem] + [anywhere] * (2 + len(consts)),
        out_specs=pl.BlockSpec(memory_space=VMEM),
        scratch_shapes=scratch,
        compiler_params=pltpu.CompilerParams(collective_id=0, has_side_effects=True),
        name="gradient",
    )(pairs, offsets, orbitals[0], ext_pot, *consts)
    gradient = pl.pallas_call(
        functools.partial(relayout_kernel, n),
        out_shape=jax.ShapeDtypeStruct((levels, cells), F32),
        in_specs=[pl.BlockSpec(memory_space=VMEM)],
        out_specs=pl.BlockSpec(memory_space=VMEM),
        name="relayout",
    )(slab_out)
    return gradient[None]


def solution(mesh):
    in_specs = (P(("grp", "own"), None, None), P(("grp", "own"), None), P("grp", None), P())
    out_specs = P(("grp", "own"), None, None)
    run = functools.partial(body, mesh.shape["own"], mesh.shape["grp"])
    return jax.shard_map(run, mesh=mesh, in_specs=in_specs, out_specs=out_specs, check_vma=False)
```

```python
import functools
import math

import jax
import jax.numpy as jnp
import ml_dtypes
import numpy as np
from jax import lax
from jax.experimental import pallas as pl
from jax.experimental.pallas import tpu as pltpu
from jax.sharding import PartitionSpec as P

SCREEN = 0.0025
MIXING = 0.25
EXCHANGE_COEF = (3.0 / math.pi) ** (1.0 / 3.0)
LANES = 128
TILE = 8
CHUNK = 16
VMEM = pltpu.VMEM
MESH = pl.DeviceIdType.MESH
F32 = jnp.float32
BF16 = jnp.bfloat16


class Sizes:
    def __init__(self, owners, groups, levels, cells, grid_cells, pairs):
        self.owners, self.groups, self.levels, self.cells, self.pairs = owners, groups, levels, cells, pairs
        self.side, self.grid = math.isqrt(cells), math.isqrt(grid_cells)
        self.depth = levels // owners
        self.each = pairs // owners
        self.rows = cells // LANES
        self.per = LANES // self.side
        self.slab = self.depth * self.rows
        self.grid_rows = grid_cells // LANES
        self.halves = self.per * self.grid // LANES
        self.waves = 2 * levels
        self.turns = 2 * self.side // self.per
        self.wide = self.per * 2 * self.side
        self.block = self.turns * CHUNK
        self.chunks = self.waves // CHUNK


def halves_of(table):
    high = table.astype(ml_dtypes.bfloat16)
    low = (table - high.astype(np.float64)).astype(ml_dtypes.bfloat16)
    return high, low


def cas(angle):
    return np.cos(angle) + np.sin(angle)


def tables(n):
    side, per, levels = n.side, n.per, n.levels
    along_z = cas(2.0 * np.pi / n.waves * np.outer(np.arange(n.waves), np.arange(levels)))
    high, low = halves_of(along_z)
    to_waves = np.concatenate([high, high, low], axis=1)
    high, low = halves_of(along_z.T)
    from_waves = np.concatenate([high, high, low], axis=1)
    along_x = cas(np.pi / side * np.outer(np.arange(side), np.arange(2 * side)))
    phase = 2.0 * np.pi / per * np.outer(np.arange(per), np.arange(per))
    lane = np.concatenate(
        [np.einsum("yh,xk->yxhk", wave(phase), along_x).reshape(LANES, n.wide) for wave in (np.cos, np.sin)]
    )
    lane = np.stack(halves_of(lane))
    lane_back = np.ascontiguousarray(np.swapaxes(lane, 1, 2))
    angle = np.pi / side * np.outer(np.arange(n.turns), np.arange(LANES) // side)
    twiddle = np.concatenate([cas(angle), cas(-angle)]).astype(np.float32)

    def squares(length):
        m = np.arange(length)
        return (2.0 * np.pi / length * np.where(m < length // 2, m, m - length)) ** 2

    z = squares(n.waves).reshape(n.chunks, 1, CHUNK, 1, 1)
    y = squares(2 * side).reshape(per, n.turns).T.reshape(1, n.turns, 1, per, 1)
    x = squares(2 * side).reshape(1, 1, 1, 1, 2 * side)
    green = 4.0 * np.pi / (z + y + x + SCREEN) / (n.waves * 4.0 * side * side)
    green = green.reshape(n.chunks * n.block, n.wide).astype(np.float32)
    spread = np.zeros((LANES, n.halves * LANES), ml_dtypes.bfloat16)
    for cell in range(LANES):
        spread[cell, cell // side * n.grid + cell % side] = 1
    gather = np.ascontiguousarray(spread.T)
    return to_waves, from_waves, lane, lane_back, twiddle, green, spread, gather


def far_first(n, me):
    near = n.owners >> ((n.owners.bit_length() - 1) // 2)
    near = n.owners // near
    far = n.owners // near
    z, y = me // near, lax.rem(me, near)
    low = (z < far // 2).astype(jnp.int32)
    here = low * (far - 1 - z) + (1 - low) * z
    peers = []
    for k in range(far - 1):
        place = k + (k >= here).astype(jnp.int32)
        level = low * (far - 1 - place) + (1 - low) * place
        peers += [level * near + lax.rem(y + 1 + step, near) for step in range(near)]
    return peers + [z * near + lax.rem(y + step, near) for step in range(1, near + 1)]


def split(value):
    high = value.astype(BF16)
    return high, (value - high.astype(F32)).astype(BF16)


def dot(left, right):
    return jnp.dot(left, right, preferred_element_type=F32)


def thrice(high, low, matrix):
    return dot(high, matrix[0]) + dot(low, matrix[0]) + dot(high, matrix[1])


def flat_roll(value, amount):
    carried = lax.rem(amount, LANES)
    down = amount // LANES
    rows = value.shape[1]
    turned = pltpu.roll(value, carried, axis=2)
    here = pltpu.roll(turned, down, axis=1)
    above = pltpu.roll(turned, lax.rem(down + 1, rows), axis=1)
    lane = lax.broadcasted_iota(jnp.int32, value.shape, 2)
    return jnp.where(lane >= carried, here, above)


def slide(n, value, shift_y, shift_x):
    shape = value.shape
    value = value.reshape(shape[0] // n.rows, n.rows, LANES)
    row = lax.broadcasted_iota(jnp.int32, value.shape, 1)
    lane = lax.broadcasted_iota(jnp.int32, value.shape, 2)
    y = row * n.per + lane // n.side - shift_y
    x = lax.rem(lane, n.side) - shift_x
    inside = (y >= 0) & (y < n.side) & (x >= 0) & (x < n.side)
    amount = lax.rem(shift_y * n.side + shift_x + 2 * n.cells, n.cells)
    return jnp.where(inside, flat_roll(value, amount), 0.0).reshape(shape)


def wave_sums(n, values):
    top, half = n.turns // 2, n.turns // 4
    cosines, sines = [None] * (top + 1), [None] * (top + 1)
    for q in range(half + 1):
        sums = []
        for wave in (math.cos, math.sin):
            for parity in (0, 1):
                total = None
                for s in range(parity, n.rows, 2):
                    factor = wave(2.0 * math.pi * q * s / n.turns)
                    total = weighted(total, factor, values[s])
                sums.append(total)
        even_cos, odd_cos, even_sin, odd_sin = sums
        cosines[q] = plus(even_cos, odd_cos)
        cosines[top - q] = minus(even_cos, odd_cos)
        sines[q] = plus(even_sin, odd_sin)
        sines[top - q] = minus(odd_sin, even_sin)
    return cosines, sines


def weighted(total, factor, value):
    if value is None or abs(factor) < 1e-12:
        return total
    if abs(abs(factor) - 1.0) < 1e-12:
        if factor > 0:
            return value if total is None else total + value
        return -value if total is None else total - value
    term = factor * value
    return term if total is None else total + term


def plus(left, right):
    if left is None or right is None:
        return right if left is None else left
    return left + right


def minus(left, right):
    if right is None:
        return left
    return -right if left is None else left - right


def cell_sums(n, cosines, sines):
    top, half = n.turns // 2, n.turns // 4
    values = []
    folded = {}
    for q in range(half + 1):
        if q == top - q:
            folded[q] = (cosines[q], cosines[q], sines[q], sines[q])
        else:
            c, d, s, t = cosines[q], cosines[top - q], sines[q], sines[top - q]
            folded[q] = (plus(c, d), minus(c, d), minus(s, t), plus(s, t))
    for s in range(n.rows):
        total = None
        odd = s % 2
        for q in range(half + 1):
            angle = 2.0 * math.pi * q * s / n.turns
            total = weighted(total, math.cos(angle), folded[q][odd])
            total = weighted(total, math.sin(angle), folded[q][2 + odd])
        values.append(total)
    return values


def solve(n, rho, stack, waves, high_ref, low_ref, back, spectrum, to_waves, from_waves, lane, lane_back, twiddle, green):
    levels = n.levels
    for s in range(n.rows):
        columns = slice(s * LANES, (s + 1) * LANES)
        high, low = split(rho[pl.ds(s, levels, stride=n.rows), :])
        stack[0:levels, columns] = high
        stack[levels : 2 * levels, columns] = low
        stack[2 * levels : 3 * levels, columns] = high
    waves[...] = dot(to_waves[...], stack[...])
    top = n.turns // 2
    for chunk in range(n.chunks):
        band = slice(chunk * CHUNK, (chunk + 1) * CHUNK)
        cosines, sines = wave_sums(n, [waves[band, s * LANES : (s + 1) * LANES] for s in range(n.rows)])
        for q in range(n.turns):
            same = q <= top
            a = cosines[q if same else n.turns - q]
            b = sines[q if same else n.turns - q]
            ahead = twiddle[q : q + 1, :]
            behind = twiddle[n.turns + q : n.turns + q + 1, :]
            u, w = ahead * a, behind * a
            if b is not None and q % top:
                u = u + behind * b if same else u - behind * b
                w = w - ahead * b if same else w + ahead * b
            rows = slice(chunk * n.block + q * CHUNK, chunk * n.block + (q + 1) * CHUNK)
            for index, part in enumerate((u, w)):
                columns = slice(index * LANES, (index + 1) * LANES)
                high_ref[rows, columns], low_ref[rows, columns] = split(part)
    for chunk in range(n.chunks):
        rows = slice(chunk * n.block, (chunk + 1) * n.block)
        value = thrice(high_ref[rows, :], low_ref[rows, :], lane) * green[rows, :]
        high, low = split(value)
        back[rows, :] = thrice(high, low, lane_back)
    for chunk in range(n.chunks):
        cosines, sines = [None] * (top + 1), [None] * (top + 1)
        for q in range(n.turns):
            rows = slice(chunk * n.block + q * CHUNK, chunk * n.block + (q + 1) * CHUNK)
            u, w = back[rows, 0:LANES], back[rows, LANES : 2 * LANES]
            ahead = twiddle[q : q + 1, :]
            behind = twiddle[n.turns + q : n.turns + q + 1, :]
            a = ahead * u + behind * w
            if q <= top:
                cosines[q] = a
            else:
                cosines[n.turns - q] = cosines[n.turns - q] + a
            if q % top:
                b = behind * u - ahead * w
                sines[q if q <= top else n.turns - q] = (
                    b if q <= top else sines[n.turns - q] - b
                )
        values = cell_sums(n, cosines, sines)
        for s in range(n.rows):
            columns = slice(s * LANES, (s + 1) * LANES)
            high, low = split(values[s])
            for place, part in enumerate((high, low, high)):
                start = place * n.waves + chunk * CHUNK
                spectrum[start : start + CHUNK, columns] = part
    return dot(from_waves[...], spectrum[...])


def kernel(n, listed, placed, orbital, external, *refs):
    table_refs, refs = refs[:8], refs[8:]
    out, refs = refs[0], refs[1:]
    table_dst, refs = refs[:8], refs[8:]
    (own_box, flat, box_send, box_land, place_send, place_land, corner, near, moved, rho_send, rho_land) = refs[:11]
    (field_send, field_land, ext_block, ext_flat, dens_grid, dens_send, dens_land, level, read_in, read) = refs[11:21]
    (grad_send, stack, waves, high_ref, low_ref, back, spectrum) = refs[21:28]
    pairs, listed_in, placed_in, local_sem, own_send, own_recv, grp_send, grp_recv = refs[28:]
    to_waves, from_waves, lane, lane_back, twiddle, green, spread, gather = table_dst
    owners, groups, depth, slab = n.owners, n.groups, n.depth, n.slab
    me, team = lax.axis_index("own"), lax.axis_index("grp")
    partner = team + 1 - 2 * lax.rem(team, 2)
    barrier = pltpu.get_barrier_semaphore()
    peers = far_first(n, me)
    for peer in peers:
        there = {"own": peer, "grp": partner}
        pl.semaphore_signal(barrier, inc=1, device_id=there, device_id_type=MESH)
    base = team - lax.rem(team, 2)
    distant = [lax.rem(base + step, groups) for step in range(2, groups)]
    others = [*distant, partner]
    for peer in distant:
        pl.semaphore_signal(barrier, inc=1, device_id={"grp": peer}, device_id_type=MESH)

    small_in = [
        pltpu.make_async_copy(placed, placed_in, local_sem.at[2 + len(table_refs)]),
        pltpu.make_async_copy(listed, listed_in, local_sem.at[3 + len(table_refs)]),
    ]
    for item in small_in:
        item.start()
    own_in = pltpu.make_async_copy(orbital, own_box, local_sem.at[0])
    own_in.start()
    first_level = pl.multiple_of(me * depth // TILE * TILE, TILE)
    taken = ext_block.shape[0]
    ext_in = pltpu.make_async_copy(external.at[pl.ds(first_level, taken)], ext_block, local_sem.at[1])
    ext_in.start()
    table_in = [
        pltpu.make_async_copy(source, target, local_sem.at[2 + i])
        for i, (source, target) in enumerate(zip(table_refs, table_dst))
    ]
    for item in table_in:
        item.start()
    row_index = lax.broadcasted_iota(jnp.int32, place_send.shape, 0)
    for item in small_in:
        item.wait()
    pair_index = lax.broadcasted_iota(jnp.int32, listed_in.shape, 1)
    header = jnp.where(row_index == 0, placed_in[0:1, 0:1], placed_in[0:1, 1:2])
    for turn in range(n.each):
        mine = jnp.sum(jnp.where(pair_index == me * n.each + turn, listed_in[...], 0), axis=1, keepdims=True)
        header = jnp.where(row_index == 2 + 2 * turn, mine[0:1], header)
        header = jnp.where(row_index == 3 + 2 * turn, mine[1:2], header)
    place_send[...] = header
    own_in.wait()
    for s in range(n.rows):
        flat[pl.ds(s, n.levels, stride=n.rows), :] = own_box[:, s * LANES : (s + 1) * LANES].astype(F32)
    for owner in range(owners):
        box_send[owner] = flat[owner * slab : (owner + 1) * slab, :].astype(BF16)
    pl.semaphore_wait(barrier, owners + groups - 2)

    def to_owner(phase, peer, source, target):
        return pltpu.make_async_remote_copy(
            src_ref=source,
            dst_ref=target,
            send_sem=own_send.at[phase, peer],
            recv_sem=own_recv.at[phase, me],
            device_id={"own": peer, "grp": partner},
            device_id_type=MESH,
        )

    def arrived(phase, source, target):
        for peer in reversed(peers):
            pltpu.make_async_remote_copy(
                src_ref=source,
                dst_ref=target(peer),
                send_sem=own_send.at[phase, peer],
                recv_sem=own_recv.at[phase, peer],
                device_id={"own": peer, "grp": partner},
                device_id_type=MESH,
            ).wait_recv()

    def rows_of(index):
        return pl.ds(pl.multiple_of(index * slab, slab), slab)

    sent = []
    boxes_in = []
    for peer in peers:
        boxes_in.append(to_owner(0, peer, place_send, place_land.at[me]))
        boxes_in.append(to_owner(1, peer, box_send.at[peer], box_land.at[me]))
        boxes_in[-2].start()
        boxes_in[-1].start()
    sent += boxes_in
    arrived(0, place_send, lambda peer: place_land.at[peer])
    arrived(1, box_send.at[0], lambda peer: box_land.at[peer])
    for owner in range(owners):
        corner[owner, 0] = place_land[owner, 0, 0]
        corner[owner, 1] = place_land[owner, 1, 0]
        for turn in range(n.each):
            pairs[owner * n.each + turn, 0] = place_land[owner, 2 + 2 * turn, 0]
            pairs[owner * n.each + turn, 1] = place_land[owner, 3 + 2 * turn, 0]

    def shift_of(row):
        first, second = pairs[row, 0], pairs[row, 1]
        return corner[second, 0] - corner[first, 0], corner[second, 1] - corner[first, 1]

    rho_in = []
    for peer in peers:
        for turn in range(n.each):
            row = peer * n.each + turn
            dy, dx = shift_of(row)
            a = box_land[pairs[row, 0]].astype(F32)
            b = slide(n, box_land[pairs[row, 1]].astype(F32), dy, dx)
            near[row] = a
            moved[row] = b
            rho_send[peer, turn] = a * b
            rho_in.append(to_owner(2 + turn, peer, rho_send.at[peer, turn], rho_land.at[turn, rows_of(me)]))
            rho_in[-1].start()
    sent += rho_in

    for item in table_in:
        item.wait()
    grid_shape = (depth, n.grid_rows, LANES)
    for owner in range(owners):
        value = box_land[owner].astype(F32)
        high, low = split(value * value)
        wide = dot(high, spread[...]) + dot(low, spread[...])
        for z in range(depth):
            start = z * n.grid_rows
            for half in range(n.halves):
                rows = pl.ds(start + half, n.rows, stride=n.halves)
                dens_grid[owner, rows, :] = wide[z * n.rows : (z + 1) * n.rows, half * LANES : (half + 1) * LANES]
            rest = n.grid_rows - n.rows * n.halves
            dens_grid[owner, start + n.rows * n.halves : start + n.grid_rows, :] = jnp.zeros((rest, LANES), F32)
    total = jnp.zeros(grid_shape, F32)
    for owner in range(owners):
        amount = corner[owner, 0] * n.grid + corner[owner, 1]
        total = total + flat_roll(dens_grid[owner].reshape(grid_shape), amount)
    dens_send[...] = total.reshape(dens_send.shape)
    dens_land[team] = dens_send[...]

    def dens_copy(peer, sender):
        return pltpu.make_async_remote_copy(
            src_ref=dens_send,
            dst_ref=dens_land.at[sender],
            send_sem=grp_send.at[peer],
            recv_sem=grp_recv.at[sender],
            device_id={"grp": peer},
            device_id_type=MESH,
        )

    for peer in others:
        dens_copy(peer, team).start()

    for turn in range(n.each):
        arrived(2 + turn, rho_send.at[0, turn], lambda peer: rho_land.at[turn, rows_of(peer)])
    field_in = []
    for turn in range(n.each):
        field = solve(
            n, rho_land.at[turn], stack, waves, high_ref, low_ref, back, spectrum,
            to_waves, from_waves, lane, lane_back, twiddle, green,
        )
        for s in range(n.rows):
            field_send[turn, pl.ds(s, n.levels, stride=n.rows), :] = field[:, s * LANES : (s + 1) * LANES]
        for peer in peers:
            source = field_send.at[turn, rows_of(peer)]
            field_in.append(to_owner(2 + n.each + turn, peer, source, field_land.at[me * n.each + turn]))
            field_in[-1].start()
    sent += field_in

    ext_in.wait()
    ext_values = ext_block[...].astype(F32)
    for k in range(n.grid_rows):
        ext_flat[pl.ds(k, taken, stride=n.grid_rows), :] = ext_values[:, k * LANES : (k + 1) * LANES]
    for peer in others:
        dens_copy(peer, peer).wait_recv()
    density = dens_land[0]
    for index in range(1, groups):
        density = density + dens_land[index]
    start = pl.multiple_of((me * depth - first_level) * n.grid_rows, n.grid_rows)
    outside = ext_flat[pl.ds(start, depth * n.grid_rows), :]
    safe = jnp.where(density > 0.0, density, 1.0)
    root = jnp.exp(jnp.log(safe) * (1.0 / 3.0))
    root = root - (root - safe / (root * root)) * (1.0 / 3.0)
    level[...] = outside - EXCHANGE_COEF * jnp.where(density > 0.0, root, 0.0)
    whole = n.grid_rows * LANES
    for owner in range(owners):
        amount = lax.rem(whole - corner[owner, 0] * n.grid - corner[owner, 1], whole)
        turned = flat_roll(level[...].reshape(grid_shape), amount)
        read_in[owner] = turned.reshape(read_in.shape[1:])
        parts = []
        for z in range(depth):
            pieces = [
                read_in[owner, pl.ds(z * n.grid_rows + half, n.rows, stride=n.halves), :] for half in range(n.halves)
            ]
            parts.append(jnp.concatenate(pieces, axis=1) if n.halves > 1 else pieces[0])
        value = jnp.concatenate(parts, axis=0) if depth > 1 else parts[0]
        high, low = split(value)
        read[owner] = (dot(high, gather[...]) + dot(low, gather[...])) * box_land[owner].astype(F32)

    for turn in range(n.each):
        arrived(2 + n.each + turn, field_send.at[turn, 0:slab], lambda peer: field_land.at[peer * n.each + turn])
    for row in range(n.pairs):
        dy, dx = shift_of(row)
        field = field_land[row] * MIXING
        moved[row] = field * moved[row]
        near[row] = slide(n, field * near[row], -dy, -dx)
    for peer in peers:
        total = read[peer]
        for row in range(n.pairs):
            total = total - jnp.where(pairs[row, 0] == peer, moved[row], 0.0)
            total = total - jnp.where(pairs[row, 1] == peer, near[row], 0.0)
        grad_send[peer] = total
        sent.append(to_owner(2 + 2 * n.each, peer, grad_send.at[peer], out.at[rows_of(me)]))
        sent[-1].start()
    arrived(2 + 2 * n.each, grad_send.at[0], lambda peer: out.at[rows_of(peer)])
    for item in sent:
        item.wait_send()
    for peer in others:
        dens_copy(peer, team).wait_send()


def relayout_kernel(n, slabs, out):
    for s in range(n.rows):
        out[:, s * LANES : (s + 1) * LANES] = slabs[pl.ds(s, n.levels, stride=n.rows), :]


def body(owners, groups, orbitals, offsets, pairs, ext_pot):
    _, levels, cells = orbitals.shape
    n = Sizes(owners, groups, levels, cells, ext_pot.shape[1], pairs.shape[0])
    consts = tables(n)
    taken = max(n.depth, TILE)
    header = -(-(2 + 2 * n.each) // TILE) * TILE
    slabs = (n.owners, n.slab, LANES)
    flat_rows = levels * n.rows
    scratch = [VMEM(c.shape, c.dtype) for c in consts]
    scratch += [
        VMEM((levels, cells), BF16),
        VMEM((flat_rows, LANES), F32),
        VMEM(slabs, BF16),
        VMEM(slabs, BF16),
        VMEM((header, LANES), jnp.int32),
        VMEM((owners, header, LANES), jnp.int32),
        pltpu.SMEM((owners, 2), jnp.int32),
        VMEM((n.pairs, n.slab, LANES), F32),
        VMEM((n.pairs, n.slab, LANES), F32),
        VMEM((owners, n.each, n.slab, LANES), F32),
        VMEM((n.each, flat_rows, LANES), F32),
        VMEM((n.each, flat_rows, LANES), F32),
        VMEM((n.pairs, n.slab, LANES), F32),
        VMEM((taken, ext_pot.shape[1]), BF16),
        VMEM((taken * n.grid_rows, LANES), F32),
        VMEM((owners, n.depth * n.grid_rows, LANES), F32),
        VMEM((n.depth * n.grid_rows, LANES), F32),
        VMEM((groups, n.depth * n.grid_rows, LANES), F32),
        VMEM((n.depth * n.grid_rows, LANES), F32),
        VMEM((owners, n.depth * n.grid_rows, LANES), F32),
        VMEM(slabs, F32),
        VMEM(slabs, F32),
        VMEM((3 * levels, cells), BF16),
        VMEM((n.waves, cells), F32),
        VMEM((n.chunks * n.block, 2 * LANES), BF16),
        VMEM((n.chunks * n.block, 2 * LANES), BF16),
        VMEM((n.chunks * n.block, 2 * LANES), F32),
        VMEM((3 * n.waves, cells), BF16),
        pltpu.SMEM(pairs.shape, jnp.int32),
        VMEM(pairs.shape[::-1], jnp.int32),
        VMEM(offsets.shape, jnp.int32),
        pltpu.SemaphoreType.DMA((4 + len(consts),)),
        pltpu.SemaphoreType.DMA((3 + 2 * n.each, owners)),
        pltpu.SemaphoreType.DMA((3 + 2 * n.each, owners)),
        pltpu.SemaphoreType.DMA((groups,)),
        pltpu.SemaphoreType.DMA((groups,)),
    ]
    anywhere = pl.BlockSpec(memory_space=pl.ANY)
    slab_out = pl.pallas_call(
        functools.partial(kernel, n),
        out_shape=jax.ShapeDtypeStruct((flat_rows, LANES), F32),
        in_specs=[anywhere] * (4 + len(consts)),
        out_specs=pl.BlockSpec(memory_space=VMEM),
        scratch_shapes=scratch,
        compiler_params=pltpu.CompilerParams(collective_id=0, has_side_effects=True),
        name="gradient",
    )(pairs.T, offsets, orbitals[0], ext_pot, *consts)
    gradient = pl.pallas_call(
        functools.partial(relayout_kernel, n),
        out_shape=jax.ShapeDtypeStruct((levels, cells), F32),
        in_specs=[pl.BlockSpec(memory_space=VMEM)],
        out_specs=pl.BlockSpec(memory_space=VMEM),
        name="relayout",
    )(slab_out)
    return gradient[None]


def solution(mesh):
    in_specs = (P(("grp", "own"), None, None), P(("grp", "own"), None), P("grp", None), P())
    out_specs = P(("grp", "own"), None, None)
    run = functools.partial(body, mesh.shape["own"], mesh.shape["grp"])
    return jax.shard_map(run, mesh=mesh, in_specs=in_specs, out_specs=out_specs, check_vma=False)
```

```python
import functools
import math

import jax
import jax.numpy as jnp
import ml_dtypes
import numpy as np
from jax import lax
from jax.experimental import pallas as pl
from jax.experimental.pallas import tpu as pltpu
from jax.sharding import PartitionSpec as P

SCREEN = 0.0025
MIXING = 0.25
EXCHANGE_COEF = (3.0 / math.pi) ** (1.0 / 3.0)
LANES = 128
TILE = 8
VMEM = pltpu.VMEM
MESH = pl.DeviceIdType.MESH
F32 = jnp.float32
BF16 = jnp.bfloat16


class Sizes:
    def __init__(self, owners, groups, levels, cells, grid_cells, pairs):
        self.owners, self.groups, self.levels, self.cells, self.pairs = owners, groups, levels, cells, pairs
        self.side, self.grid = math.isqrt(cells), math.isqrt(grid_cells)
        self.depth = levels // owners
        self.each = pairs // owners
        self.rows = cells // LANES
        self.per = LANES // self.side
        self.slab = self.depth * self.rows
        self.grid_rows = grid_cells // LANES
        self.halves = self.per * self.grid // LANES
        self.waves = 2 * levels
        self.turns = 2 * self.side // self.per
        self.wide = self.per * 2 * self.side
        self.bands = levels // TILE
        self.share = TILE // self.depth


def halves_of(table):
    high = table.astype(ml_dtypes.bfloat16)
    low = (table - high.astype(np.float64)).astype(ml_dtypes.bfloat16)
    return high, low


def cas(angle):
    return np.cos(angle) + np.sin(angle)


def tables(n):
    side, per, levels = n.side, n.per, n.levels
    along_z = cas(2.0 * np.pi / n.waves * np.outer(np.arange(n.waves), np.arange(levels)))
    high, low = halves_of(along_z)
    to_waves = np.concatenate([high, high, low], axis=1)
    high, low = halves_of(along_z.T)
    from_waves = np.concatenate([high, high, low], axis=1)
    along_x = cas(np.pi / side * np.outer(np.arange(side), np.arange(2 * side)))
    phase = 2.0 * np.pi / per * np.outer(np.arange(per), np.arange(per))
    lane = np.concatenate(
        [np.einsum("yh,xk->yxhk", wave(phase), along_x).reshape(LANES, n.wide) for wave in (np.cos, np.sin)]
    )
    lane = np.stack(halves_of(lane))
    lane_back = np.ascontiguousarray(np.swapaxes(lane, 1, 2))
    angle = np.pi / side * np.outer(np.arange(n.turns), np.arange(LANES) // side)
    twiddle = np.concatenate([cas(angle), cas(-angle)]).astype(np.float32)

    def squares(length):
        m = np.arange(length)
        return (2.0 * np.pi / length * np.where(m < length // 2, m, m - length)) ** 2

    z = squares(n.waves).reshape(n.waves, 1, 1, 1)
    y = squares(2 * side).reshape(per, n.turns).T.reshape(1, n.turns, per, 1)
    x = squares(2 * side).reshape(1, 1, 1, 2 * side)
    green = 4.0 * np.pi / (z + y + x + SCREEN) / (n.waves * 4.0 * side * side)
    green = green.reshape(n.waves, n.turns * n.wide).astype(np.float32)
    spread = np.zeros((LANES, n.halves * LANES), ml_dtypes.bfloat16)
    for cell in range(LANES):
        spread[cell, cell // side * n.grid + cell % side] = 1
    gather = np.ascontiguousarray(spread.T)
    return to_waves, from_waves, lane, lane_back, twiddle, green, spread, gather


def far_first(n, me):
    near = n.owners >> ((n.owners.bit_length() - 1) // 2)
    near = n.owners // near
    far = n.owners // near
    z, y = me // near, lax.rem(me, near)
    low = (z < far // 2).astype(jnp.int32)
    here = low * (far - 1 - z) + (1 - low) * z
    peers = []
    for k in range(far - 1):
        place = k + (k >= here).astype(jnp.int32)
        level = low * (far - 1 - place) + (1 - low) * place
        peers += [level * near + lax.rem(y + 1 + step, near) for step in range(near)]
    return peers + [z * near + lax.rem(y + step, near) for step in range(1, near + 1)]


def split(value):
    high = value.astype(BF16)
    return high, (value - high.astype(F32)).astype(BF16)


def dot(left, right):
    return jnp.dot(left, right, preferred_element_type=F32)


def thrice(high, low, matrix):
    return dot(high, matrix[0]) + dot(low, matrix[0]) + dot(high, matrix[1])


def flat_roll(value, amount):
    carried = lax.rem(amount, LANES)
    down = amount // LANES
    rows = value.shape[1]
    turned = pltpu.roll(value, carried, axis=2)
    here = pltpu.roll(turned, down, axis=1)
    above = pltpu.roll(turned, lax.rem(down + 1, rows), axis=1)
    lane = lax.broadcasted_iota(jnp.int32, value.shape, 2)
    return jnp.where(lane >= carried, here, above)


def slide(n, value, shift_y, shift_x):
    shape = value.shape
    value = value.reshape(shape[0] // n.rows, n.rows, LANES)
    row = lax.broadcasted_iota(jnp.int32, value.shape, 1)
    lane = lax.broadcasted_iota(jnp.int32, value.shape, 2)
    y = row * n.per + lane // n.side - shift_y
    x = lax.rem(lane, n.side) - shift_x
    inside = (y >= 0) & (y < n.side) & (x >= 0) & (x < n.side)
    amount = lax.rem(shift_y * n.side + shift_x + 2 * n.cells, n.cells)
    return jnp.where(inside, flat_roll(value, amount), 0.0).reshape(shape)


def wave_sums(n, values):
    top, half = n.turns // 2, n.turns // 4
    cosines, sines = [None] * (top + 1), [None] * (top + 1)
    for q in range(half + 1):
        sums = []
        for wave in (math.cos, math.sin):
            for parity in (0, 1):
                total = None
                for s in range(parity, n.rows, 2):
                    factor = wave(2.0 * math.pi * q * s / n.turns)
                    total = weighted(total, factor, values[s])
                sums.append(total)
        even_cos, odd_cos, even_sin, odd_sin = sums
        cosines[q] = plus(even_cos, odd_cos)
        cosines[top - q] = minus(even_cos, odd_cos)
        sines[q] = plus(even_sin, odd_sin)
        sines[top - q] = minus(odd_sin, even_sin)
    return cosines, sines


def weighted(total, factor, value):
    if value is None or abs(factor) < 1e-12:
        return total
    if abs(abs(factor) - 1.0) < 1e-12:
        if factor > 0:
            return value if total is None else total + value
        return -value if total is None else total - value
    term = factor * value
    return term if total is None else total + term


def plus(left, right):
    if left is None or right is None:
        return right if left is None else left
    return left + right


def minus(left, right):
    if right is None:
        return left
    return -right if left is None else left - right


def cell_sums(n, cosines, sines):
    top, half = n.turns // 2, n.turns // 4
    values = []
    folded = {}
    for q in range(half + 1):
        if q == top - q:
            folded[q] = (cosines[q], cosines[q], sines[q], sines[q])
        else:
            c, d, s, t = cosines[q], cosines[top - q], sines[q], sines[top - q]
            folded[q] = (plus(c, d), minus(c, d), minus(s, t), plus(s, t))
    for s in range(n.rows):
        total = None
        odd = s % 2
        for q in range(half + 1):
            angle = 2.0 * math.pi * q * s / n.turns
            total = weighted(total, math.cos(angle), folded[q][odd])
            total = weighted(total, math.sin(angle), folded[q][2 + odd])
        values.append(total)
    return values


def forward_band(n, rho, band, planes, lane, twiddle):
    start = pl.multiple_of(band * (TILE * n.rows), TILE * n.rows)
    values = [rho[pl.ds(start + s, TILE, stride=n.rows), :] for s in range(n.rows)]
    cosines, sines = wave_sums(n, values)
    top = n.turns // 2
    first, second = [], []
    for q in range(n.turns):
        same = q <= top
        a = cosines[q if same else n.turns - q]
        b = sines[q if same else n.turns - q]
        ahead = twiddle[q : q + 1, :]
        behind = twiddle[n.turns + q : n.turns + q + 1, :]
        u, w = ahead * a, behind * a
        if q % top:
            u = u + behind * b if same else u - behind * b
            w = w - ahead * b if same else w + ahead * b
        first.append(u)
        second.append(w)
    value = jnp.concatenate([jnp.concatenate(first, axis=0), jnp.concatenate(second, axis=0)], axis=1)
    high, low = split(value)
    value = thrice(high, low, lane)
    rows = pl.ds(pl.multiple_of(band * TILE, TILE), TILE)
    for q in range(n.turns):
        planes[rows, q * n.wide : (q + 1) * n.wide] = value[q * TILE : (q + 1) * TILE, :]


def stacked(value):
    high, low = split(value)
    return jnp.concatenate([high, low, high], axis=0)


def along_z(planes, to_waves, from_waves, green):
    value = dot(to_waves[...], stacked(planes[...])) * green[...]
    planes[...] = dot(from_waves[...], stacked(value))


def back_band(n, planes, band, field, lane_back, twiddle):
    rows = pl.ds(pl.multiple_of(band * TILE, TILE), TILE)
    value = jnp.concatenate([planes[rows, q * n.wide : (q + 1) * n.wide] for q in range(n.turns)], axis=0)
    high, low = split(value)
    value = thrice(high, low, lane_back)
    top = n.turns // 2
    cosines, sines = [None] * (top + 1), [None] * (top + 1)
    for q in range(n.turns):
        part = slice(q * TILE, (q + 1) * TILE)
        u, w = value[part, 0:LANES], value[part, LANES : 2 * LANES]
        ahead = twiddle[q : q + 1, :]
        behind = twiddle[n.turns + q : n.turns + q + 1, :]
        a = ahead * u + behind * w
        b = behind * u - ahead * w
        if q <= top:
            cosines[q] = a
            sines[q] = b if q % top else None
        else:
            cosines[n.turns - q] = cosines[n.turns - q] + a
            sines[n.turns - q] = sines[n.turns - q] - b
    start = pl.multiple_of(band * (TILE * n.rows), TILE * n.rows)
    for s, part in enumerate(cell_sums(n, cosines, sines)):
        field[pl.ds(start + s, TILE, stride=n.rows), :] = part


def kernel(n, listed, placed, orbital, external, *refs):
    table_refs, refs = refs[:8], refs[8:]
    out, refs = refs[0], refs[1:]
    table_dst, refs = refs[:8], refs[8:]
    (own_box, flat, box_send, box_land, place_send, place_land, corner, near, moved, rho_send, rho_land) = refs[:11]
    (field_send, field_land, ext_block, ext_flat, dens_grid, dens_send, dens_land, level, read_in, read) = refs[11:21]
    (grad_send, planes, pairs, listed_in, placed_in) = refs[21:26]
    local_sem, own_send, own_recv, grp_send, grp_recv = refs[26:]
    to_waves, from_waves, lane, lane_back, twiddle, green, spread, gather = table_dst
    owners, groups, depth, slab = n.owners, n.groups, n.depth, n.slab
    me, team = lax.axis_index("own"), lax.axis_index("grp")
    partner = team + 1 - 2 * lax.rem(team, 2)
    barrier = pltpu.get_barrier_semaphore()
    peers = far_first(n, me)
    for peer in peers:
        there = {"own": peer, "grp": partner}
        pl.semaphore_signal(barrier, inc=1, device_id=there, device_id_type=MESH)
    base = team - lax.rem(team, 2)
    distant = [lax.rem(base + step, groups) for step in range(2, groups)]
    others = [*distant, partner]
    for peer in distant:
        pl.semaphore_signal(barrier, inc=1, device_id={"grp": peer}, device_id_type=MESH)

    small_in = [
        pltpu.make_async_copy(placed, placed_in, local_sem.at[2 + len(table_refs)]),
        pltpu.make_async_copy(listed, listed_in, local_sem.at[3 + len(table_refs)]),
    ]
    for item in small_in:
        item.start()
    own_in = pltpu.make_async_copy(orbital, own_box, local_sem.at[0])
    own_in.start()
    first_level = pl.multiple_of(me * depth // TILE * TILE, TILE)
    taken = ext_block.shape[0]
    ext_in = pltpu.make_async_copy(external.at[pl.ds(first_level, taken)], ext_block, local_sem.at[1])
    ext_in.start()
    table_in = [
        pltpu.make_async_copy(source, target, local_sem.at[2 + i])
        for i, (source, target) in enumerate(zip(table_refs, table_dst))
    ]
    for item in table_in:
        item.start()
    row_index = lax.broadcasted_iota(jnp.int32, place_send.shape, 0)
    for item in small_in:
        item.wait()
    pair_index = lax.broadcasted_iota(jnp.int32, listed_in.shape, 1)
    header = jnp.where(row_index == 0, placed_in[0:1, 0:1], placed_in[0:1, 1:2])
    for turn in range(n.each):
        mine = jnp.sum(jnp.where(pair_index == me * n.each + turn, listed_in[...], 0), axis=1, keepdims=True)
        header = jnp.where(row_index == 2 + 2 * turn, mine[0:1], header)
        header = jnp.where(row_index == 3 + 2 * turn, mine[1:2], header)
    place_send[...] = header
    own_in.wait()
    for s in range(n.rows):
        flat[pl.ds(s, n.levels, stride=n.rows), :] = own_box[:, s * LANES : (s + 1) * LANES].astype(F32)
    for owner in range(owners):
        box_send[owner] = flat[owner * slab : (owner + 1) * slab, :].astype(BF16)
    pl.semaphore_wait(barrier, owners + groups - 2)

    def to_owner(phase, peer, source, target):
        return pltpu.make_async_remote_copy(
            src_ref=source,
            dst_ref=target,
            send_sem=own_send.at[phase, peer],
            recv_sem=own_recv.at[phase, me],
            device_id={"own": peer, "grp": partner},
            device_id_type=MESH,
        )

    def arrive(phase, peer, source, target):
        pltpu.make_async_remote_copy(
            src_ref=source,
            dst_ref=target,
            send_sem=own_send.at[phase, peer],
            recv_sem=own_recv.at[phase, peer],
            device_id={"own": peer, "grp": partner},
            device_id_type=MESH,
        ).wait_recv()

    def arrived(phase, source, target):
        for peer in reversed(peers):
            arrive(phase, peer, source, target(peer))

    def rows_of(index):
        return pl.ds(pl.multiple_of(index * slab, slab), slab)

    sent = []
    boxes_in = []
    for peer in peers:
        boxes_in.append(to_owner(0, peer, place_send, place_land.at[me]))
        boxes_in.append(to_owner(1, peer, box_send.at[peer], box_land.at[me]))
        boxes_in[-2].start()
        boxes_in[-1].start()
    sent += boxes_in
    arrived(0, place_send, lambda peer: place_land.at[peer])
    arrived(1, box_send.at[0], lambda peer: box_land.at[peer])
    for owner in range(owners):
        corner[owner, 0] = place_land[owner, 0, 0]
        corner[owner, 1] = place_land[owner, 1, 0]
        for turn in range(n.each):
            pairs[owner * n.each + turn, 0] = place_land[owner, 2 + 2 * turn, 0]
            pairs[owner * n.each + turn, 1] = place_land[owner, 3 + 2 * turn, 0]

    def shift_of(row):
        first, second = pairs[row, 0], pairs[row, 1]
        return corner[second, 0] - corner[first, 0], corner[second, 1] - corner[first, 1]

    rho_in = []
    for peer in peers:
        for turn in range(n.each):
            row = peer * n.each + turn
            dy, dx = shift_of(row)
            a = box_land[pairs[row, 0]].astype(F32)
            b = slide(n, box_land[pairs[row, 1]].astype(F32), dy, dx)
            near[row] = a
            moved[row] = b
            rho_send[peer, turn] = a * b
            rho_in.append(to_owner(2 + turn, peer, rho_send.at[peer, turn], rho_land.at[turn, rows_of(me)]))
            rho_in[-1].start()
    sent += rho_in

    for item in table_in:
        item.wait()
    grid_shape = (depth, n.grid_rows, LANES)
    for owner in range(owners):
        value = box_land[owner].astype(F32)
        high, low = split(value * value)
        wide = dot(high, spread[...]) + dot(low, spread[...])
        for z in range(depth):
            start = z * n.grid_rows
            for half in range(n.halves):
                rows = pl.ds(start + half, n.rows, stride=n.halves)
                dens_grid[owner, rows, :] = wide[z * n.rows : (z + 1) * n.rows, half * LANES : (half + 1) * LANES]
            rest = n.grid_rows - n.rows * n.halves
            dens_grid[owner, start + n.rows * n.halves : start + n.grid_rows, :] = jnp.zeros((rest, LANES), F32)
    total = jnp.zeros(grid_shape, F32)
    for owner in range(owners):
        amount = corner[owner, 0] * n.grid + corner[owner, 1]
        total = total + flat_roll(dens_grid[owner].reshape(grid_shape), amount)
    dens_send[...] = total.reshape(dens_send.shape)
    dens_land[team] = dens_send[...]

    def dens_copy(peer, sender):
        return pltpu.make_async_remote_copy(
            src_ref=dens_send,
            dst_ref=dens_land.at[sender],
            send_sem=grp_send.at[peer],
            recv_sem=grp_recv.at[sender],
            device_id={"grp": peer},
            device_id_type=MESH,
        )

    for peer in others:
        dens_copy(peer, team).start()

    low = (me < owners // 2).astype(jnp.int32)
    far_bands = [low * (n.bands - 1 - k) + (1 - low) * k for k in range(n.bands)]
    field_in = []
    for turn in range(n.each):
        for band in reversed(far_bands):
            for index in range(n.share):
                peer = band * n.share + index
                arrive(2 + turn, peer, rho_send.at[0, turn], rho_land.at[turn, rows_of(peer)])
            forward_band(n, rho_land.at[turn], band, planes, lane, twiddle)
        along_z(planes, to_waves, from_waves, green)
        for band in far_bands:
            back_band(n, planes, band, field_send.at[turn], lane_back, twiddle)
            for index in range(n.share):
                peer = band * n.share + index
                source = field_send.at[turn, rows_of(peer)]
                field_in.append(to_owner(2 + n.each + turn, peer, source, field_land.at[me * n.each + turn]))
                field_in[-1].start()
    sent += field_in

    ext_in.wait()
    ext_values = ext_block[...].astype(F32)
    for k in range(n.grid_rows):
        ext_flat[pl.ds(k, taken, stride=n.grid_rows), :] = ext_values[:, k * LANES : (k + 1) * LANES]
    for peer in others:
        dens_copy(peer, peer).wait_recv()
    density = dens_land[0]
    for index in range(1, groups):
        density = density + dens_land[index]
    start = pl.multiple_of((me * depth - first_level) * n.grid_rows, n.grid_rows)
    outside = ext_flat[pl.ds(start, depth * n.grid_rows), :]
    safe = jnp.where(density > 0.0, density, 1.0)
    root = jnp.exp(jnp.log(safe) * (1.0 / 3.0))
    root = root - (root - safe / (root * root)) * (1.0 / 3.0)
    level[...] = outside - EXCHANGE_COEF * jnp.where(density > 0.0, root, 0.0)
    whole = n.grid_rows * LANES
    for owner in range(owners):
        amount = lax.rem(whole - corner[owner, 0] * n.grid - corner[owner, 1], whole)
        turned = flat_roll(level[...].reshape(grid_shape), amount)
        read_in[owner] = turned.reshape(read_in.shape[1:])
        parts = []
        for z in range(depth):
            pieces = [
                read_in[owner, pl.ds(z * n.grid_rows + half, n.rows, stride=n.halves), :] for half in range(n.halves)
            ]
            parts.append(jnp.concatenate(pieces, axis=1) if n.halves > 1 else pieces[0])
        value = jnp.concatenate(parts, axis=0) if depth > 1 else parts[0]
        high, low = split(value)
        read[owner] = (dot(high, gather[...]) + dot(low, gather[...])) * box_land[owner].astype(F32)

    for turn in range(n.each):
        arrived(2 + n.each + turn, field_send.at[turn, 0:slab], lambda peer: field_land.at[peer * n.each + turn])
    for row in range(n.pairs):
        dy, dx = shift_of(row)
        field = field_land[row] * MIXING
        moved[row] = field * moved[row]
        near[row] = slide(n, field * near[row], -dy, -dx)
    for peer in peers:
        total = read[peer]
        for row in range(n.pairs):
            total = total - jnp.where(pairs[row, 0] == peer, moved[row], 0.0)
            total = total - jnp.where(pairs[row, 1] == peer, near[row], 0.0)
        grad_send[peer] = total
        sent.append(to_owner(2 + 2 * n.each, peer, grad_send.at[peer], out.at[rows_of(me)]))
        sent[-1].start()
    arrived(2 + 2 * n.each, grad_send.at[0], lambda peer: out.at[rows_of(peer)])
    for item in sent:
        item.wait_send()
    for peer in others:
        dens_copy(peer, team).wait_send()


def body(owners, groups, orbitals, offsets, pairs, ext_pot):
    _, levels, cells = orbitals.shape
    n = Sizes(owners, groups, levels, cells, ext_pot.shape[1], pairs.shape[0])
    consts = tables(n)
    taken = max(n.depth, TILE)
    header = -(-(2 + 2 * n.each) // TILE) * TILE
    slabs = (n.owners, n.slab, LANES)
    flat_rows = levels * n.rows
    scratch = [VMEM(c.shape, c.dtype) for c in consts]
    scratch += [
        VMEM((levels, cells), BF16),
        VMEM((flat_rows, LANES), F32),
        VMEM(slabs, BF16),
        VMEM(slabs, BF16),
        VMEM((header, LANES), jnp.int32),
        VMEM((owners, header, LANES), jnp.int32),
        pltpu.SMEM((owners, 2), jnp.int32),
        VMEM((n.pairs, n.slab, LANES), F32),
        VMEM((n.pairs, n.slab, LANES), F32),
        VMEM((owners, n.each, n.slab, LANES), F32),
        VMEM((n.each, flat_rows, LANES), F32),
        VMEM((n.each, flat_rows, LANES), F32),
        VMEM((n.pairs, n.slab, LANES), F32),
        VMEM((taken, ext_pot.shape[1]), BF16),
        VMEM((taken * n.grid_rows, LANES), F32),
        VMEM((owners, n.depth * n.grid_rows, LANES), F32),
        VMEM((n.depth * n.grid_rows, LANES), F32),
        VMEM((groups, n.depth * n.grid_rows, LANES), F32),
        VMEM((n.depth * n.grid_rows, LANES), F32),
        VMEM((owners, n.depth * n.grid_rows, LANES), F32),
        VMEM(slabs, F32),
        VMEM(slabs, F32),
        VMEM((levels, n.turns * n.wide), F32),
        pltpu.SMEM(pairs.shape, jnp.int32),
        VMEM(pairs.shape[::-1], jnp.int32),
        VMEM(offsets.shape, jnp.int32),
        pltpu.SemaphoreType.DMA((4 + len(consts),)),
        pltpu.SemaphoreType.DMA((3 + 2 * n.each, owners)),
        pltpu.SemaphoreType.DMA((3 + 2 * n.each, owners)),
        pltpu.SemaphoreType.DMA((groups,)),
        pltpu.SemaphoreType.DMA((groups,)),
    ]
    anywhere = pl.BlockSpec(memory_space=pl.ANY)
    slab_out = pl.pallas_call(
        functools.partial(kernel, n),
        out_shape=VMEM((flat_rows, LANES), F32),
        in_specs=[anywhere] * (4 + len(consts)),
        out_specs=pl.BlockSpec(memory_space=VMEM),
        scratch_shapes=scratch,
        compiler_params=pltpu.CompilerParams(collective_id=0, has_side_effects=True),
        name="gradient",
    )(pairs.T, offsets, orbitals[0], ext_pot, *consts)
    return slab_out.reshape(1, levels, cells)


def solution(mesh):
    in_specs = (P(("grp", "own"), None, None), P(("grp", "own"), None), P("grp", None), P())
    out_specs = P(("grp", "own"), None, None)
    run = functools.partial(body, mesh.shape["own"], mesh.shape["grp"])
    return jax.shard_map(run, mesh=mesh, in_specs=in_specs, out_specs=out_specs, check_vma=False)
```

```python
import functools
import math

import jax
import jax.numpy as jnp
import ml_dtypes
import numpy as np
from jax import lax
from jax.experimental import pallas as pl
from jax.experimental.pallas import tpu as pltpu
from jax.sharding import PartitionSpec as P

SCREEN = 0.0025
MIXING = 0.25
EXCHANGE_COEF = (3.0 / math.pi) ** (1.0 / 3.0)
LANES = 128
TILE = 8
VMEM = pltpu.VMEM
MESH = pl.DeviceIdType.MESH
F32 = jnp.float32
BF16 = jnp.bfloat16


class Sizes:
    def __init__(self, owners, groups, levels, cells, grid_cells, pairs):
        self.owners, self.groups, self.levels, self.cells, self.pairs = owners, groups, levels, cells, pairs
        self.side, self.grid = math.isqrt(cells), math.isqrt(grid_cells)
        self.depth = levels // owners
        self.each = pairs // owners
        self.rows = cells // LANES
        self.per = LANES // self.side
        self.slab = self.depth * self.rows
        self.grid_rows = grid_cells // LANES
        self.halves = self.per * self.grid // LANES
        self.waves = 2 * levels
        self.turns = 2 * self.side // self.per
        self.wide = self.per * 2 * self.side
        self.bands = levels // TILE
        self.share = TILE // self.depth


def halves_of(table):
    high = table.astype(ml_dtypes.bfloat16)
    low = (table - high.astype(np.float64)).astype(ml_dtypes.bfloat16)
    return high, low


def cas(angle):
    return np.cos(angle) + np.sin(angle)


def tables(n):
    side, per, levels = n.side, n.per, n.levels
    along_z = cas(2.0 * np.pi / n.waves * np.outer(np.arange(n.waves), np.arange(levels)))
    high, low = halves_of(along_z)
    to_waves = np.concatenate([high, high, low], axis=1)
    high, low = halves_of(along_z.T)
    from_waves = np.concatenate([high, high, low], axis=1)
    along_x = cas(np.pi / side * np.outer(np.arange(side), np.arange(2 * side)))
    phase = 2.0 * np.pi / per * np.outer(np.arange(per), np.arange(per))
    lane = np.concatenate(
        [np.einsum("yh,xk->yxhk", wave(phase), along_x).reshape(LANES, n.wide) for wave in (np.cos, np.sin)]
    )
    lane = np.stack(halves_of(lane))
    lane_back = np.ascontiguousarray(np.swapaxes(lane, 1, 2))
    angle = np.pi / side * np.outer(np.arange(n.turns), np.arange(LANES) // side)
    twiddle = np.concatenate([cas(angle), cas(-angle)]).astype(np.float32)

    def squares(length):
        m = np.arange(length)
        return (2.0 * np.pi / length * np.where(m < length // 2, m, m - length)) ** 2

    z = squares(n.waves).reshape(n.waves, 1, 1, 1)
    y = squares(2 * side).reshape(per, n.turns).T.reshape(1, n.turns, per, 1)
    x = squares(2 * side).reshape(1, 1, 1, 2 * side)
    green = 4.0 * np.pi / (z + y + x + SCREEN) / (n.waves * 4.0 * side * side)
    green = green.reshape(n.waves, n.turns * n.wide).astype(np.float32)
    spread = np.zeros((LANES, n.halves * LANES), ml_dtypes.bfloat16)
    for cell in range(LANES):
        spread[cell, cell // side * n.grid + cell % side] = 1
    gather = np.ascontiguousarray(spread.T)
    return to_waves, from_waves, lane, lane_back, twiddle, green, spread, gather


def far_first(n, me):
    near = n.owners >> ((n.owners.bit_length() - 1) // 2)
    near = n.owners // near
    far = n.owners // near
    z, y = me // near, lax.rem(me, near)
    low = (z < far // 2).astype(jnp.int32)
    here = low * (far - 1 - z) + (1 - low) * z
    peers = []
    for k in range(far - 1):
        place = k + (k >= here).astype(jnp.int32)
        level = low * (far - 1 - place) + (1 - low) * place
        peers += [level * near + lax.rem(y + 1 + step, near) for step in range(near)]
    return peers + [z * near + lax.rem(y + step, near) for step in range(1, near + 1)]


def split(value):
    high = value.astype(BF16)
    return high, (value - high.astype(F32)).astype(BF16)


def dot(left, right):
    return jnp.dot(left, right, preferred_element_type=F32)


def thrice(high, low, matrix):
    return dot(high, matrix[0]) + dot(low, matrix[0]) + dot(high, matrix[1])


def flat_roll(value, amount):
    carried = lax.rem(amount, LANES)
    down = amount // LANES
    rows = value.shape[1]
    turned = pltpu.roll(value, carried, axis=2)
    here = pltpu.roll(turned, down, axis=1)
    above = pltpu.roll(turned, lax.rem(down + 1, rows), axis=1)
    lane = lax.broadcasted_iota(jnp.int32, value.shape, 2)
    return jnp.where(lane >= carried, here, above)


def slide(n, value, shift_y, shift_x):
    shape = value.shape
    value = value.reshape(shape[0] // n.rows, n.rows, LANES)
    row = lax.broadcasted_iota(jnp.int32, value.shape, 1)
    lane = lax.broadcasted_iota(jnp.int32, value.shape, 2)
    y = row * n.per + lane // n.side - shift_y
    x = lax.rem(lane, n.side) - shift_x
    inside = (y >= 0) & (y < n.side) & (x >= 0) & (x < n.side)
    amount = lax.rem(shift_y * n.side + shift_x + 2 * n.cells, n.cells)
    return jnp.where(inside, flat_roll(value, amount), 0.0).reshape(shape)


def wave_sums(n, values):
    top, half = n.turns // 2, n.turns // 4
    cosines, sines = [None] * (top + 1), [None] * (top + 1)
    for q in range(half + 1):
        sums = []
        for wave in (math.cos, math.sin):
            for parity in (0, 1):
                total = None
                for s in range(parity, n.rows, 2):
                    factor = wave(2.0 * math.pi * q * s / n.turns)
                    total = weighted(total, factor, values[s])
                sums.append(total)
        even_cos, odd_cos, even_sin, odd_sin = sums
        cosines[q] = plus(even_cos, odd_cos)
        cosines[top - q] = minus(even_cos, odd_cos)
        sines[q] = plus(even_sin, odd_sin)
        sines[top - q] = minus(odd_sin, even_sin)
    return cosines, sines


def weighted(total, factor, value):
    if value is None or abs(factor) < 1e-12:
        return total
    if abs(abs(factor) - 1.0) < 1e-12:
        if factor > 0:
            return value if total is None else total + value
        return -value if total is None else total - value
    term = factor * value
    return term if total is None else total + term


def plus(left, right):
    if left is None or right is None:
        return right if left is None else left
    return left + right


def minus(left, right):
    if right is None:
        return left
    return -right if left is None else left - right


def cell_sums(n, cosines, sines):
    top, half = n.turns // 2, n.turns // 4
    values = []
    folded = {}
    for q in range(half + 1):
        if q == top - q:
            folded[q] = (cosines[q], cosines[q], sines[q], sines[q])
        else:
            c, d, s, t = cosines[q], cosines[top - q], sines[q], sines[top - q]
            folded[q] = (plus(c, d), minus(c, d), minus(s, t), plus(s, t))
    for s in range(n.rows):
        total = None
        odd = s % 2
        for q in range(half + 1):
            angle = 2.0 * math.pi * q * s / n.turns
            total = weighted(total, math.cos(angle), folded[q][odd])
            total = weighted(total, math.sin(angle), folded[q][2 + odd])
        values.append(total)
    return values


def forward_band(n, rho, band, planes, lane, twiddle):
    start = pl.multiple_of(band * (TILE * n.rows), TILE * n.rows)
    values = [rho[pl.ds(start + s, TILE, stride=n.rows), :] for s in range(n.rows)]
    cosines, sines = wave_sums(n, values)
    top = n.turns // 2
    first, second = [], []
    for q in range(n.turns):
        same = q <= top
        a = cosines[q if same else n.turns - q]
        b = sines[q if same else n.turns - q]
        ahead = twiddle[q : q + 1, :]
        behind = twiddle[n.turns + q : n.turns + q + 1, :]
        u, w = ahead * a, behind * a
        if q % top:
            u = u + behind * b if same else u - behind * b
            w = w - ahead * b if same else w + ahead * b
        first.append(u)
        second.append(w)
    value = jnp.concatenate([jnp.concatenate(first, axis=0), jnp.concatenate(second, axis=0)], axis=1)
    high, low = split(value)
    value = thrice(high, low, lane)
    rows = pl.ds(pl.multiple_of(band * TILE, TILE), TILE)
    for q in range(n.turns):
        planes[rows, q * n.wide : (q + 1) * n.wide] = value[q * TILE : (q + 1) * TILE, :]


def stacked(value):
    high, low = split(value)
    return jnp.concatenate([high, low, high], axis=0)


def along_z(planes, to_waves, from_waves, green):
    value = dot(to_waves[...], stacked(planes[...])) * green[...]
    planes[...] = dot(from_waves[...], stacked(value))


def back_band(n, planes, band, field, lane_back, twiddle):
    rows = pl.ds(pl.multiple_of(band * TILE, TILE), TILE)
    value = jnp.concatenate([planes[rows, q * n.wide : (q + 1) * n.wide] for q in range(n.turns)], axis=0)
    high, low = split(value)
    value = thrice(high, low, lane_back)
    top = n.turns // 2
    cosines, sines = [None] * (top + 1), [None] * (top + 1)
    for q in range(n.turns):
        part = slice(q * TILE, (q + 1) * TILE)
        u, w = value[part, 0:LANES], value[part, LANES : 2 * LANES]
        ahead = twiddle[q : q + 1, :]
        behind = twiddle[n.turns + q : n.turns + q + 1, :]
        a = ahead * u + behind * w
        b = behind * u - ahead * w
        if q <= top:
            cosines[q] = a
            sines[q] = b if q % top else None
        else:
            cosines[n.turns - q] = cosines[n.turns - q] + a
            sines[n.turns - q] = sines[n.turns - q] - b
    start = pl.multiple_of(band * (TILE * n.rows), TILE * n.rows)
    for s, part in enumerate(cell_sums(n, cosines, sines)):
        field[pl.ds(start + s, TILE, stride=n.rows), :] = part


def kernel(n, listed, placed, orbital, external, *refs):
    table_refs, refs = refs[:8], refs[8:]
    out, refs = refs[0], refs[1:]
    table_dst, refs = refs[:8], refs[8:]
    (own_box, flat, box_send, box_land, place_send, place_land, corner, near, moved, rho_send, rho_land) = refs[:11]
    (field_send, field_land, ext_block, ext_flat, dens_grid, dens_send, dens_land, level, read_in, read) = refs[11:21]
    (grad_send, planes, pairs, listed_in, placed_in) = refs[21:26]
    local_sem, own_send, own_recv, grp_send, grp_recv = refs[26:]
    to_waves, from_waves, lane, lane_back, twiddle, green, spread, gather = table_dst
    owners, groups, depth, slab = n.owners, n.groups, n.depth, n.slab
    me, team = lax.axis_index("own"), lax.axis_index("grp")
    partner = team + 1 - 2 * lax.rem(team, 2)
    barrier = pltpu.get_barrier_semaphore()
    peers = far_first(n, me)
    for peer in peers:
        there = {"own": peer, "grp": partner}
        pl.semaphore_signal(barrier, inc=1, device_id=there, device_id_type=MESH)
    base = team - lax.rem(team, 2)
    distant = [lax.rem(base + step, groups) for step in range(2, groups)]
    others = [*distant, partner]
    for peer in distant:
        pl.semaphore_signal(barrier, inc=1, device_id={"grp": peer}, device_id_type=MESH)

    small_in = [
        pltpu.make_async_copy(placed, placed_in, local_sem.at[2 + len(table_refs)]),
        pltpu.make_async_copy(listed, listed_in, local_sem.at[3 + len(table_refs)]),
    ]
    for item in small_in:
        item.start()
    own_in = pltpu.make_async_copy(orbital, own_box, local_sem.at[0])
    own_in.start()
    first_level = pl.multiple_of(me * depth // TILE * TILE, TILE)
    taken = ext_block.shape[0]
    ext_in = pltpu.make_async_copy(external.at[pl.ds(first_level, taken)], ext_block, local_sem.at[1])
    ext_in.start()
    table_in = [
        pltpu.make_async_copy(source, target, local_sem.at[2 + i])
        for i, (source, target) in enumerate(zip(table_refs, table_dst))
    ]
    for item in table_in:
        item.start()
    place_index = lax.broadcasted_iota(jnp.int32, place_send.shape, 1)
    for item in small_in:
        item.wait()
    pair_index = lax.broadcasted_iota(jnp.int32, listed_in.shape, 1)
    header = jnp.where(place_index == 0, placed_in[0:1, 0:1], placed_in[0:1, 1:2])
    for turn in range(n.each):
        mine = jnp.sum(jnp.where(pair_index == me * n.each + turn, listed_in[...], 0), axis=1, keepdims=True)
        header = jnp.where(place_index == 2 + 2 * turn, mine[0:1], header)
        header = jnp.where(place_index == 3 + 2 * turn, mine[1:2], header)
    place_send[...] = header
    own_in.wait()
    for s in range(n.rows):
        flat[pl.ds(s, n.levels, stride=n.rows), :] = own_box[:, s * LANES : (s + 1) * LANES].astype(F32)
    for owner in range(owners):
        box_send[owner] = flat[owner * slab : (owner + 1) * slab, :].astype(BF16)
    pl.semaphore_wait(barrier, owners + groups - 2)

    def to_owner(phase, peer, source, target):
        return pltpu.make_async_remote_copy(
            src_ref=source,
            dst_ref=target,
            send_sem=own_send.at[phase, peer],
            recv_sem=own_recv.at[phase, me],
            device_id={"own": peer, "grp": partner},
            device_id_type=MESH,
        )

    def arrive(phase, peer, source, target):
        pltpu.make_async_remote_copy(
            src_ref=source,
            dst_ref=target,
            send_sem=own_send.at[phase, peer],
            recv_sem=own_recv.at[phase, peer],
            device_id={"own": peer, "grp": partner},
            device_id_type=MESH,
        ).wait_recv()

    def arrived(phase, source, target):
        for peer in reversed(peers):
            arrive(phase, peer, source, target(peer))

    def rows_of(index):
        return pl.ds(pl.multiple_of(index * slab, slab), slab)

    sent = []
    boxes_in = []
    for peer in peers:
        boxes_in.append(to_owner(0, peer, place_send, place_land.at[me]))
        boxes_in.append(to_owner(1, peer, box_send.at[peer], box_land.at[me]))
        boxes_in[-2].start()
        boxes_in[-1].start()
    sent += boxes_in
    arrived(0, place_send, lambda peer: place_land.at[peer])
    arrived(1, box_send.at[0], lambda peer: box_land.at[peer])
    for owner in range(owners):
        corner[owner, 0] = place_land[owner, 0, 0]
        corner[owner, 1] = place_land[owner, 0, 1]
        for turn in range(n.each):
            pairs[owner * n.each + turn, 0] = place_land[owner, 0, 2 + 2 * turn]
            pairs[owner * n.each + turn, 1] = place_land[owner, 0, 3 + 2 * turn]

    def shift_of(row):
        first, second = pairs[row, 0], pairs[row, 1]
        return corner[second, 0] - corner[first, 0], corner[second, 1] - corner[first, 1]

    rho_in = []
    for peer in peers:
        for turn in range(n.each):
            row = peer * n.each + turn
            dy, dx = shift_of(row)
            a = box_land[pairs[row, 0]].astype(F32)
            b = slide(n, box_land[pairs[row, 1]].astype(F32), dy, dx)
            near[row] = a
            moved[row] = b
            rho_send[peer, turn] = a * b
            rho_in.append(to_owner(2 + turn, peer, rho_send.at[peer, turn], rho_land.at[turn, rows_of(me)]))
            rho_in[-1].start()
    sent += rho_in

    for item in table_in:
        item.wait()
    grid_shape = (depth, n.grid_rows, LANES)
    for owner in range(owners):
        value = box_land[owner].astype(F32)
        high, low = split(value * value)
        wide = dot(high, spread[...]) + dot(low, spread[...])
        for z in range(depth):
            start = z * n.grid_rows
            for half in range(n.halves):
                rows = pl.ds(start + half, n.rows, stride=n.halves)
                dens_grid[owner, rows, :] = wide[z * n.rows : (z + 1) * n.rows, half * LANES : (half + 1) * LANES]
            rest = n.grid_rows - n.rows * n.halves
            dens_grid[owner, start + n.rows * n.halves : start + n.grid_rows, :] = jnp.zeros((rest, LANES), F32)
    total = jnp.zeros(grid_shape, F32)
    for owner in range(owners):
        amount = corner[owner, 0] * n.grid + corner[owner, 1]
        total = total + flat_roll(dens_grid[owner].reshape(grid_shape), amount)
    dens_send[...] = total.reshape(dens_send.shape)
    dens_land[team] = dens_send[...]

    def dens_copy(peer, sender):
        return pltpu.make_async_remote_copy(
            src_ref=dens_send,
            dst_ref=dens_land.at[sender],
            send_sem=grp_send.at[peer],
            recv_sem=grp_recv.at[sender],
            device_id={"grp": peer},
            device_id_type=MESH,
        )

    for peer in others:
        dens_copy(peer, team).start()

    low = (me < owners // 2).astype(jnp.int32)
    far_bands = [low * (n.bands - 1 - k) + (1 - low) * k for k in range(n.bands)]
    field_in = []
    for turn in range(n.each):
        for band in reversed(far_bands):
            for index in range(n.share):
                peer = band * n.share + index
                arrive(2 + turn, peer, rho_send.at[0, turn], rho_land.at[turn, rows_of(peer)])
            forward_band(n, rho_land.at[turn], band, planes, lane, twiddle)
        along_z(planes, to_waves, from_waves, green)
        for band in far_bands:
            back_band(n, planes, band, field_send.at[turn], lane_back, twiddle)
            for index in range(n.share):
                peer = band * n.share + index
                source = field_send.at[turn, rows_of(peer)]
                field_in.append(to_owner(2 + n.each + turn, peer, source, field_land.at[me * n.each + turn]))
                field_in[-1].start()
    sent += field_in

    ext_in.wait()
    ext_values = ext_block[...].astype(F32)
    for k in range(n.grid_rows):
        ext_flat[pl.ds(k, taken, stride=n.grid_rows), :] = ext_values[:, k * LANES : (k + 1) * LANES]
    for peer in others:
        dens_copy(peer, peer).wait_recv()
    density = dens_land[0]
    for index in range(1, groups):
        density = density + dens_land[index]
    start = pl.multiple_of((me * depth - first_level) * n.grid_rows, n.grid_rows)
    outside = ext_flat[pl.ds(start, depth * n.grid_rows), :]
    safe = jnp.where(density > 0.0, density, 1.0)
    root = jnp.exp(jnp.log(safe) * (1.0 / 3.0))
    root = root - (root - safe / (root * root)) * (1.0 / 3.0)
    level[...] = outside - EXCHANGE_COEF * jnp.where(density > 0.0, root, 0.0)
    whole = n.grid_rows * LANES
    for owner in range(owners):
        amount = lax.rem(whole - corner[owner, 0] * n.grid - corner[owner, 1], whole)
        turned = flat_roll(level[...].reshape(grid_shape), amount)
        read_in[owner] = turned.reshape(read_in.shape[1:])
        parts = []
        for z in range(depth):
            pieces = [
                read_in[owner, pl.ds(z * n.grid_rows + half, n.rows, stride=n.halves), :] for half in range(n.halves)
            ]
            parts.append(jnp.concatenate(pieces, axis=1) if n.halves > 1 else pieces[0])
        value = jnp.concatenate(parts, axis=0) if depth > 1 else parts[0]
        high, low = split(value)
        read[owner] = (dot(high, gather[...]) + dot(low, gather[...])) * box_land[owner].astype(F32)

    for turn in range(n.each):
        arrived(2 + n.each + turn, field_send.at[turn, 0:slab], lambda peer: field_land.at[peer * n.each + turn])
    for row in range(n.pairs):
        dy, dx = shift_of(row)
        field = field_land[row] * MIXING
        moved[row] = field * moved[row]
        near[row] = slide(n, field * near[row], -dy, -dx)
    for peer in peers:
        total = read[peer]
        for row in range(n.pairs):
            total = total - jnp.where(pairs[row, 0] == peer, moved[row], 0.0)
            total = total - jnp.where(pairs[row, 1] == peer, near[row], 0.0)
        grad_send[peer] = total
        sent.append(to_owner(2 + 2 * n.each, peer, grad_send.at[peer], out.at[rows_of(me)]))
        sent[-1].start()
    arrived(2 + 2 * n.each, grad_send.at[0], lambda peer: out.at[rows_of(peer)])
    for item in sent:
        item.wait_send()
    for peer in others:
        dens_copy(peer, team).wait_send()


def body(owners, groups, orbitals, offsets, pairs, ext_pot):
    _, levels, cells = orbitals.shape
    n = Sizes(owners, groups, levels, cells, ext_pot.shape[1], pairs.shape[0])
    consts = tables(n)
    taken = max(n.depth, TILE)
    slabs = (n.owners, n.slab, LANES)
    flat_rows = levels * n.rows
    scratch = [VMEM(c.shape, c.dtype) for c in consts]
    scratch += [
        VMEM((levels, cells), BF16),
        VMEM((flat_rows, LANES), F32),
        VMEM(slabs, BF16),
        VMEM(slabs, BF16),
        VMEM((1, LANES), jnp.int32),
        VMEM((owners, 1, LANES), jnp.int32),
        pltpu.SMEM((owners, 2), jnp.int32),
        VMEM((n.pairs, n.slab, LANES), F32),
        VMEM((n.pairs, n.slab, LANES), F32),
        VMEM((owners, n.each, n.slab, LANES), F32),
        VMEM((n.each, flat_rows, LANES), F32),
        VMEM((n.each, flat_rows, LANES), F32),
        VMEM((n.pairs, n.slab, LANES), F32),
        VMEM((taken, ext_pot.shape[1]), BF16),
        VMEM((taken * n.grid_rows, LANES), F32),
        VMEM((owners, n.depth * n.grid_rows, LANES), F32),
        VMEM((n.depth * n.grid_rows, LANES), F32),
        VMEM((groups, n.depth * n.grid_rows, LANES), F32),
        VMEM((n.depth * n.grid_rows, LANES), F32),
        VMEM((owners, n.depth * n.grid_rows, LANES), F32),
        VMEM(slabs, F32),
        VMEM(slabs, F32),
        VMEM((levels, n.turns * n.wide), F32),
        pltpu.SMEM(pairs.shape, jnp.int32),
        VMEM(pairs.shape[::-1], jnp.int32),
        VMEM(offsets.shape, jnp.int32),
        pltpu.SemaphoreType.DMA((4 + len(consts),)),
        pltpu.SemaphoreType.DMA((3 + 2 * n.each, owners)),
        pltpu.SemaphoreType.DMA((3 + 2 * n.each, owners)),
        pltpu.SemaphoreType.DMA((groups,)),
        pltpu.SemaphoreType.DMA((groups,)),
    ]
    anywhere = pl.BlockSpec(memory_space=pl.ANY)
    slab_out = pl.pallas_call(
        functools.partial(kernel, n),
        out_shape=VMEM((flat_rows, LANES), F32),
        in_specs=[anywhere] * (4 + len(consts)),
        out_specs=pl.BlockSpec(memory_space=VMEM),
        scratch_shapes=scratch,
        compiler_params=pltpu.CompilerParams(collective_id=0, has_side_effects=True),
        name="gradient",
    )(pairs.T, offsets, orbitals[0], ext_pot, *consts)
    return slab_out.reshape(1, levels, cells)


def solution(mesh):
    in_specs = (P(("grp", "own"), None, None), P(("grp", "own"), None), P("grp", None), P())
    out_specs = P(("grp", "own"), None, None)
    run = functools.partial(body, mesh.shape["own"], mesh.shape["grp"])
    return jax.shard_map(run, mesh=mesh, in_specs=in_specs, out_specs=out_specs, check_vma=False)
```

```python
import functools
import math

import jax
import jax.numpy as jnp
import ml_dtypes
import numpy as np
from jax import lax
from jax.experimental import pallas as pl
from jax.experimental.pallas import tpu as pltpu
from jax.sharding import PartitionSpec as P

SCREEN = 0.0025
MIXING = 0.25
EXCHANGE_COEF = (3.0 / math.pi) ** (1.0 / 3.0)
LANES = 128
TILE = 8
VMEM = pltpu.VMEM
MESH = pl.DeviceIdType.MESH
F32 = jnp.float32
BF16 = jnp.bfloat16
CODE = jnp.int16
STEPS = 32767.0
TINY = 1e-30


class Sizes:
    def __init__(self, owners, groups, levels, cells, grid_cells, pairs):
        self.owners, self.groups, self.levels, self.cells, self.pairs = owners, groups, levels, cells, pairs
        self.side, self.grid = math.isqrt(cells), math.isqrt(grid_cells)
        self.depth = levels // owners
        self.each = pairs // owners
        self.rows = cells // LANES
        self.per = LANES // self.side
        self.slab = self.depth * self.rows
        self.grid_rows = grid_cells // LANES
        self.halves = self.per * self.grid // LANES
        self.waves = 2 * levels
        self.turns = 2 * self.side // self.per
        self.wide = self.per * 2 * self.side
        self.bands = levels // TILE
        self.share = TILE // self.depth


def halves_of(table):
    high = table.astype(ml_dtypes.bfloat16)
    low = (table - high.astype(np.float64)).astype(ml_dtypes.bfloat16)
    return high, low


def cas(angle):
    return np.cos(angle) + np.sin(angle)


def tables(n):
    side, per, levels = n.side, n.per, n.levels
    along_z = cas(2.0 * np.pi / n.waves * np.outer(np.arange(n.waves), np.arange(levels)))
    high, low = halves_of(along_z)
    to_waves = np.concatenate([high, high, low], axis=1)
    high, low = halves_of(along_z.T)
    from_waves = np.concatenate([high, high, low], axis=1)
    along_x = cas(np.pi / side * np.outer(np.arange(side), np.arange(2 * side)))
    phase = 2.0 * np.pi / per * np.outer(np.arange(per), np.arange(per))
    lane = np.concatenate(
        [np.einsum("yh,xk->yxhk", wave(phase), along_x).reshape(LANES, n.wide) for wave in (np.cos, np.sin)]
    )
    lane = np.stack(halves_of(lane))
    lane_back = np.ascontiguousarray(np.swapaxes(lane, 1, 2))
    angle = np.pi / side * np.outer(np.arange(n.turns), np.arange(LANES) // side)
    twiddle = np.concatenate([cas(angle), cas(-angle)]).astype(np.float32)

    def squares(length):
        m = np.arange(length)
        return (2.0 * np.pi / length * np.where(m < length // 2, m, m - length)) ** 2

    z = squares(n.waves).reshape(n.waves, 1, 1, 1)
    y = squares(2 * side).reshape(per, n.turns).T.reshape(1, n.turns, per, 1)
    x = squares(2 * side).reshape(1, 1, 1, 2 * side)
    green = 4.0 * np.pi / (z + y + x + SCREEN) / (n.waves * 4.0 * side * side)
    green = green.reshape(n.waves, n.turns * n.wide).astype(np.float32)
    spread = np.zeros((LANES, n.halves * LANES), ml_dtypes.bfloat16)
    for cell in range(LANES):
        spread[cell, cell // side * n.grid + cell % side] = 1
    gather = np.ascontiguousarray(spread.T)
    return to_waves, from_waves, lane, lane_back, twiddle, green, spread, gather


def far_first(n, me):
    near = n.owners >> ((n.owners.bit_length() - 1) // 2)
    near = n.owners // near
    far = n.owners // near
    z, y = me // near, lax.rem(me, near)
    low = (z < far // 2).astype(jnp.int32)
    here = low * (far - 1 - z) + (1 - low) * z
    peers = []
    for k in range(far - 1):
        place = k + (k >= here).astype(jnp.int32)
        level = low * (far - 1 - place) + (1 - low) * place
        peers += [level * near + lax.rem(y + 1 + step, near) for step in range(near)]
    return peers + [z * near + lax.rem(y + step, near) for step in range(1, near + 1)]


def split(value):
    high = value.astype(BF16)
    return high, (value - high.astype(F32)).astype(BF16)


def encode(value):
    largest = jnp.max(jnp.abs(value), axis=0, keepdims=True)
    largest = jnp.maximum(largest, TINY)
    code = jnp.round(value * (STEPS / largest)).astype(jnp.int32)
    return code.astype(CODE), largest * (1.0 / STEPS)


def decode(code, step):
    return code.astype(jnp.int32).astype(F32) * step


def dot(left, right):
    return jnp.dot(left, right, preferred_element_type=F32)


def thrice(high, low, matrix):
    return dot(high, matrix[0]) + dot(low, matrix[0]) + dot(high, matrix[1])


def flat_roll(value, amount):
    carried = lax.rem(amount, LANES)
    down = amount // LANES
    rows = value.shape[1]
    turned = pltpu.roll(value, carried, axis=2)
    here = pltpu.roll(turned, down, axis=1)
    above = pltpu.roll(turned, lax.rem(down + 1, rows), axis=1)
    lane = lax.broadcasted_iota(jnp.int32, value.shape, 2)
    return jnp.where(lane >= carried, here, above)


def slide(n, value, shift_y, shift_x):
    shape = value.shape
    value = value.reshape(shape[0] // n.rows, n.rows, LANES)
    row = lax.broadcasted_iota(jnp.int32, value.shape, 1)
    lane = lax.broadcasted_iota(jnp.int32, value.shape, 2)
    y = row * n.per + lane // n.side - shift_y
    x = lax.rem(lane, n.side) - shift_x
    inside = (y >= 0) & (y < n.side) & (x >= 0) & (x < n.side)
    amount = lax.rem(shift_y * n.side + shift_x + 2 * n.cells, n.cells)
    return jnp.where(inside, flat_roll(value, amount), 0.0).reshape(shape)


def wave_sums(n, values):
    top, half = n.turns // 2, n.turns // 4
    cosines, sines = [None] * (top + 1), [None] * (top + 1)
    for q in range(half + 1):
        sums = []
        for wave in (math.cos, math.sin):
            for parity in (0, 1):
                total = None
                for s in range(parity, n.rows, 2):
                    factor = wave(2.0 * math.pi * q * s / n.turns)
                    total = weighted(total, factor, values[s])
                sums.append(total)
        even_cos, odd_cos, even_sin, odd_sin = sums
        cosines[q] = plus(even_cos, odd_cos)
        cosines[top - q] = minus(even_cos, odd_cos)
        sines[q] = plus(even_sin, odd_sin)
        sines[top - q] = minus(odd_sin, even_sin)
    return cosines, sines


def weighted(total, factor, value):
    if value is None or abs(factor) < 1e-12:
        return total
    if abs(abs(factor) - 1.0) < 1e-12:
        if factor > 0:
            return value if total is None else total + value
        return -value if total is None else total - value
    term = factor * value
    return term if total is None else total + term


def plus(left, right):
    if left is None or right is None:
        return right if left is None else left
    return left + right


def minus(left, right):
    if right is None:
        return left
    return -right if left is None else left - right


def cell_sums(n, cosines, sines):
    top, half = n.turns // 2, n.turns // 4
    values = []
    folded = {}
    for q in range(half + 1):
        if q == top - q:
            folded[q] = (cosines[q], cosines[q], sines[q], sines[q])
        else:
            c, d, s, t = cosines[q], cosines[top - q], sines[q], sines[top - q]
            folded[q] = (plus(c, d), minus(c, d), minus(s, t), plus(s, t))
    for s in range(n.rows):
        total = None
        odd = s % 2
        for q in range(half + 1):
            angle = 2.0 * math.pi * q * s / n.turns
            total = weighted(total, math.cos(angle), folded[q][odd])
            total = weighted(total, math.sin(angle), folded[q][2 + odd])
        values.append(total)
    return values


def forward_band(n, rho, band, planes, lane, twiddle):
    start = pl.multiple_of(band * (TILE * n.rows), TILE * n.rows)
    values = [rho[pl.ds(start + s, TILE, stride=n.rows), :] for s in range(n.rows)]
    cosines, sines = wave_sums(n, values)
    top = n.turns // 2
    first, second = [], []
    for q in range(n.turns):
        same = q <= top
        a = cosines[q if same else n.turns - q]
        b = sines[q if same else n.turns - q]
        ahead = twiddle[q : q + 1, :]
        behind = twiddle[n.turns + q : n.turns + q + 1, :]
        u, w = ahead * a, behind * a
        if q % top:
            u = u + behind * b if same else u - behind * b
            w = w - ahead * b if same else w + ahead * b
        first.append(u)
        second.append(w)
    value = jnp.concatenate([jnp.concatenate(first, axis=0), jnp.concatenate(second, axis=0)], axis=1)
    high, low = split(value)
    value = thrice(high, low, lane)
    rows = pl.ds(pl.multiple_of(band * TILE, TILE), TILE)
    for q in range(n.turns):
        planes[rows, q * n.wide : (q + 1) * n.wide] = value[q * TILE : (q + 1) * TILE, :]


def stacked(value):
    high, low = split(value)
    return jnp.concatenate([high, low, high], axis=0)


def along_z(planes, to_waves, from_waves, green):
    value = dot(to_waves[...], stacked(planes[...])) * green[...]
    planes[...] = dot(from_waves[...], stacked(value))


def back_band(n, planes, band, field, lane_back, twiddle):
    rows = pl.ds(pl.multiple_of(band * TILE, TILE), TILE)
    value = jnp.concatenate([planes[rows, q * n.wide : (q + 1) * n.wide] for q in range(n.turns)], axis=0)
    high, low = split(value)
    value = thrice(high, low, lane_back)
    top = n.turns // 2
    cosines, sines = [None] * (top + 1), [None] * (top + 1)
    for q in range(n.turns):
        part = slice(q * TILE, (q + 1) * TILE)
        u, w = value[part, 0:LANES], value[part, LANES : 2 * LANES]
        ahead = twiddle[q : q + 1, :]
        behind = twiddle[n.turns + q : n.turns + q + 1, :]
        a = ahead * u + behind * w
        b = behind * u - ahead * w
        if q <= top:
            cosines[q] = a
            sines[q] = b if q % top else None
        else:
            cosines[n.turns - q] = cosines[n.turns - q] + a
            sines[n.turns - q] = sines[n.turns - q] - b
    start = pl.multiple_of(band * (TILE * n.rows), TILE * n.rows)
    for s, part in enumerate(cell_sums(n, cosines, sines)):
        field[pl.ds(start + s, TILE, stride=n.rows), :] = part


def kernel(n, listed, placed, orbital, external, *refs):
    table_refs, refs = refs[:8], refs[8:]
    out, refs = refs[0], refs[1:]
    table_dst, refs = refs[:8], refs[8:]
    (own_box, flat, box_send, box_land, place_send, place_land, corner, near, moved, rho, field_flat) = refs[:11]
    (ext_block, ext_flat, dens_grid, dens_send, dens_land, level, read_in, read, planes, pairs) = refs[11:21]
    (listed_in, placed_in, rho_send, rho_land, field_send, field_land, grad_send, grad_land) = refs[21:29]
    (rho_step, rho_steps, field_step, field_steps, grad_step, grad_steps) = refs[29:35]
    local_sem, own_send, own_recv, grp_send, grp_recv = refs[35:]
    to_waves, from_waves, lane, lane_back, twiddle, green, spread, gather = table_dst
    owners, groups, depth, slab = n.owners, n.groups, n.depth, n.slab
    me, team = lax.axis_index("own"), lax.axis_index("grp")
    partner = team + 1 - 2 * lax.rem(team, 2)
    barrier = pltpu.get_barrier_semaphore()
    peers = far_first(n, me)
    for peer in peers:
        there = {"own": peer, "grp": partner}
        pl.semaphore_signal(barrier, inc=1, device_id=there, device_id_type=MESH)
    base = team - lax.rem(team, 2)
    distant = [lax.rem(base + step, groups) for step in range(2, groups)]
    others = [*distant, partner]
    for peer in distant:
        pl.semaphore_signal(barrier, inc=1, device_id={"grp": peer}, device_id_type=MESH)

    small_in = [
        pltpu.make_async_copy(placed, placed_in, local_sem.at[2 + len(table_refs)]),
        pltpu.make_async_copy(listed, listed_in, local_sem.at[3 + len(table_refs)]),
    ]
    for item in small_in:
        item.start()
    own_in = pltpu.make_async_copy(orbital, own_box, local_sem.at[0])
    own_in.start()
    first_level = pl.multiple_of(me * depth // TILE * TILE, TILE)
    taken = ext_block.shape[0]
    ext_in = pltpu.make_async_copy(external.at[pl.ds(first_level, taken)], ext_block, local_sem.at[1])
    ext_in.start()
    table_in = [
        pltpu.make_async_copy(source, target, local_sem.at[2 + i])
        for i, (source, target) in enumerate(zip(table_refs, table_dst))
    ]
    for item in table_in:
        item.start()
    place_index = lax.broadcasted_iota(jnp.int32, place_send.shape, 1)
    for item in small_in:
        item.wait()
    pair_index = lax.broadcasted_iota(jnp.int32, listed_in.shape, 1)
    header = jnp.where(place_index == 0, placed_in[0:1, 0:1], placed_in[0:1, 1:2])
    for turn in range(n.each):
        mine = jnp.sum(jnp.where(pair_index == me * n.each + turn, listed_in[...], 0), axis=1, keepdims=True)
        header = jnp.where(place_index == 2 + 2 * turn, mine[0:1], header)
        header = jnp.where(place_index == 3 + 2 * turn, mine[1:2], header)
    place_send[...] = header
    own_in.wait()
    for s in range(n.rows):
        flat[pl.ds(s, n.levels, stride=n.rows), :] = own_box[:, s * LANES : (s + 1) * LANES].astype(F32)
    for owner in range(owners):
        box_send[owner] = flat[owner * slab : (owner + 1) * slab, :].astype(BF16)
    pl.semaphore_wait(barrier, owners + groups - 2)

    def to_owner(phase, peer, source, target):
        return pltpu.make_async_remote_copy(
            src_ref=source,
            dst_ref=target,
            send_sem=own_send.at[phase, peer],
            recv_sem=own_recv.at[phase, me],
            device_id={"own": peer, "grp": partner},
            device_id_type=MESH,
        )

    def arrive(phase, peer, source, target):
        pltpu.make_async_remote_copy(
            src_ref=source,
            dst_ref=target,
            send_sem=own_send.at[phase, peer],
            recv_sem=own_recv.at[phase, peer],
            device_id={"own": peer, "grp": partner},
            device_id_type=MESH,
        ).wait_recv()

    def arrived(phase, source, target):
        for peer in reversed(peers):
            arrive(phase, peer, source, target(peer))

    def rows_of(index):
        return pl.ds(pl.multiple_of(index * slab, slab), slab)

    def send_coded(phase, peer, value, here, there):
        slot, codes, steps = here
        codes[slot], steps[slot] = encode(value)
        landing, far_codes, far_steps = there
        copies = [
            to_owner(phase, peer, codes.at[slot], far_codes.at[landing]),
            to_owner(phase + 1, peer, steps.at[slot], far_steps.at[landing]),
        ]
        for item in copies:
            item.start()
        return copies

    def take_coded(phase, peer, slot, codes, steps):
        arrive(phase, peer, codes.at[slot], codes.at[slot])
        arrive(phase + 1, peer, steps.at[slot], steps.at[slot])
        return decode(codes[slot], steps[slot])

    sent = []
    boxes_in = []
    for peer in peers:
        boxes_in.append(to_owner(0, peer, place_send, place_land.at[me]))
        boxes_in.append(to_owner(1, peer, box_send.at[peer], box_land.at[me]))
        boxes_in[-2].start()
        boxes_in[-1].start()
    sent += boxes_in
    arrived(0, place_send, lambda peer: place_land.at[peer])
    arrived(1, box_send.at[0], lambda peer: box_land.at[peer])
    for owner in range(owners):
        corner[owner, 0] = place_land[owner, 0, 0]
        corner[owner, 1] = place_land[owner, 0, 1]
        for turn in range(n.each):
            pairs[owner * n.each + turn, 0] = place_land[owner, 0, 2 + 2 * turn]
            pairs[owner * n.each + turn, 1] = place_land[owner, 0, 3 + 2 * turn]

    def shift_of(row):
        first, second = pairs[row, 0], pairs[row, 1]
        return corner[second, 0] - corner[first, 0], corner[second, 1] - corner[first, 1]

    rho_in = []
    for peer in peers:
        for turn in range(n.each):
            row = peer * n.each + turn
            dy, dx = shift_of(row)
            a = box_land[pairs[row, 0]].astype(F32)
            b = slide(n, box_land[pairs[row, 1]].astype(F32), dy, dx)
            near[row] = a
            moved[row] = b
            rho_in += send_coded(2 + 2 * turn, peer, a * b, (row, rho_send, rho_step), (me * n.each + turn, rho_land, rho_steps))
    sent += rho_in

    for item in table_in:
        item.wait()
    grid_shape = (depth, n.grid_rows, LANES)
    for owner in range(owners):
        value = box_land[owner].astype(F32)
        high, low = split(value * value)
        wide = dot(high, spread[...]) + dot(low, spread[...])
        for z in range(depth):
            start = z * n.grid_rows
            for half in range(n.halves):
                rows = pl.ds(start + half, n.rows, stride=n.halves)
                dens_grid[owner, rows, :] = wide[z * n.rows : (z + 1) * n.rows, half * LANES : (half + 1) * LANES]
            rest = n.grid_rows - n.rows * n.halves
            dens_grid[owner, start + n.rows * n.halves : start + n.grid_rows, :] = jnp.zeros((rest, LANES), F32)
    total = jnp.zeros(grid_shape, F32)
    for owner in range(owners):
        amount = corner[owner, 0] * n.grid + corner[owner, 1]
        total = total + flat_roll(dens_grid[owner].reshape(grid_shape), amount)
    dens_send[...] = total.reshape(dens_send.shape)
    dens_land[team] = dens_send[...]

    def dens_copy(peer, sender):
        return pltpu.make_async_remote_copy(
            src_ref=dens_send,
            dst_ref=dens_land.at[sender],
            send_sem=grp_send.at[peer],
            recv_sem=grp_recv.at[sender],
            device_id={"grp": peer},
            device_id_type=MESH,
        )

    for peer in others:
        dens_copy(peer, team).start()

    low = (me < owners // 2).astype(jnp.int32)
    far_bands = [low * (n.bands - 1 - k) + (1 - low) * k for k in range(n.bands)]
    rho_base = 2
    field_base = rho_base + 2 * n.each
    grad_base = field_base + 2 * n.each
    field_in = []
    for turn in range(n.each):
        for band in reversed(far_bands):
            for index in range(n.share):
                peer = band * n.share + index
                rho[rows_of(peer), :] = take_coded(rho_base + 2 * turn, peer, peer * n.each + turn, rho_land, rho_steps)
            forward_band(n, rho, band, planes, lane, twiddle)
        along_z(planes, to_waves, from_waves, green)
        for band in far_bands:
            back_band(n, planes, band, field_flat, lane_back, twiddle)
            for index in range(n.share):
                peer = band * n.share + index
                slot = peer * n.each + turn
                here, there = (slot, field_send, field_step), (me * n.each + turn, field_land, field_steps)
                field_in += send_coded(field_base + 2 * turn, peer, field_flat[rows_of(peer), :], here, there)
    sent += field_in

    ext_in.wait()
    ext_values = ext_block[...].astype(F32)
    for k in range(n.grid_rows):
        ext_flat[pl.ds(k, taken, stride=n.grid_rows), :] = ext_values[:, k * LANES : (k + 1) * LANES]
    for peer in others:
        dens_copy(peer, peer).wait_recv()
    density = dens_land[0]
    for index in range(1, groups):
        density = density + dens_land[index]
    start = pl.multiple_of((me * depth - first_level) * n.grid_rows, n.grid_rows)
    outside = ext_flat[pl.ds(start, depth * n.grid_rows), :]
    safe = jnp.where(density > 0.0, density, 1.0)
    root = jnp.exp(jnp.log(safe) * (1.0 / 3.0))
    root = root - (root - safe / (root * root)) * (1.0 / 3.0)
    level[...] = outside - EXCHANGE_COEF * jnp.where(density > 0.0, root, 0.0)
    whole = n.grid_rows * LANES
    for owner in range(owners):
        amount = lax.rem(whole - corner[owner, 0] * n.grid - corner[owner, 1], whole)
        turned = flat_roll(level[...].reshape(grid_shape), amount)
        read_in[owner] = turned.reshape(read_in.shape[1:])
        parts = []
        for z in range(depth):
            pieces = [
                read_in[owner, pl.ds(z * n.grid_rows + half, n.rows, stride=n.halves), :] for half in range(n.halves)
            ]
            parts.append(jnp.concatenate(pieces, axis=1) if n.halves > 1 else pieces[0])
        value = jnp.concatenate(parts, axis=0) if depth > 1 else parts[0]
        high, low = split(value)
        read[owner] = (dot(high, gather[...]) + dot(low, gather[...])) * box_land[owner].astype(F32)

    for peer in reversed(peers):
        for turn in range(n.each):
            row = peer * n.each + turn
            dy, dx = shift_of(row)
            field = take_coded(field_base + 2 * turn, peer, row, field_land, field_steps) * MIXING
            moved[row] = field * moved[row]
            near[row] = slide(n, field * near[row], -dy, -dx)
    for peer in peers:
        total = read[peer]
        for row in range(n.pairs):
            total = total - jnp.where(pairs[row, 0] == peer, moved[row], 0.0)
            total = total - jnp.where(pairs[row, 1] == peer, near[row], 0.0)
        sent += send_coded(grad_base, peer, total, (peer, grad_send, grad_step), (me, grad_land, grad_steps))
    for peer in reversed(peers):
        out[rows_of(peer), :] = take_coded(grad_base, peer, peer, grad_land, grad_steps)
    for item in sent:
        item.wait_send()
    for peer in others:
        dens_copy(peer, team).wait_send()


def body(owners, groups, orbitals, offsets, pairs, ext_pot):
    _, levels, cells = orbitals.shape
    n = Sizes(owners, groups, levels, cells, ext_pot.shape[1], pairs.shape[0])
    consts = tables(n)
    taken = max(n.depth, TILE)
    slabs = (n.owners, n.slab, LANES)
    flat_rows = levels * n.rows
    scratch = [VMEM(c.shape, c.dtype) for c in consts]
    counts = (n.pairs, n.pairs, n.pairs, n.pairs, owners, owners)
    scratch += [
        VMEM((levels, cells), BF16),
        VMEM((flat_rows, LANES), F32),
        VMEM(slabs, BF16),
        VMEM(slabs, BF16),
        VMEM((1, LANES), jnp.int32),
        VMEM((owners, 1, LANES), jnp.int32),
        pltpu.SMEM((owners, 2), jnp.int32),
        VMEM((n.pairs, n.slab, LANES), F32),
        VMEM((n.pairs, n.slab, LANES), F32),
        VMEM((flat_rows, LANES), F32),
        VMEM((flat_rows, LANES), F32),
        VMEM((taken, ext_pot.shape[1]), BF16),
        VMEM((taken * n.grid_rows, LANES), F32),
        VMEM((owners, n.depth * n.grid_rows, LANES), F32),
        VMEM((n.depth * n.grid_rows, LANES), F32),
        VMEM((groups, n.depth * n.grid_rows, LANES), F32),
        VMEM((n.depth * n.grid_rows, LANES), F32),
        VMEM((owners, n.depth * n.grid_rows, LANES), F32),
        VMEM(slabs, F32),
        VMEM((levels, n.turns * n.wide), F32),
        pltpu.SMEM(pairs.shape, jnp.int32),
        VMEM(pairs.shape[::-1], jnp.int32),
        VMEM(offsets.shape, jnp.int32),
        *[VMEM((count, n.slab, LANES), CODE) for count in counts],
        *[VMEM((count, 1, LANES), F32) for count in counts],
        pltpu.SemaphoreType.DMA((4 + len(consts),)),
        pltpu.SemaphoreType.DMA((4 + 4 * n.each, owners)),
        pltpu.SemaphoreType.DMA((4 + 4 * n.each, owners)),
        pltpu.SemaphoreType.DMA((groups,)),
        pltpu.SemaphoreType.DMA((groups,)),
    ]
    anywhere = pl.BlockSpec(memory_space=pl.ANY)
    slab_out = pl.pallas_call(
        functools.partial(kernel, n),
        out_shape=VMEM((flat_rows, LANES), F32),
        in_specs=[anywhere] * (4 + len(consts)),
        out_specs=pl.BlockSpec(memory_space=VMEM),
        scratch_shapes=scratch,
        compiler_params=pltpu.CompilerParams(collective_id=0, has_side_effects=True),
        name="gradient",
    )(pairs.T, offsets, orbitals[0], ext_pot, *consts)
    return slab_out.reshape(1, levels, cells)


def solution(mesh):
    in_specs = (P(("grp", "own"), None, None), P(("grp", "own"), None), P("grp", None), P())
    out_specs = P(("grp", "own"), None, None)
    run = functools.partial(body, mesh.shape["own"], mesh.shape["grp"])
    return jax.shard_map(run, mesh=mesh, in_specs=in_specs, out_specs=out_specs, check_vma=False)
```

```python
import functools
import math

import jax
import jax.numpy as jnp
import ml_dtypes
import numpy as np
from jax import lax
from jax.experimental import pallas as pl
from jax.experimental.pallas import tpu as pltpu
from jax.sharding import PartitionSpec as P

SCREEN = 0.0025
MIXING = 0.25
EXCHANGE_COEF = (3.0 / math.pi) ** (1.0 / 3.0)
LANES = 128
TILE = 8
AHEAD = 16
BEHIND = 8
VMEM = pltpu.VMEM
MESH = pl.DeviceIdType.MESH
F32 = jnp.float32
BF16 = jnp.bfloat16
CODE = jnp.int16
STEPS = 32767.0
TINY = 1e-30


class Sizes:
    def __init__(self, owners, groups, levels, cells, grid_cells, pairs):
        self.owners, self.groups, self.levels, self.cells, self.pairs = owners, groups, levels, cells, pairs
        self.side, self.grid = math.isqrt(cells), math.isqrt(grid_cells)
        self.depth = levels // owners
        self.each = pairs // owners
        self.rows = cells // LANES
        self.per = LANES // self.side
        self.slab = self.depth * self.rows
        self.grid_rows = grid_cells // LANES
        self.halves = self.per * self.grid // LANES
        self.waves = 2 * levels
        self.turns = 2 * self.side // self.per
        self.wide = self.per * 2 * self.side
        self.ahead, self.behind = min(AHEAD, levels), min(BEHIND, levels)


def halves_of(table):
    high = table.astype(ml_dtypes.bfloat16)
    low = (table - high.astype(np.float64)).astype(ml_dtypes.bfloat16)
    return high, low


def cas(angle):
    return np.cos(angle) + np.sin(angle)


def tables(n):
    side, per, levels = n.side, n.per, n.levels
    along_z = cas(2.0 * np.pi / n.waves * np.outer(np.arange(n.waves), np.arange(levels)))
    high, low = halves_of(along_z)
    to_waves = np.concatenate([high, high, low], axis=1)
    high, low = halves_of(along_z.T)
    from_waves = np.concatenate([high, high, low], axis=1)
    along_x = cas(np.pi / side * np.outer(np.arange(side), np.arange(2 * side)))
    phase = 2.0 * np.pi / per * np.outer(np.arange(per), np.arange(per))
    lane = np.concatenate(
        [np.einsum("yh,xk->yxhk", wave(phase), along_x).reshape(LANES, n.wide) for wave in (np.cos, np.sin)]
    )
    lane = np.stack(halves_of(lane))
    lane_back = np.ascontiguousarray(np.swapaxes(lane, 1, 2))
    angle = np.pi / side * np.outer(np.arange(n.turns), np.arange(LANES) // side)
    twiddle = np.concatenate([cas(angle), cas(-angle)]).astype(np.float32)

    def squares(length):
        m = np.arange(length)
        return (2.0 * np.pi / length * np.where(m < length // 2, m, m - length)) ** 2

    z = squares(n.waves).reshape(n.waves, 1, 1, 1)
    y = squares(2 * side).reshape(per, n.turns).T.reshape(1, n.turns, per, 1)
    x = squares(2 * side).reshape(1, 1, 1, 2 * side)
    green = 4.0 * np.pi / (z + y + x + SCREEN) / (n.waves * 4.0 * side * side)
    green = green.reshape(n.waves, n.turns * n.wide).astype(np.float32)
    spread = np.zeros((LANES, n.halves * LANES), ml_dtypes.bfloat16)
    for cell in range(LANES):
        spread[cell, cell // side * n.grid + cell % side] = 1
    gather = np.ascontiguousarray(spread.T)
    return to_waves, from_waves, lane, lane_back, twiddle, green, spread, gather


def far_first(n, me):
    near = n.owners >> ((n.owners.bit_length() - 1) // 2)
    near = n.owners // near
    far = n.owners // near
    z, y = me // near, lax.rem(me, near)
    low = (z < far // 2).astype(jnp.int32)
    here = low * (far - 1 - z) + (1 - low) * z
    peers = []
    for k in range(far - 1):
        place = k + (k >= here).astype(jnp.int32)
        level = low * (far - 1 - place) + (1 - low) * place
        peers += [level * near + lax.rem(y + 1 + step, near) for step in range(near)]
    return peers + [z * near + lax.rem(y + step, near) for step in range(1, near + 1)]


def split(value):
    high = value.astype(BF16)
    return high, (value - high.astype(F32)).astype(BF16)


def encode(value):
    largest = jnp.max(jnp.abs(value), axis=0, keepdims=True)
    largest = jnp.maximum(largest, TINY)
    code = jnp.round(value * (STEPS / largest)).astype(jnp.int32)
    return code.astype(CODE), largest * (1.0 / STEPS)


def decode(code, step):
    return code.astype(jnp.int32).astype(F32) * step


def dot(left, right):
    return jnp.dot(left, right, preferred_element_type=F32)


def thrice(high, low, matrix):
    return dot(high, matrix[0]) + dot(low, matrix[0]) + dot(high, matrix[1])


def flat_roll(value, amount):
    carried = lax.rem(amount, LANES)
    down = amount // LANES
    rows = value.shape[1]
    turned = pltpu.roll(value, carried, axis=2)
    here = pltpu.roll(turned, down, axis=1)
    above = pltpu.roll(turned, lax.rem(down + 1, rows), axis=1)
    lane = lax.broadcasted_iota(jnp.int32, value.shape, 2)
    return jnp.where(lane >= carried, here, above)


def slide(n, value, shift_y, shift_x):
    shape = value.shape
    value = value.reshape(shape[0] // n.rows, n.rows, LANES)
    row = lax.broadcasted_iota(jnp.int32, value.shape, 1)
    lane = lax.broadcasted_iota(jnp.int32, value.shape, 2)
    y = row * n.per + lane // n.side - shift_y
    x = lax.rem(lane, n.side) - shift_x
    inside = (y >= 0) & (y < n.side) & (x >= 0) & (x < n.side)
    amount = lax.rem(shift_y * n.side + shift_x + 2 * n.cells, n.cells)
    return jnp.where(inside, flat_roll(value, amount), 0.0).reshape(shape)


def wave_sums(n, values):
    top, half = n.turns // 2, n.turns // 4
    cosines, sines = [None] * (top + 1), [None] * (top + 1)
    for q in range(half + 1):
        sums = []
        for wave in (math.cos, math.sin):
            for parity in (0, 1):
                total = None
                for s in range(parity, n.rows, 2):
                    factor = wave(2.0 * math.pi * q * s / n.turns)
                    total = weighted(total, factor, values[s])
                sums.append(total)
        even_cos, odd_cos, even_sin, odd_sin = sums
        cosines[q] = plus(even_cos, odd_cos)
        cosines[top - q] = minus(even_cos, odd_cos)
        sines[q] = plus(even_sin, odd_sin)
        sines[top - q] = minus(odd_sin, even_sin)
    return cosines, sines


def weighted(total, factor, value):
    if value is None or abs(factor) < 1e-12:
        return total
    if abs(abs(factor) - 1.0) < 1e-12:
        if factor > 0:
            return value if total is None else total + value
        return -value if total is None else total - value
    term = factor * value
    return term if total is None else total + term


def plus(left, right):
    if left is None or right is None:
        return right if left is None else left
    return left + right


def minus(left, right):
    if right is None:
        return left
    return -right if left is None else left - right


def cell_sums(n, cosines, sines):
    top, half = n.turns // 2, n.turns // 4
    values = []
    folded = {}
    for q in range(half + 1):
        if q == top - q:
            folded[q] = (cosines[q], cosines[q], sines[q], sines[q])
        else:
            c, d, s, t = cosines[q], cosines[top - q], sines[q], sines[top - q]
            folded[q] = (plus(c, d), minus(c, d), minus(s, t), plus(s, t))
    for s in range(n.rows):
        total = None
        odd = s % 2
        for q in range(half + 1):
            angle = 2.0 * math.pi * q * s / n.turns
            total = weighted(total, math.cos(angle), folded[q][odd])
            total = weighted(total, math.sin(angle), folded[q][2 + odd])
        values.append(total)
    return values


def forward_band(n, rho, band, size, planes, lane, twiddle):
    start = pl.multiple_of(band * (size * n.rows), size * n.rows)
    values = [rho[pl.ds(start + s, size, stride=n.rows), :] for s in range(n.rows)]
    cosines, sines = wave_sums(n, values)
    top = n.turns // 2
    first, second = [], []
    for q in range(n.turns):
        same = q <= top
        a = cosines[q if same else n.turns - q]
        b = sines[q if same else n.turns - q]
        ahead = twiddle[q : q + 1, :]
        behind = twiddle[n.turns + q : n.turns + q + 1, :]
        u, w = ahead * a, behind * a
        if q % top:
            u = u + behind * b if same else u - behind * b
            w = w - ahead * b if same else w + ahead * b
        first.append(u)
        second.append(w)
    value = jnp.concatenate([jnp.concatenate(first, axis=0), jnp.concatenate(second, axis=0)], axis=1)
    high, low = split(value)
    value = thrice(high, low, lane)
    rows = pl.ds(pl.multiple_of(band * size, size), size)
    for q in range(n.turns):
        planes[rows, q * n.wide : (q + 1) * n.wide] = value[q * size : (q + 1) * size, :]


def stacked(value):
    high, low = split(value)
    return jnp.concatenate([high, low, high], axis=0)


def along_z(planes, to_waves, from_waves, green):
    value = dot(to_waves[...], stacked(planes[...])) * green[...]
    planes[...] = dot(from_waves[...], stacked(value))


def back_band(n, planes, band, size, field, lane_back, twiddle):
    rows = pl.ds(pl.multiple_of(band * size, size), size)
    value = jnp.concatenate([planes[rows, q * n.wide : (q + 1) * n.wide] for q in range(n.turns)], axis=0)
    high, low = split(value)
    value = thrice(high, low, lane_back)
    top = n.turns // 2
    cosines, sines = [None] * (top + 1), [None] * (top + 1)
    for q in range(n.turns):
        part = slice(q * size, (q + 1) * size)
        u, w = value[part, 0:LANES], value[part, LANES : 2 * LANES]
        ahead = twiddle[q : q + 1, :]
        behind = twiddle[n.turns + q : n.turns + q + 1, :]
        a = ahead * u + behind * w
        b = behind * u - ahead * w
        if q <= top:
            cosines[q] = a
            sines[q] = b if q % top else None
        else:
            cosines[n.turns - q] = cosines[n.turns - q] + a
            sines[n.turns - q] = sines[n.turns - q] - b
    start = pl.multiple_of(band * (size * n.rows), size * n.rows)
    for s, part in enumerate(cell_sums(n, cosines, sines)):
        field[pl.ds(start + s, size, stride=n.rows), :] = part


def kernel(n, listed, placed, orbital, external, *refs):
    table_refs, refs = refs[:8], refs[8:]
    out, refs = refs[0], refs[1:]
    table_dst, refs = refs[:8], refs[8:]
    (own_box, flat, box_send, box_land, place_send, place_land, corner, near, moved, rho, field_flat) = refs[:11]
    (ext_block, ext_flat, dens_grid, dens_send, dens_land, level, read_in, read, planes, pairs) = refs[11:21]
    (listed_in, placed_in, rho_send, rho_land, field_send, field_land, grad_send, grad_land) = refs[21:29]
    (rho_step, rho_steps, field_step, field_steps, grad_step, grad_steps) = refs[29:35]
    local_sem, own_send, own_recv, grp_send, grp_recv = refs[35:]
    to_waves, from_waves, lane, lane_back, twiddle, green, spread, gather = table_dst
    owners, groups, depth, slab = n.owners, n.groups, n.depth, n.slab
    me, team = lax.axis_index("own"), lax.axis_index("grp")
    partner = team + 1 - 2 * lax.rem(team, 2)
    barrier = pltpu.get_barrier_semaphore()
    peers = far_first(n, me)
    for peer in peers:
        there = {"own": peer, "grp": partner}
        pl.semaphore_signal(barrier, inc=1, device_id=there, device_id_type=MESH)
    base = team - lax.rem(team, 2)
    distant = [lax.rem(base + step, groups) for step in range(2, groups)]
    others = [*distant, partner]
    for peer in distant:
        pl.semaphore_signal(barrier, inc=1, device_id={"grp": peer}, device_id_type=MESH)

    small_in = [
        pltpu.make_async_copy(placed, placed_in, local_sem.at[2 + len(table_refs)]),
        pltpu.make_async_copy(listed, listed_in, local_sem.at[3 + len(table_refs)]),
    ]
    for item in small_in:
        item.start()
    own_in = pltpu.make_async_copy(orbital, own_box, local_sem.at[0])
    own_in.start()
    first_level = pl.multiple_of(me * depth // TILE * TILE, TILE)
    taken = ext_block.shape[0]
    ext_in = pltpu.make_async_copy(external.at[pl.ds(first_level, taken)], ext_block, local_sem.at[1])
    ext_in.start()
    table_in = [
        pltpu.make_async_copy(source, target, local_sem.at[2 + i])
        for i, (source, target) in enumerate(zip(table_refs, table_dst))
    ]
    for item in table_in:
        item.start()
    place_index = lax.broadcasted_iota(jnp.int32, place_send.shape, 1)
    for item in small_in:
        item.wait()
    pair_index = lax.broadcasted_iota(jnp.int32, listed_in.shape, 1)
    header = jnp.where(place_index == 0, placed_in[0:1, 0:1], placed_in[0:1, 1:2])
    for turn in range(n.each):
        mine = jnp.sum(jnp.where(pair_index == me * n.each + turn, listed_in[...], 0), axis=1, keepdims=True)
        header = jnp.where(place_index == 2 + 2 * turn, mine[0:1], header)
        header = jnp.where(place_index == 3 + 2 * turn, mine[1:2], header)
    place_send[...] = header
    own_in.wait()
    for s in range(n.rows):
        flat[pl.ds(s, n.levels, stride=n.rows), :] = own_box[:, s * LANES : (s + 1) * LANES].astype(F32)
    for owner in range(owners):
        box_send[owner] = flat[owner * slab : (owner + 1) * slab, :].astype(BF16)
    pl.semaphore_wait(barrier, owners + groups - 2)

    def to_owner(phase, peer, source, target):
        return pltpu.make_async_remote_copy(
            src_ref=source,
            dst_ref=target,
            send_sem=own_send.at[phase, peer],
            recv_sem=own_recv.at[phase, me],
            device_id={"own": peer, "grp": partner},
            device_id_type=MESH,
        )

    def arrive(phase, peer, source, target):
        pltpu.make_async_remote_copy(
            src_ref=source,
            dst_ref=target,
            send_sem=own_send.at[phase, peer],
            recv_sem=own_recv.at[phase, peer],
            device_id={"own": peer, "grp": partner},
            device_id_type=MESH,
        ).wait_recv()

    def arrived(phase, source, target):
        for peer in reversed(peers):
            arrive(phase, peer, source, target(peer))

    def rows_of(index):
        return pl.ds(pl.multiple_of(index * slab, slab), slab)

    def send_coded(phase, peer, value, here, there):
        slot, codes, steps = here
        codes[slot], steps[slot] = encode(value)
        landing, far_codes, far_steps = there
        copies = [
            to_owner(phase, peer, codes.at[slot], far_codes.at[landing]),
            to_owner(phase + 1, peer, steps.at[slot], far_steps.at[landing]),
        ]
        for item in copies:
            item.start()
        return copies

    def take_coded(phase, peer, slot, codes, steps):
        arrive(phase, peer, codes.at[slot], codes.at[slot])
        arrive(phase + 1, peer, steps.at[slot], steps.at[slot])
        return decode(codes[slot], steps[slot])

    sent = []
    boxes_in = []
    for peer in peers:
        boxes_in.append(to_owner(0, peer, place_send, place_land.at[me]))
        boxes_in.append(to_owner(1, peer, box_send.at[peer], box_land.at[me]))
        boxes_in[-2].start()
        boxes_in[-1].start()
    sent += boxes_in
    arrived(0, place_send, lambda peer: place_land.at[peer])
    arrived(1, box_send.at[0], lambda peer: box_land.at[peer])
    for owner in range(owners):
        corner[owner, 0] = place_land[owner, 0, 0]
        corner[owner, 1] = place_land[owner, 0, 1]
        for turn in range(n.each):
            pairs[owner * n.each + turn, 0] = place_land[owner, 0, 2 + 2 * turn]
            pairs[owner * n.each + turn, 1] = place_land[owner, 0, 3 + 2 * turn]

    def shift_of(row):
        first, second = pairs[row, 0], pairs[row, 1]
        return corner[second, 0] - corner[first, 0], corner[second, 1] - corner[first, 1]

    rho_in = []
    for peer in peers:
        for turn in range(n.each):
            row = peer * n.each + turn
            dy, dx = shift_of(row)
            a = box_land[pairs[row, 0]].astype(F32)
            b = slide(n, box_land[pairs[row, 1]].astype(F32), dy, dx)
            near[row] = a
            moved[row] = b
            rho_in += send_coded(2 + 2 * turn, peer, a * b, (row, rho_send, rho_step), (me * n.each + turn, rho_land, rho_steps))
    sent += rho_in

    for item in table_in:
        item.wait()
    grid_shape = (depth, n.grid_rows, LANES)
    for owner in range(owners):
        value = box_land[owner].astype(F32)
        high, low = split(value * value)
        wide = dot(high, spread[...]) + dot(low, spread[...])
        for z in range(depth):
            start = z * n.grid_rows
            for half in range(n.halves):
                rows = pl.ds(start + half, n.rows, stride=n.halves)
                dens_grid[owner, rows, :] = wide[z * n.rows : (z + 1) * n.rows, half * LANES : (half + 1) * LANES]
            rest = n.grid_rows - n.rows * n.halves
            dens_grid[owner, start + n.rows * n.halves : start + n.grid_rows, :] = jnp.zeros((rest, LANES), F32)
    total = jnp.zeros(grid_shape, F32)
    for owner in range(owners):
        amount = corner[owner, 0] * n.grid + corner[owner, 1]
        total = total + flat_roll(dens_grid[owner].reshape(grid_shape), amount)
    dens_send[...] = total.reshape(dens_send.shape)
    dens_land[team] = dens_send[...]

    def dens_copy(peer, sender):
        return pltpu.make_async_remote_copy(
            src_ref=dens_send,
            dst_ref=dens_land.at[sender],
            send_sem=grp_send.at[peer],
            recv_sem=grp_recv.at[sender],
            device_id={"grp": peer},
            device_id_type=MESH,
        )

    for peer in others:
        dens_copy(peer, team).start()

    low = (me < owners // 2).astype(jnp.int32)

    def far_bands(size):
        count = n.levels // size
        return [low * (count - 1 - k) + (1 - low) * k for k in range(count)]

    rho_base = 2
    field_base = rho_base + 2 * n.each
    grad_base = field_base + 2 * n.each
    field_in = []
    for turn in range(n.each):
        for band in reversed(far_bands(n.ahead)):
            for index in range(n.ahead // depth):
                peer = band * (n.ahead // depth) + index
                rho[rows_of(peer), :] = take_coded(rho_base + 2 * turn, peer, peer * n.each + turn, rho_land, rho_steps)
            forward_band(n, rho, band, n.ahead, planes, lane, twiddle)
        along_z(planes, to_waves, from_waves, green)
        for band in far_bands(n.behind):
            back_band(n, planes, band, n.behind, field_flat, lane_back, twiddle)
            for index in range(n.behind // depth):
                peer = band * (n.behind // depth) + index
                slot = peer * n.each + turn
                here, there = (slot, field_send, field_step), (me * n.each + turn, field_land, field_steps)
                field_in += send_coded(field_base + 2 * turn, peer, field_flat[rows_of(peer), :], here, there)
    sent += field_in

    ext_in.wait()
    ext_values = ext_block[...].astype(F32)
    for k in range(n.grid_rows):
        ext_flat[pl.ds(k, taken, stride=n.grid_rows), :] = ext_values[:, k * LANES : (k + 1) * LANES]
    for peer in others:
        dens_copy(peer, peer).wait_recv()
    density = dens_land[0]
    for index in range(1, groups):
        density = density + dens_land[index]
    start = pl.multiple_of((me * depth - first_level) * n.grid_rows, n.grid_rows)
    outside = ext_flat[pl.ds(start, depth * n.grid_rows), :]
    safe = jnp.where(density > 0.0, density, 1.0)
    root = jnp.exp(jnp.log(safe) * (1.0 / 3.0))
    root = root - (root - safe / (root * root)) * (1.0 / 3.0)
    level[...] = outside - EXCHANGE_COEF * jnp.where(density > 0.0, root, 0.0)
    whole = n.grid_rows * LANES
    for owner in range(owners):
        amount = lax.rem(whole - corner[owner, 0] * n.grid - corner[owner, 1], whole)
        turned = flat_roll(level[...].reshape(grid_shape), amount)
        read_in[owner] = turned.reshape(read_in.shape[1:])
        parts = []
        for z in range(depth):
            pieces = [
                read_in[owner, pl.ds(z * n.grid_rows + half, n.rows, stride=n.halves), :] for half in range(n.halves)
            ]
            parts.append(jnp.concatenate(pieces, axis=1) if n.halves > 1 else pieces[0])
        value = jnp.concatenate(parts, axis=0) if depth > 1 else parts[0]
        high, low = split(value)
        read[owner] = (dot(high, gather[...]) + dot(low, gather[...])) * box_land[owner].astype(F32)

    for peer in reversed(peers):
        for turn in range(n.each):
            row = peer * n.each + turn
            dy, dx = shift_of(row)
            field = take_coded(field_base + 2 * turn, peer, row, field_land, field_steps) * MIXING
            moved[row] = field * moved[row]
            near[row] = slide(n, field * near[row], -dy, -dx)
    for peer in peers:
        total = read[peer]
        for row in range(n.pairs):
            total = total - jnp.where(pairs[row, 0] == peer, moved[row], 0.0)
            total = total - jnp.where(pairs[row, 1] == peer, near[row], 0.0)
        sent += send_coded(grad_base, peer, total, (peer, grad_send, grad_step), (me, grad_land, grad_steps))
    for peer in reversed(peers):
        out[rows_of(peer), :] = take_coded(grad_base, peer, peer, grad_land, grad_steps)
    for item in sent:
        item.wait_send()
    for peer in others:
        dens_copy(peer, team).wait_send()


def body(owners, groups, orbitals, offsets, pairs, ext_pot):
    _, levels, cells = orbitals.shape
    n = Sizes(owners, groups, levels, cells, ext_pot.shape[1], pairs.shape[0])
    consts = tables(n)
    taken = max(n.depth, TILE)
    slabs = (n.owners, n.slab, LANES)
    flat_rows = levels * n.rows
    scratch = [VMEM(c.shape, c.dtype) for c in consts]
    counts = (n.pairs, n.pairs, n.pairs, n.pairs, owners, owners)
    scratch += [
        VMEM((levels, cells), BF16),
        VMEM((flat_rows, LANES), F32),
        VMEM(slabs, BF16),
        VMEM(slabs, BF16),
        VMEM((1, LANES), jnp.int32),
        VMEM((owners, 1, LANES), jnp.int32),
        pltpu.SMEM((owners, 2), jnp.int32),
        VMEM((n.pairs, n.slab, LANES), F32),
        VMEM((n.pairs, n.slab, LANES), F32),
        VMEM((flat_rows, LANES), F32),
        VMEM((flat_rows, LANES), F32),
        VMEM((taken, ext_pot.shape[1]), BF16),
        VMEM((taken * n.grid_rows, LANES), F32),
        VMEM((owners, n.depth * n.grid_rows, LANES), F32),
        VMEM((n.depth * n.grid_rows, LANES), F32),
        VMEM((groups, n.depth * n.grid_rows, LANES), F32),
        VMEM((n.depth * n.grid_rows, LANES), F32),
        VMEM((owners, n.depth * n.grid_rows, LANES), F32),
        VMEM(slabs, F32),
        VMEM((levels, n.turns * n.wide), F32),
        pltpu.SMEM(pairs.shape, jnp.int32),
        VMEM(pairs.shape[::-1], jnp.int32),
        VMEM(offsets.shape, jnp.int32),
        *[VMEM((count, n.slab, LANES), CODE) for count in counts],
        *[VMEM((count, 1, LANES), F32) for count in counts],
        pltpu.SemaphoreType.DMA((4 + len(consts),)),
        pltpu.SemaphoreType.DMA((4 + 4 * n.each, owners)),
        pltpu.SemaphoreType.DMA((4 + 4 * n.each, owners)),
        pltpu.SemaphoreType.DMA((groups,)),
        pltpu.SemaphoreType.DMA((groups,)),
    ]
    anywhere = pl.BlockSpec(memory_space=pl.ANY)
    slab_out = pl.pallas_call(
        functools.partial(kernel, n),
        out_shape=VMEM((flat_rows, LANES), F32),
        in_specs=[anywhere] * (4 + len(consts)),
        out_specs=pl.BlockSpec(memory_space=VMEM),
        scratch_shapes=scratch,
        compiler_params=pltpu.CompilerParams(collective_id=0, has_side_effects=True),
        name="gradient",
    )(pairs.T, offsets, orbitals[0], ext_pot, *consts)
    return slab_out.reshape(1, levels, cells)


def solution(mesh):
    in_specs = (P(("grp", "own"), None, None), P(("grp", "own"), None), P("grp", None), P())
    out_specs = P(("grp", "own"), None, None)
    run = functools.partial(body, mesh.shape["own"], mesh.shape["grp"])
    return jax.shard_map(run, mesh=mesh, in_specs=in_specs, out_specs=out_specs, check_vma=False)
```

```python
import functools
import math

import jax
import jax.numpy as jnp
import ml_dtypes
import numpy as np
from jax import lax
from jax.experimental import pallas as pl
from jax.experimental.pallas import tpu as pltpu
from jax.sharding import PartitionSpec as P

SCREEN = 0.0025
MIXING = 0.25
EXCHANGE_COEF = (3.0 / math.pi) ** (1.0 / 3.0)
LANES = 128
TILE = 8
AHEAD = 16
BEHIND = 8
VMEM = pltpu.VMEM
MESH = pl.DeviceIdType.MESH
F32 = jnp.float32
BF16 = jnp.bfloat16
CODE = jnp.int16
STEPS = 32767.0
TINY = 1e-30


class Sizes:
    def __init__(self, owners, groups, levels, cells, grid_cells, pairs):
        self.owners, self.groups, self.levels, self.cells, self.pairs = owners, groups, levels, cells, pairs
        self.side, self.grid = math.isqrt(cells), math.isqrt(grid_cells)
        self.depth = levels // owners
        self.each = pairs // owners
        self.rows = cells // LANES
        self.per = LANES // self.side
        self.slab = self.depth * self.rows
        self.grid_rows = grid_cells // LANES
        self.halves = self.per * self.grid // LANES
        self.waves = 2 * levels
        self.turns = 2 * self.side // self.per
        self.wide = self.per * 2 * self.side
        self.ahead, self.behind = min(AHEAD, levels), min(BEHIND, levels)


def halves_of(table):
    high = table.astype(ml_dtypes.bfloat16)
    low = (table - high.astype(np.float64)).astype(ml_dtypes.bfloat16)
    return high, low


def cas(angle):
    return np.cos(angle) + np.sin(angle)


def tables(n):
    side, per, levels = n.side, n.per, n.levels
    along_z = cas(2.0 * np.pi / n.waves * np.outer(np.arange(n.waves), np.arange(levels)))
    high, low = halves_of(along_z)
    to_waves = np.concatenate([high, high, low], axis=1)
    high, low = halves_of(along_z.T)
    from_waves = np.concatenate([high, high, low], axis=1)
    along_x = cas(np.pi / side * np.outer(np.arange(side), np.arange(2 * side)))
    phase = 2.0 * np.pi / per * np.outer(np.arange(per), np.arange(per))
    lane = np.concatenate(
        [np.einsum("yh,xk->yxhk", wave(phase), along_x).reshape(LANES, n.wide) for wave in (np.cos, np.sin)]
    )
    lane = np.stack(halves_of(lane))
    lane_back = np.ascontiguousarray(np.swapaxes(lane, 1, 2))
    angle = np.pi / side * np.outer(np.arange(n.turns), np.arange(LANES) // side)
    twiddle = np.concatenate([cas(angle), cas(-angle)]).astype(np.float32)

    def squares(length):
        m = np.arange(length)
        return (2.0 * np.pi / length * np.where(m < length // 2, m, m - length)) ** 2

    z = squares(n.waves).reshape(n.waves, 1, 1, 1)
    y = squares(2 * side).reshape(per, n.turns).T.reshape(1, n.turns, per, 1)
    x = squares(2 * side).reshape(1, 1, 1, 2 * side)
    green = 4.0 * np.pi / (z + y + x + SCREEN) / (n.waves * 4.0 * side * side)
    green = green.reshape(n.waves, n.turns * n.wide).astype(np.float32)
    spread = np.zeros((LANES, n.halves * LANES), ml_dtypes.bfloat16)
    for cell in range(LANES):
        spread[cell, cell // side * n.grid + cell % side] = 1
    gather = np.ascontiguousarray(spread.T)
    return to_waves, from_waves, lane, lane_back, twiddle, green, spread, gather


def far_first(n, me):
    near = n.owners >> ((n.owners.bit_length() - 1) // 2)
    near = n.owners // near
    far = n.owners // near
    z, y = me // near, lax.rem(me, near)
    low = (z < far // 2).astype(jnp.int32)
    here = low * (far - 1 - z) + (1 - low) * z
    peers = []
    for k in range(far - 1):
        place = k + (k >= here).astype(jnp.int32)
        level = low * (far - 1 - place) + (1 - low) * place
        peers += [level * near + lax.rem(y + 1 + step, near) for step in range(near)]
    return peers + [z * near + lax.rem(y + step, near) for step in range(1, near + 1)]


def split(value):
    high = value.astype(BF16)
    return high, (value - high.astype(F32)).astype(BF16)


def encode(value):
    largest = jnp.max(jnp.abs(value), axis=0, keepdims=True)
    largest = jnp.maximum(largest, TINY)
    code = (value * (STEPS / largest) + (STEPS + 1.5)).astype(jnp.int32) - (int(STEPS) + 1)
    return code.astype(CODE), largest * (1.0 / STEPS)


def decode(code, step):
    return code.astype(jnp.int32).astype(F32) * step


def dot(left, right):
    return jnp.dot(left, right, preferred_element_type=F32)


def thrice(high, low, matrix):
    return dot(high, matrix[0]) + dot(low, matrix[0]) + dot(high, matrix[1])


def flat_roll(value, amount):
    carried = lax.rem(amount, LANES)
    down = amount // LANES
    rows = value.shape[1]
    turned = pltpu.roll(value, carried, axis=2)
    here = pltpu.roll(turned, down, axis=1)
    above = pltpu.roll(turned, lax.rem(down + 1, rows), axis=1)
    lane = lax.broadcasted_iota(jnp.int32, value.shape, 2)
    return jnp.where(lane >= carried, here, above)


def slide(n, value, shift_y, shift_x):
    shape = value.shape
    value = value.reshape(shape[0] // n.rows, n.rows, LANES)
    row = lax.broadcasted_iota(jnp.int32, value.shape, 1)
    lane = lax.broadcasted_iota(jnp.int32, value.shape, 2)
    y = row * n.per + lane // n.side - shift_y
    x = lax.rem(lane, n.side) - shift_x
    inside = (y >= 0) & (y < n.side) & (x >= 0) & (x < n.side)
    amount = lax.rem(shift_y * n.side + shift_x + 2 * n.cells, n.cells)
    return jnp.where(inside, flat_roll(value, amount), 0.0).reshape(shape)


def wave_sums(n, values):
    top, half = n.turns // 2, n.turns // 4
    cosines, sines = [None] * (top + 1), [None] * (top + 1)
    for q in range(half + 1):
        sums = []
        for wave in (math.cos, math.sin):
            for parity in (0, 1):
                total = None
                for s in range(parity, n.rows, 2):
                    factor = wave(2.0 * math.pi * q * s / n.turns)
                    total = weighted(total, factor, values[s])
                sums.append(total)
        even_cos, odd_cos, even_sin, odd_sin = sums
        cosines[q] = plus(even_cos, odd_cos)
        cosines[top - q] = minus(even_cos, odd_cos)
        sines[q] = plus(even_sin, odd_sin)
        sines[top - q] = minus(odd_sin, even_sin)
    return cosines, sines


def weighted(total, factor, value):
    if value is None or abs(factor) < 1e-12:
        return total
    if abs(abs(factor) - 1.0) < 1e-12:
        if factor > 0:
            return value if total is None else total + value
        return -value if total is None else total - value
    term = factor * value
    return term if total is None else total + term


def plus(left, right):
    if left is None or right is None:
        return right if left is None else left
    return left + right


def minus(left, right):
    if right is None:
        return left
    return -right if left is None else left - right


def cell_sums(n, cosines, sines):
    top, half = n.turns // 2, n.turns // 4
    values = []
    folded = {}
    for q in range(half + 1):
        if q == top - q:
            folded[q] = (cosines[q], cosines[q], sines[q], sines[q])
        else:
            c, d, s, t = cosines[q], cosines[top - q], sines[q], sines[top - q]
            folded[q] = (plus(c, d), minus(c, d), minus(s, t), plus(s, t))
    for s in range(n.rows):
        total = None
        odd = s % 2
        for q in range(half + 1):
            angle = 2.0 * math.pi * q * s / n.turns
            total = weighted(total, math.cos(angle), folded[q][odd])
            total = weighted(total, math.sin(angle), folded[q][2 + odd])
        values.append(total)
    return values


def forward_band(n, rho, band, size, planes, lane, twiddle):
    start = pl.multiple_of(band * (size * n.rows), size * n.rows)
    values = [rho[pl.ds(start + s, size, stride=n.rows), :] for s in range(n.rows)]
    cosines, sines = wave_sums(n, values)
    top = n.turns // 2
    first, second = [], []
    for q in range(n.turns):
        same = q <= top
        a = cosines[q if same else n.turns - q]
        b = sines[q if same else n.turns - q]
        ahead = twiddle[q : q + 1, :]
        behind = twiddle[n.turns + q : n.turns + q + 1, :]
        u, w = ahead * a, behind * a
        if q % top:
            u = u + behind * b if same else u - behind * b
            w = w - ahead * b if same else w + ahead * b
        first.append(u)
        second.append(w)
    value = jnp.concatenate([jnp.concatenate(first, axis=0), jnp.concatenate(second, axis=0)], axis=1)
    high, low = split(value)
    value = thrice(high, low, lane)
    rows = pl.ds(pl.multiple_of(band * size, size), size)
    for q in range(n.turns):
        planes[rows, q * n.wide : (q + 1) * n.wide] = value[q * size : (q + 1) * size, :]


def stacked(value):
    high, low = split(value)
    return jnp.concatenate([high, low, high], axis=0)


def along_z(planes, to_waves, from_waves, green):
    value = dot(to_waves[...], stacked(planes[...])) * green[...]
    planes[...] = dot(from_waves[...], stacked(value))


def back_band(n, planes, band, size, field, lane_back, twiddle):
    rows = pl.ds(pl.multiple_of(band * size, size), size)
    value = jnp.concatenate([planes[rows, q * n.wide : (q + 1) * n.wide] for q in range(n.turns)], axis=0)
    high, low = split(value)
    value = thrice(high, low, lane_back)
    top = n.turns // 2
    cosines, sines = [None] * (top + 1), [None] * (top + 1)
    for q in range(n.turns):
        part = slice(q * size, (q + 1) * size)
        u, w = value[part, 0:LANES], value[part, LANES : 2 * LANES]
        ahead = twiddle[q : q + 1, :]
        behind = twiddle[n.turns + q : n.turns + q + 1, :]
        a = ahead * u + behind * w
        b = behind * u - ahead * w
        if q <= top:
            cosines[q] = a
            sines[q] = b if q % top else None
        else:
            cosines[n.turns - q] = cosines[n.turns - q] + a
            sines[n.turns - q] = sines[n.turns - q] - b
    start = pl.multiple_of(band * (size * n.rows), size * n.rows)
    for s, part in enumerate(cell_sums(n, cosines, sines)):
        field[pl.ds(start + s, size, stride=n.rows), :] = part


def kernel(n, listed, placed, orbital, external, *refs):
    table_refs, refs = refs[:8], refs[8:]
    out, refs = refs[0], refs[1:]
    table_dst, refs = refs[:8], refs[8:]
    (own_box, flat, box_send, box_land, place_send, place_land, corner, near, moved, rho, field_flat) = refs[:11]
    (ext_block, ext_flat, dens_grid, dens_send, dens_land, level, read_in, read, planes, pairs) = refs[11:21]
    (listed_in, placed_in, rho_send, rho_land, field_send, field_land, grad_send, grad_land) = refs[21:29]
    (rho_step, rho_steps, field_step, field_steps, grad_step, grad_steps) = refs[29:35]
    local_sem, own_send, own_recv, grp_send, grp_recv = refs[35:]
    to_waves, from_waves, lane, lane_back, twiddle, green, spread, gather = table_dst
    owners, groups, depth, slab = n.owners, n.groups, n.depth, n.slab
    me, team = lax.axis_index("own"), lax.axis_index("grp")
    partner = team + 1 - 2 * lax.rem(team, 2)
    barrier = pltpu.get_barrier_semaphore()
    peers = far_first(n, me)
    for peer in peers:
        there = {"own": peer, "grp": partner}
        pl.semaphore_signal(barrier, inc=1, device_id=there, device_id_type=MESH)
    base = team - lax.rem(team, 2)
    distant = [lax.rem(base + step, groups) for step in range(2, groups)]
    others = [*distant, partner]
    for peer in distant:
        pl.semaphore_signal(barrier, inc=1, device_id={"grp": peer}, device_id_type=MESH)

    small_in = [
        pltpu.make_async_copy(placed, placed_in, local_sem.at[2 + len(table_refs)]),
        pltpu.make_async_copy(listed, listed_in, local_sem.at[3 + len(table_refs)]),
    ]
    for item in small_in:
        item.start()
    own_in = pltpu.make_async_copy(orbital, own_box, local_sem.at[0])
    own_in.start()
    first_level = pl.multiple_of(me * depth // TILE * TILE, TILE)
    taken = ext_block.shape[0]
    ext_in = pltpu.make_async_copy(external.at[pl.ds(first_level, taken)], ext_block, local_sem.at[1])
    ext_in.start()
    table_in = [
        pltpu.make_async_copy(source, target, local_sem.at[2 + i])
        for i, (source, target) in enumerate(zip(table_refs, table_dst))
    ]
    for item in table_in:
        item.start()
    place_index = lax.broadcasted_iota(jnp.int32, place_send.shape, 1)
    for item in small_in:
        item.wait()
    pair_index = lax.broadcasted_iota(jnp.int32, listed_in.shape, 1)
    header = jnp.where(place_index == 0, placed_in[0:1, 0:1], placed_in[0:1, 1:2])
    for turn in range(n.each):
        mine = jnp.sum(jnp.where(pair_index == me * n.each + turn, listed_in[...], 0), axis=1, keepdims=True)
        header = jnp.where(place_index == 2 + 2 * turn, mine[0:1], header)
        header = jnp.where(place_index == 3 + 2 * turn, mine[1:2], header)
    place_send[...] = header
    own_in.wait()
    for s in range(n.rows):
        flat[pl.ds(s, n.levels, stride=n.rows), :] = own_box[:, s * LANES : (s + 1) * LANES].astype(F32)
    for owner in range(owners):
        box_send[owner] = flat[owner * slab : (owner + 1) * slab, :].astype(BF16)
    pl.semaphore_wait(barrier, owners + groups - 2)

    def to_owner(phase, peer, source, target):
        return pltpu.make_async_remote_copy(
            src_ref=source,
            dst_ref=target,
            send_sem=own_send.at[phase, peer],
            recv_sem=own_recv.at[phase, me],
            device_id={"own": peer, "grp": partner},
            device_id_type=MESH,
        )

    def arrive(phase, peer, source, target):
        pltpu.make_async_remote_copy(
            src_ref=source,
            dst_ref=target,
            send_sem=own_send.at[phase, peer],
            recv_sem=own_recv.at[phase, peer],
            device_id={"own": peer, "grp": partner},
            device_id_type=MESH,
        ).wait_recv()

    def arrived(phase, source, target):
        for peer in reversed(peers):
            arrive(phase, peer, source, target(peer))

    def rows_of(index):
        return pl.ds(pl.multiple_of(index * slab, slab), slab)

    def send_coded(phase, peer, value, here, there):
        slot, codes, steps = here
        codes[slot], steps[slot] = encode(value)
        landing, far_codes, far_steps = there
        copies = [
            to_owner(phase, peer, codes.at[slot], far_codes.at[landing]),
            to_owner(phase + 1, peer, steps.at[slot], far_steps.at[landing]),
        ]
        for item in copies:
            item.start()
        return copies

    def take_coded(phase, peer, slot, codes, steps):
        arrive(phase, peer, codes.at[slot], codes.at[slot])
        arrive(phase + 1, peer, steps.at[slot], steps.at[slot])
        return decode(codes[slot], steps[slot])

    sent = []
    boxes_in = []
    for peer in peers:
        boxes_in.append(to_owner(0, peer, place_send, place_land.at[me]))
        boxes_in.append(to_owner(1, peer, box_send.at[peer], box_land.at[me]))
        boxes_in[-2].start()
        boxes_in[-1].start()
    sent += boxes_in
    arrived(0, place_send, lambda peer: place_land.at[peer])
    for owner in range(owners):
        corner[owner, 0] = place_land[owner, 0, 0]
        corner[owner, 1] = place_land[owner, 0, 1]
        for turn in range(n.each):
            pairs[owner * n.each + turn, 0] = place_land[owner, 0, 2 + 2 * turn]
            pairs[owner * n.each + turn, 1] = place_land[owner, 0, 3 + 2 * turn]
    arrived(1, box_send.at[0], lambda peer: box_land.at[peer])

    def shift_of(row):
        first, second = pairs[row, 0], pairs[row, 1]
        return corner[second, 0] - corner[first, 0], corner[second, 1] - corner[first, 1]

    rho_in = []
    for peer in peers:
        for turn in range(n.each):
            row = peer * n.each + turn
            dy, dx = shift_of(row)
            a = box_land[pairs[row, 0]].astype(F32)
            b = slide(n, box_land[pairs[row, 1]].astype(F32), dy, dx)
            near[row] = a
            moved[row] = b
            rho_in += send_coded(2 + 2 * turn, peer, a * b, (row, rho_send, rho_step), (me * n.each + turn, rho_land, rho_steps))
    sent += rho_in

    for item in table_in:
        item.wait()
    grid_shape = (depth, n.grid_rows, LANES)
    for owner in range(owners):
        value = box_land[owner].astype(F32)
        high, low = split(value * value)
        wide = dot(high, spread[...]) + dot(low, spread[...])
        for z in range(depth):
            start = z * n.grid_rows
            for half in range(n.halves):
                rows = pl.ds(start + half, n.rows, stride=n.halves)
                dens_grid[owner, rows, :] = wide[z * n.rows : (z + 1) * n.rows, half * LANES : (half + 1) * LANES]
            rest = n.grid_rows - n.rows * n.halves
            dens_grid[owner, start + n.rows * n.halves : start + n.grid_rows, :] = jnp.zeros((rest, LANES), F32)
    total = jnp.zeros(grid_shape, F32)
    for owner in range(owners):
        amount = corner[owner, 0] * n.grid + corner[owner, 1]
        total = total + flat_roll(dens_grid[owner].reshape(grid_shape), amount)
    dens_send[...] = total.reshape(dens_send.shape)
    dens_land[team] = dens_send[...]

    def dens_copy(peer, sender):
        return pltpu.make_async_remote_copy(
            src_ref=dens_send,
            dst_ref=dens_land.at[sender],
            send_sem=grp_send.at[peer],
            recv_sem=grp_recv.at[sender],
            device_id={"grp": peer},
            device_id_type=MESH,
        )

    for peer in others:
        dens_copy(peer, team).start()

    low = (me < owners // 2).astype(jnp.int32)

    def far_bands(size):
        count = n.levels // size
        return [low * (count - 1 - k) + (1 - low) * k for k in range(count)]

    rho_base = 2
    field_base = rho_base + 2 * n.each
    grad_base = field_base + 2 * n.each
    field_in = []
    for turn in range(n.each):
        for band in reversed(far_bands(n.ahead)):
            for index in range(n.ahead // depth):
                peer = band * (n.ahead // depth) + index
                rho[rows_of(peer), :] = take_coded(rho_base + 2 * turn, peer, peer * n.each + turn, rho_land, rho_steps)
            forward_band(n, rho, band, n.ahead, planes, lane, twiddle)
        along_z(planes, to_waves, from_waves, green)
        for band in far_bands(n.behind):
            back_band(n, planes, band, n.behind, field_flat, lane_back, twiddle)
            for index in range(n.behind // depth):
                peer = band * (n.behind // depth) + index
                slot = peer * n.each + turn
                here, there = (slot, field_send, field_step), (me * n.each + turn, field_land, field_steps)
                field_in += send_coded(field_base + 2 * turn, peer, field_flat[rows_of(peer), :], here, there)
    sent += field_in

    ext_in.wait()
    ext_values = ext_block[...].astype(F32)
    for k in range(n.grid_rows):
        ext_flat[pl.ds(k, taken, stride=n.grid_rows), :] = ext_values[:, k * LANES : (k + 1) * LANES]
    for peer in others:
        dens_copy(peer, peer).wait_recv()
    density = dens_land[0]
    for index in range(1, groups):
        density = density + dens_land[index]
    start = pl.multiple_of((me * depth - first_level) * n.grid_rows, n.grid_rows)
    outside = ext_flat[pl.ds(start, depth * n.grid_rows), :]
    safe = jnp.where(density > 0.0, density, 1.0)
    root = jnp.exp(jnp.log(safe) * (1.0 / 3.0))
    root = root - (root - safe / (root * root)) * (1.0 / 3.0)
    level[...] = outside - EXCHANGE_COEF * jnp.where(density > 0.0, root, 0.0)
    whole = n.grid_rows * LANES
    for owner in range(owners):
        amount = lax.rem(whole - corner[owner, 0] * n.grid - corner[owner, 1], whole)
        turned = flat_roll(level[...].reshape(grid_shape), amount)
        read_in[owner] = turned.reshape(read_in.shape[1:])
        parts = []
        for z in range(depth):
            pieces = [
                read_in[owner, pl.ds(z * n.grid_rows + half, n.rows, stride=n.halves), :] for half in range(n.halves)
            ]
            parts.append(jnp.concatenate(pieces, axis=1) if n.halves > 1 else pieces[0])
        value = jnp.concatenate(parts, axis=0) if depth > 1 else parts[0]
        high, low = split(value)
        read[owner] = (dot(high, gather[...]) + dot(low, gather[...])) * box_land[owner].astype(F32)

    for peer in reversed(peers):
        for turn in range(n.each):
            row = peer * n.each + turn
            dy, dx = shift_of(row)
            field = take_coded(field_base + 2 * turn, peer, row, field_land, field_steps) * MIXING
            moved[row] = field * moved[row]
            near[row] = slide(n, field * near[row], -dy, -dx)
    for peer in peers:
        total = read[peer]
        for row in range(n.pairs):
            total = total - jnp.where(pairs[row, 0] == peer, moved[row], 0.0)
            total = total - jnp.where(pairs[row, 1] == peer, near[row], 0.0)
        sent += send_coded(grad_base, peer, total, (peer, grad_send, grad_step), (me, grad_land, grad_steps))
    for peer in reversed(peers):
        out[rows_of(peer), :] = take_coded(grad_base, peer, peer, grad_land, grad_steps)
    for item in sent:
        item.wait_send()
    for peer in others:
        dens_copy(peer, team).wait_send()


def body(owners, groups, orbitals, offsets, pairs, ext_pot):
    _, levels, cells = orbitals.shape
    n = Sizes(owners, groups, levels, cells, ext_pot.shape[1], pairs.shape[0])
    consts = tables(n)
    taken = max(n.depth, TILE)
    slabs = (n.owners, n.slab, LANES)
    flat_rows = levels * n.rows
    scratch = [VMEM(c.shape, c.dtype) for c in consts]
    counts = (n.pairs, n.pairs, n.pairs, n.pairs, owners, owners)
    scratch += [
        VMEM((levels, cells), BF16),
        VMEM((flat_rows, LANES), F32),
        VMEM(slabs, BF16),
        VMEM(slabs, BF16),
        VMEM((1, LANES), jnp.int32),
        VMEM((owners, 1, LANES), jnp.int32),
        pltpu.SMEM((owners, 2), jnp.int32),
        VMEM((n.pairs, n.slab, LANES), F32),
        VMEM((n.pairs, n.slab, LANES), F32),
        VMEM((flat_rows, LANES), F32),
        VMEM((flat_rows, LANES), F32),
        VMEM((taken, ext_pot.shape[1]), BF16),
        VMEM((taken * n.grid_rows, LANES), F32),
        VMEM((owners, n.depth * n.grid_rows, LANES), F32),
        VMEM((n.depth * n.grid_rows, LANES), F32),
        VMEM((groups, n.depth * n.grid_rows, LANES), F32),
        VMEM((n.depth * n.grid_rows, LANES), F32),
        VMEM((owners, n.depth * n.grid_rows, LANES), F32),
        VMEM(slabs, F32),
        VMEM((levels, n.turns * n.wide), F32),
        pltpu.SMEM(pairs.shape, jnp.int32),
        VMEM(pairs.shape[::-1], jnp.int32),
        VMEM(offsets.shape, jnp.int32),
        *[VMEM((count, n.slab, LANES), CODE) for count in counts],
        *[VMEM((count, 1, LANES), F32) for count in counts],
        pltpu.SemaphoreType.DMA((4 + len(consts),)),
        pltpu.SemaphoreType.DMA((4 + 4 * n.each, owners)),
        pltpu.SemaphoreType.DMA((4 + 4 * n.each, owners)),
        pltpu.SemaphoreType.DMA((groups,)),
        pltpu.SemaphoreType.DMA((groups,)),
    ]
    anywhere = pl.BlockSpec(memory_space=pl.ANY)
    slab_out = pl.pallas_call(
        functools.partial(kernel, n),
        out_shape=VMEM((flat_rows, LANES), F32),
        in_specs=[anywhere] * (4 + len(consts)),
        out_specs=pl.BlockSpec(memory_space=VMEM),
        scratch_shapes=scratch,
        compiler_params=pltpu.CompilerParams(collective_id=0, has_side_effects=True),
        name="gradient",
    )(pairs.T, offsets, orbitals[0], ext_pot, *consts)
    return slab_out.reshape(1, levels, cells)


def solution(mesh):
    in_specs = (P(("grp", "own"), None, None), P(("grp", "own"), None), P("grp", None), P())
    out_specs = P(("grp", "own"), None, None)
    run = functools.partial(body, mesh.shape["own"], mesh.shape["grp"])
    return jax.shard_map(run, mesh=mesh, in_specs=in_specs, out_specs=out_specs, check_vma=False)
```

```python
import functools
import math

import jax
import jax.numpy as jnp
import ml_dtypes
import numpy as np
from jax import lax
from jax.experimental import pallas as pl
from jax.experimental.pallas import tpu as pltpu
from jax.sharding import PartitionSpec as P

SCREEN = 0.0025
MIXING = 0.25
EXCHANGE_COEF = (3.0 / math.pi) ** (1.0 / 3.0)
LANES = 128
TILE = 8
AHEAD = 16
BEHIND = 8
VMEM = pltpu.VMEM
MESH = pl.DeviceIdType.MESH
F32 = jnp.float32
BF16 = jnp.bfloat16
CODE = jnp.int16
STEPS = 32767.0
TINY = 1e-30


class Sizes:
    def __init__(self, owners, groups, levels, cells, grid_cells, pairs):
        self.owners, self.groups, self.levels, self.cells, self.pairs = owners, groups, levels, cells, pairs
        self.side, self.grid = math.isqrt(cells), math.isqrt(grid_cells)
        self.depth = levels // owners
        self.each = pairs // owners
        self.rows = cells // LANES
        self.per = LANES // self.side
        self.slab = self.depth * self.rows
        self.grid_rows = grid_cells // LANES
        self.halves = self.per * self.grid // LANES
        self.waves = 2 * levels
        self.turns = 2 * self.side // self.per
        self.wide = self.per * 2 * self.side
        self.ahead, self.behind = min(AHEAD, levels), min(BEHIND, levels)


def halves_of(table):
    high = table.astype(ml_dtypes.bfloat16)
    low = (table - high.astype(np.float64)).astype(ml_dtypes.bfloat16)
    return high, low


def cas(angle):
    return np.cos(angle) + np.sin(angle)


def tables(n):
    side, per, levels = n.side, n.per, n.levels
    along_z = cas(2.0 * np.pi / n.waves * np.outer(np.arange(n.waves), np.arange(levels)))
    high, low = halves_of(along_z)
    to_waves = np.concatenate([high, high, low], axis=1)
    high, low = halves_of(along_z.T)
    from_waves = np.concatenate([high, high, low], axis=1)
    along_x = cas(np.pi / side * np.outer(np.arange(side), np.arange(2 * side)))
    phase = 2.0 * np.pi / per * np.outer(np.arange(per), np.arange(per))
    lane = np.concatenate(
        [np.einsum("yh,xk->yxhk", wave(phase), along_x).reshape(LANES, n.wide) for wave in (np.cos, np.sin)]
    )
    lane = np.stack(halves_of(lane))
    lane_back = np.ascontiguousarray(np.swapaxes(lane, 1, 2))
    angle = np.pi / side * np.outer(np.arange(n.turns), np.arange(LANES) // side)
    twiddle = np.concatenate([cas(angle), cas(-angle)]).astype(np.float32)

    def squares(length):
        m = np.arange(length)
        return (2.0 * np.pi / length * np.where(m < length // 2, m, m - length)) ** 2

    z = squares(n.waves).reshape(n.waves, 1, 1, 1)
    y = squares(2 * side).reshape(per, n.turns).T.reshape(1, n.turns, per, 1)
    x = squares(2 * side).reshape(1, 1, 1, 2 * side)
    green = 4.0 * np.pi / (z + y + x + SCREEN) / (n.waves * 4.0 * side * side)
    green = green.reshape(n.waves, n.turns * n.wide).astype(np.float32)
    spread = np.zeros((LANES, n.halves * LANES), ml_dtypes.bfloat16)
    for cell in range(LANES):
        spread[cell, cell // side * n.grid + cell % side] = 1
    gather = np.ascontiguousarray(spread.T)
    return to_waves, from_waves, lane, lane_back, twiddle, green, spread, gather


def far_first(n, me):
    near = n.owners >> ((n.owners.bit_length() - 1) // 2)
    near = n.owners // near
    far = n.owners // near
    z, y = me // near, lax.rem(me, near)
    low = (z < far // 2).astype(jnp.int32)
    here = low * (far - 1 - z) + (1 - low) * z
    peers = []
    for k in range(far - 1):
        place = k + (k >= here).astype(jnp.int32)
        level = low * (far - 1 - place) + (1 - low) * place
        peers += [level * near + lax.rem(y + 1 + step, near) for step in range(near)]
    return peers + [z * near + lax.rem(y + step, near) for step in range(1, near + 1)]


def split(value):
    high = value.astype(BF16)
    return high, (value - high.astype(F32)).astype(BF16)


def encode(value):
    largest = jnp.max(jnp.abs(value), axis=0, keepdims=True)
    largest = jnp.maximum(largest, TINY)
    code = (value * (STEPS / largest) + (STEPS + 1.5)).astype(jnp.int32) - (int(STEPS) + 1)
    return code.astype(CODE), largest * (1.0 / STEPS)


def decode(code, step):
    return code.astype(jnp.int32).astype(F32) * step


def dot(left, right):
    return jnp.dot(left, right, preferred_element_type=F32)


def thrice(high, low, matrix):
    return dot(high, matrix[0]) + dot(low, matrix[0]) + dot(high, matrix[1])


def flat_roll(value, amount):
    carried = lax.rem(amount, LANES)
    down = amount // LANES
    rows = value.shape[1]
    turned = pltpu.roll(value, carried, axis=2)
    here = pltpu.roll(turned, down, axis=1)
    above = pltpu.roll(turned, lax.rem(down + 1, rows), axis=1)
    lane = lax.broadcasted_iota(jnp.int32, value.shape, 2)
    return jnp.where(lane >= carried, here, above)


def carry(n, value, shift_y, shift_x):
    shape = value.shape
    value = value.reshape(shape[0] // n.rows, n.rows, LANES)
    amount = lax.rem(shift_y * n.side + shift_x + 2 * n.cells, n.cells)
    return flat_roll(value, amount).reshape(shape)


def slide(n, value, shift_y, shift_x):
    shape = value.shape
    value = value.reshape(shape[0] // n.rows, n.rows, LANES)
    row = lax.broadcasted_iota(jnp.int32, value.shape, 1)
    lane = lax.broadcasted_iota(jnp.int32, value.shape, 2)
    y = row * n.per + lane // n.side - shift_y
    x = lax.rem(lane, n.side) - shift_x
    inside = (y >= 0) & (y < n.side) & (x >= 0) & (x < n.side)
    amount = lax.rem(shift_y * n.side + shift_x + 2 * n.cells, n.cells)
    return jnp.where(inside, flat_roll(value, amount), 0.0).reshape(shape)


def wave_sums(n, values):
    top, half = n.turns // 2, n.turns // 4
    cosines, sines = [None] * (top + 1), [None] * (top + 1)
    for q in range(half + 1):
        sums = []
        for wave in (math.cos, math.sin):
            for parity in (0, 1):
                total = None
                for s in range(parity, n.rows, 2):
                    factor = wave(2.0 * math.pi * q * s / n.turns)
                    total = weighted(total, factor, values[s])
                sums.append(total)
        even_cos, odd_cos, even_sin, odd_sin = sums
        cosines[q] = plus(even_cos, odd_cos)
        cosines[top - q] = minus(even_cos, odd_cos)
        sines[q] = plus(even_sin, odd_sin)
        sines[top - q] = minus(odd_sin, even_sin)
    return cosines, sines


def weighted(total, factor, value):
    if value is None or abs(factor) < 1e-12:
        return total
    if abs(abs(factor) - 1.0) < 1e-12:
        if factor > 0:
            return value if total is None else total + value
        return -value if total is None else total - value
    term = factor * value
    return term if total is None else total + term


def plus(left, right):
    if left is None or right is None:
        return right if left is None else left
    return left + right


def minus(left, right):
    if right is None:
        return left
    return -right if left is None else left - right


def cell_sums(n, cosines, sines):
    top, half = n.turns // 2, n.turns // 4
    values = []
    folded = {}
    for q in range(half + 1):
        if q == top - q:
            folded[q] = (cosines[q], cosines[q], sines[q], sines[q])
        else:
            c, d, s, t = cosines[q], cosines[top - q], sines[q], sines[top - q]
            folded[q] = (plus(c, d), minus(c, d), minus(s, t), plus(s, t))
    for s in range(n.rows):
        total = None
        odd = s % 2
        for q in range(half + 1):
            angle = 2.0 * math.pi * q * s / n.turns
            total = weighted(total, math.cos(angle), folded[q][odd])
            total = weighted(total, math.sin(angle), folded[q][2 + odd])
        values.append(total)
    return values


def forward_band(n, rho, band, size, planes, lane, twiddle):
    start = pl.multiple_of(band * (size * n.rows), size * n.rows)
    values = [rho[pl.ds(start + s, size, stride=n.rows), :] for s in range(n.rows)]
    cosines, sines = wave_sums(n, values)
    top = n.turns // 2
    first, second = [], []
    for q in range(n.turns):
        same = q <= top
        a = cosines[q if same else n.turns - q]
        b = sines[q if same else n.turns - q]
        ahead = twiddle[q : q + 1, :]
        behind = twiddle[n.turns + q : n.turns + q + 1, :]
        u, w = ahead * a, behind * a
        if q % top:
            u = u + behind * b if same else u - behind * b
            w = w - ahead * b if same else w + ahead * b
        first.append(u)
        second.append(w)
    value = jnp.concatenate([jnp.concatenate(first, axis=0), jnp.concatenate(second, axis=0)], axis=1)
    high, low = split(value)
    value = thrice(high, low, lane)
    rows = pl.ds(pl.multiple_of(band * size, size), size)
    for q in range(n.turns):
        planes[rows, q * n.wide : (q + 1) * n.wide] = value[q * size : (q + 1) * size, :]


def stacked(value):
    high, low = split(value)
    return jnp.concatenate([high, low, high], axis=0)


def along_z(planes, to_waves, from_waves, green):
    value = dot(to_waves[...], stacked(planes[...])) * green[...]
    planes[...] = dot(from_waves[...], stacked(value))


def back_band(n, planes, band, size, field, lane_back, twiddle):
    rows = pl.ds(pl.multiple_of(band * size, size), size)
    value = jnp.concatenate([planes[rows, q * n.wide : (q + 1) * n.wide] for q in range(n.turns)], axis=0)
    high, low = split(value)
    value = thrice(high, low, lane_back)
    top = n.turns // 2
    cosines, sines = [None] * (top + 1), [None] * (top + 1)
    for q in range(n.turns):
        part = slice(q * size, (q + 1) * size)
        u, w = value[part, 0:LANES], value[part, LANES : 2 * LANES]
        ahead = twiddle[q : q + 1, :]
        behind = twiddle[n.turns + q : n.turns + q + 1, :]
        a = ahead * u + behind * w
        b = behind * u - ahead * w
        if q <= top:
            cosines[q] = a
            sines[q] = b if q % top else None
        else:
            cosines[n.turns - q] = cosines[n.turns - q] + a
            sines[n.turns - q] = sines[n.turns - q] - b
    start = pl.multiple_of(band * (size * n.rows), size * n.rows)
    for s, part in enumerate(cell_sums(n, cosines, sines)):
        field[pl.ds(start + s, size, stride=n.rows), :] = part


def kernel(n, listed, placed, orbital, external, *refs):
    table_refs, refs = refs[:8], refs[8:]
    out, refs = refs[0], refs[1:]
    table_dst, refs = refs[:8], refs[8:]
    (own_box, flat, box_send, box_land, place_send, place_land, corner, near, moved, rho, field_flat) = refs[:11]
    (ext_block, ext_flat, dens_grid, dens_send, dens_land, level, read_in, read, planes, pairs) = refs[11:21]
    (listed_in, placed_in, rho_send, rho_land, field_send, field_land, grad_send, grad_land) = refs[21:29]
    (rho_step, rho_steps, field_step, field_steps, grad_step, grad_steps) = refs[29:35]
    local_sem, own_send, own_recv, grp_send, grp_recv = refs[35:]
    to_waves, from_waves, lane, lane_back, twiddle, green, spread, gather = table_dst
    owners, groups, depth, slab = n.owners, n.groups, n.depth, n.slab
    me, team = lax.axis_index("own"), lax.axis_index("grp")
    partner = team + 1 - 2 * lax.rem(team, 2)
    barrier = pltpu.get_barrier_semaphore()
    peers = far_first(n, me)
    for peer in peers:
        there = {"own": peer, "grp": partner}
        pl.semaphore_signal(barrier, inc=1, device_id=there, device_id_type=MESH)
    base = team - lax.rem(team, 2)
    distant = [lax.rem(base + step, groups) for step in range(2, groups)]
    others = [*distant, partner]
    for peer in distant:
        pl.semaphore_signal(barrier, inc=1, device_id={"grp": peer}, device_id_type=MESH)

    small_in = [
        pltpu.make_async_copy(placed, placed_in, local_sem.at[2 + len(table_refs)]),
        pltpu.make_async_copy(listed, listed_in, local_sem.at[3 + len(table_refs)]),
    ]
    for item in small_in:
        item.start()
    own_in = pltpu.make_async_copy(orbital, own_box, local_sem.at[0])
    own_in.start()
    first_level = pl.multiple_of(me * depth // TILE * TILE, TILE)
    taken = ext_block.shape[0]
    ext_in = pltpu.make_async_copy(external.at[pl.ds(first_level, taken)], ext_block, local_sem.at[1])
    ext_in.start()
    table_in = [
        pltpu.make_async_copy(source, target, local_sem.at[2 + i])
        for i, (source, target) in enumerate(zip(table_refs, table_dst))
    ]
    for item in table_in:
        item.start()
    place_index = lax.broadcasted_iota(jnp.int32, place_send.shape, 1)
    for item in small_in:
        item.wait()
    pair_index = lax.broadcasted_iota(jnp.int32, listed_in.shape, 1)
    header = jnp.where(place_index == 0, placed_in[0:1, 0:1], placed_in[0:1, 1:2])
    for turn in range(n.each):
        mine = jnp.sum(jnp.where(pair_index == me * n.each + turn, listed_in[...], 0), axis=1, keepdims=True)
        header = jnp.where(place_index == 2 + 2 * turn, mine[0:1], header)
        header = jnp.where(place_index == 3 + 2 * turn, mine[1:2], header)
    place_send[...] = header
    own_in.wait()
    for s in range(n.rows):
        flat[pl.ds(s, n.levels, stride=n.rows), :] = own_box[:, s * LANES : (s + 1) * LANES].astype(F32)
    for owner in range(owners):
        box_send[owner] = flat[owner * slab : (owner + 1) * slab, :].astype(BF16)
    pl.semaphore_wait(barrier, owners + groups - 2)

    def to_owner(phase, peer, source, target):
        return pltpu.make_async_remote_copy(
            src_ref=source,
            dst_ref=target,
            send_sem=own_send.at[phase, peer],
            recv_sem=own_recv.at[phase, me],
            device_id={"own": peer, "grp": partner},
            device_id_type=MESH,
        )

    def arrive(phase, peer, source, target):
        pltpu.make_async_remote_copy(
            src_ref=source,
            dst_ref=target,
            send_sem=own_send.at[phase, peer],
            recv_sem=own_recv.at[phase, peer],
            device_id={"own": peer, "grp": partner},
            device_id_type=MESH,
        ).wait_recv()

    def arrived(phase, source, target):
        for peer in reversed(peers):
            arrive(phase, peer, source, target(peer))

    def rows_of(index):
        return pl.ds(pl.multiple_of(index * slab, slab), slab)

    def send_coded(phase, peer, value, here, there):
        slot, codes, steps = here
        codes[slot], steps[slot] = encode(value)
        landing, far_codes, far_steps = there
        copies = [
            to_owner(phase, peer, codes.at[slot], far_codes.at[landing]),
            to_owner(phase + 1, peer, steps.at[slot], far_steps.at[landing]),
        ]
        for item in copies:
            item.start()
        return copies

    def take_coded(phase, peer, slot, codes, steps):
        arrive(phase, peer, codes.at[slot], codes.at[slot])
        arrive(phase + 1, peer, steps.at[slot], steps.at[slot])
        return decode(codes[slot], steps[slot])

    sent = []
    boxes_in = []
    for peer in peers:
        boxes_in.append(to_owner(0, peer, place_send, place_land.at[me]))
        boxes_in.append(to_owner(1, peer, box_send.at[peer], box_land.at[me]))
        boxes_in[-2].start()
        boxes_in[-1].start()
    sent += boxes_in
    arrived(0, place_send, lambda peer: place_land.at[peer])
    for owner in range(owners):
        corner[owner, 0] = place_land[owner, 0, 0]
        corner[owner, 1] = place_land[owner, 0, 1]
        for turn in range(n.each):
            pairs[owner * n.each + turn, 0] = place_land[owner, 0, 2 + 2 * turn]
            pairs[owner * n.each + turn, 1] = place_land[owner, 0, 3 + 2 * turn]
    arrived(1, box_send.at[0], lambda peer: box_land.at[peer])

    def shift_of(row):
        first, second = pairs[row, 0], pairs[row, 1]
        return corner[second, 0] - corner[first, 0], corner[second, 1] - corner[first, 1]

    rho_in = []
    for peer in peers:
        for turn in range(n.each):
            row = peer * n.each + turn
            dy, dx = shift_of(row)
            a = box_land[pairs[row, 0]].astype(F32)
            b = slide(n, box_land[pairs[row, 1]].astype(F32), dy, dx)
            moved[row] = b
            rho_in += send_coded(2 + 2 * turn, peer, a * b, (row, rho_send, rho_step), (me * n.each + turn, rho_land, rho_steps))
    sent += rho_in
    for row in range(n.pairs):
        dy, dx = shift_of(row)
        near[row] = slide(n, box_land[pairs[row, 0]].astype(F32), -dy, -dx)

    for item in table_in:
        item.wait()
    grid_shape = (depth, n.grid_rows, LANES)
    for owner in range(owners):
        value = box_land[owner].astype(F32)
        high, low = split(value * value)
        wide = dot(high, spread[...]) + dot(low, spread[...])
        for z in range(depth):
            start = z * n.grid_rows
            for half in range(n.halves):
                rows = pl.ds(start + half, n.rows, stride=n.halves)
                dens_grid[owner, rows, :] = wide[z * n.rows : (z + 1) * n.rows, half * LANES : (half + 1) * LANES]
            rest = n.grid_rows - n.rows * n.halves
            dens_grid[owner, start + n.rows * n.halves : start + n.grid_rows, :] = jnp.zeros((rest, LANES), F32)
    total = jnp.zeros(grid_shape, F32)
    for owner in range(owners):
        amount = corner[owner, 0] * n.grid + corner[owner, 1]
        total = total + flat_roll(dens_grid[owner].reshape(grid_shape), amount)
    dens_send[...] = total.reshape(dens_send.shape)
    dens_land[team] = dens_send[...]

    def dens_copy(peer, sender):
        return pltpu.make_async_remote_copy(
            src_ref=dens_send,
            dst_ref=dens_land.at[sender],
            send_sem=grp_send.at[peer],
            recv_sem=grp_recv.at[sender],
            device_id={"grp": peer},
            device_id_type=MESH,
        )

    for peer in others:
        dens_copy(peer, team).start()

    low = (me < owners // 2).astype(jnp.int32)

    def far_bands(size):
        count = n.levels // size
        return [low * (count - 1 - k) + (1 - low) * k for k in range(count)]

    rho_base = 2
    field_base = rho_base + 2 * n.each
    grad_base = field_base + 2 * n.each
    field_in = []
    for turn in range(n.each):
        for band in reversed(far_bands(n.ahead)):
            for index in range(n.ahead // depth):
                peer = band * (n.ahead // depth) + index
                rho[rows_of(peer), :] = take_coded(rho_base + 2 * turn, peer, peer * n.each + turn, rho_land, rho_steps)
            forward_band(n, rho, band, n.ahead, planes, lane, twiddle)
        along_z(planes, to_waves, from_waves, green)
        for band in far_bands(n.behind):
            back_band(n, planes, band, n.behind, field_flat, lane_back, twiddle)
            for index in range(n.behind // depth):
                peer = band * (n.behind // depth) + index
                slot = peer * n.each + turn
                here, there = (slot, field_send, field_step), (me * n.each + turn, field_land, field_steps)
                field_in += send_coded(field_base + 2 * turn, peer, field_flat[rows_of(peer), :], here, there)
    sent += field_in

    ext_in.wait()
    ext_values = ext_block[...].astype(F32)
    for k in range(n.grid_rows):
        ext_flat[pl.ds(k, taken, stride=n.grid_rows), :] = ext_values[:, k * LANES : (k + 1) * LANES]
    for peer in others:
        dens_copy(peer, peer).wait_recv()
    density = dens_land[0]
    for index in range(1, groups):
        density = density + dens_land[index]
    start = pl.multiple_of((me * depth - first_level) * n.grid_rows, n.grid_rows)
    outside = ext_flat[pl.ds(start, depth * n.grid_rows), :]
    safe = jnp.where(density > 0.0, density, 1.0)
    root = jnp.exp(jnp.log(safe) * (1.0 / 3.0))
    root = root - (root - safe / (root * root)) * (1.0 / 3.0)
    level[...] = outside - EXCHANGE_COEF * jnp.where(density > 0.0, root, 0.0)
    whole = n.grid_rows * LANES
    for owner in range(owners):
        amount = lax.rem(whole - corner[owner, 0] * n.grid - corner[owner, 1], whole)
        turned = flat_roll(level[...].reshape(grid_shape), amount)
        read_in[owner] = turned.reshape(read_in.shape[1:])
        parts = []
        for z in range(depth):
            pieces = [
                read_in[owner, pl.ds(z * n.grid_rows + half, n.rows, stride=n.halves), :] for half in range(n.halves)
            ]
            parts.append(jnp.concatenate(pieces, axis=1) if n.halves > 1 else pieces[0])
        value = jnp.concatenate(parts, axis=0) if depth > 1 else parts[0]
        high, low = split(value)
        read[owner] = (dot(high, gather[...]) + dot(low, gather[...])) * box_land[owner].astype(F32)

    for peer in reversed(peers):
        for turn in range(n.each):
            row = peer * n.each + turn
            dy, dx = shift_of(row)
            field = take_coded(field_base + 2 * turn, peer, row, field_land, field_steps) * MIXING
            moved[row] = field * moved[row]
            near[row] = carry(n, field, -dy, -dx) * near[row]
    for peer in peers:
        total = read[peer]
        for row in range(n.pairs):
            total = total - jnp.where(pairs[row, 0] == peer, moved[row], 0.0)
            total = total - jnp.where(pairs[row, 1] == peer, near[row], 0.0)
        sent += send_coded(grad_base, peer, total, (peer, grad_send, grad_step), (me, grad_land, grad_steps))
    for peer in reversed(peers):
        out[rows_of(peer), :] = take_coded(grad_base, peer, peer, grad_land, grad_steps)
    for item in sent:
        item.wait_send()
    for peer in others:
        dens_copy(peer, team).wait_send()


def body(owners, groups, orbitals, offsets, pairs, ext_pot):
    _, levels, cells = orbitals.shape
    n = Sizes(owners, groups, levels, cells, ext_pot.shape[1], pairs.shape[0])
    consts = tables(n)
    taken = max(n.depth, TILE)
    slabs = (n.owners, n.slab, LANES)
    flat_rows = levels * n.rows
    scratch = [VMEM(c.shape, c.dtype) for c in consts]
    counts = (n.pairs, n.pairs, n.pairs, n.pairs, owners, owners)
    scratch += [
        VMEM((levels, cells), BF16),
        VMEM((flat_rows, LANES), F32),
        VMEM(slabs, BF16),
        VMEM(slabs, BF16),
        VMEM((1, LANES), jnp.int32),
        VMEM((owners, 1, LANES), jnp.int32),
        pltpu.SMEM((owners, 2), jnp.int32),
        VMEM((n.pairs, n.slab, LANES), F32),
        VMEM((n.pairs, n.slab, LANES), F32),
        VMEM((flat_rows, LANES), F32),
        VMEM((flat_rows, LANES), F32),
        VMEM((taken, ext_pot.shape[1]), BF16),
        VMEM((taken * n.grid_rows, LANES), F32),
        VMEM((owners, n.depth * n.grid_rows, LANES), F32),
        VMEM((n.depth * n.grid_rows, LANES), F32),
        VMEM((groups, n.depth * n.grid_rows, LANES), F32),
        VMEM((n.depth * n.grid_rows, LANES), F32),
        VMEM((owners, n.depth * n.grid_rows, LANES), F32),
        VMEM(slabs, F32),
        VMEM((levels, n.turns * n.wide), F32),
        pltpu.SMEM(pairs.shape, jnp.int32),
        VMEM(pairs.shape[::-1], jnp.int32),
        VMEM(offsets.shape, jnp.int32),
        *[VMEM((count, n.slab, LANES), CODE) for count in counts],
        *[VMEM((count, 1, LANES), F32) for count in counts],
        pltpu.SemaphoreType.DMA((4 + len(consts),)),
        pltpu.SemaphoreType.DMA((4 + 4 * n.each, owners)),
        pltpu.SemaphoreType.DMA((4 + 4 * n.each, owners)),
        pltpu.SemaphoreType.DMA((groups,)),
        pltpu.SemaphoreType.DMA((groups,)),
    ]
    anywhere = pl.BlockSpec(memory_space=pl.ANY)
    slab_out = pl.pallas_call(
        functools.partial(kernel, n),
        out_shape=VMEM((flat_rows, LANES), F32),
        in_specs=[anywhere] * (4 + len(consts)),
        out_specs=pl.BlockSpec(memory_space=VMEM),
        scratch_shapes=scratch,
        compiler_params=pltpu.CompilerParams(collective_id=0, has_side_effects=True),
        name="gradient",
    )(pairs.T, offsets, orbitals[0], ext_pot, *consts)
    return slab_out.reshape(1, levels, cells)


def solution(mesh):
    in_specs = (P(("grp", "own"), None, None), P(("grp", "own"), None), P("grp", None), P())
    out_specs = P(("grp", "own"), None, None)
    run = functools.partial(body, mesh.shape["own"], mesh.shape["grp"])
    return jax.shard_map(run, mesh=mesh, in_specs=in_specs, out_specs=out_specs, check_vma=False)
```
